32 devices in a mesh: dp: 8 (over z, x), tensor: 4 (over y, core).
Axes of the slice: x: 2, y: 2, z: 4, core: 2. Of those that a mesh axis runs over, the one named last changes fastest.
Arguments:
- hidden_in: bfloat16 [16, 1024, 1024], P('dp', 'tensor'), may hold values from -6 to 6
- out_grad: bfloat16 [16, 1024, 1024], P('dp', 'tensor'), may hold values from -6 to 6
- doc_ids: int32 [16, 1, 1024], P('dp'), may hold values from 0 to 2, never falling along the last dimension, each value on 1 to 512 neighbouring positions
- w_query: bfloat16 [1024, 1024], P('dp', 'tensor'), may hold values from -0.1875 to 0.1875
- w_key: bfloat16 [1024, 1024], P('dp', 'tensor'), may hold values from -0.1875 to 0.1875
- w_value: bfloat16 [1024, 1024], P('dp', 'tensor'), may hold values from -0.1875 to 0.1875
- w_output: bfloat16 [1024, 1024], P('tensor', 'dp'), may hold values from -0.1875 to 0.1875
- w_up: bfloat16 [1024, 4096], P('dp', 'tensor'), may hold values from -0.1875 to 0.1875
- w_gate: bfloat16 [1024, 4096], P('dp', 'tensor'), may hold values from -0.1875 to 0.1875
- w_down: bfloat16 [4096, 1024], P('tensor', 'dp'), may hold values from -0.09375 to 0.09375
- scale_qk: float32 [1024], P(('dp', 'tensor')), may hold values from 0.8 to 1.6
- alpha_attn: float32 [1024], P(('dp', 'tensor')), may hold values from 0.2 to 0.8
- alpha_mlp: float32 [1024], P(('dp', 'tensor')), may hold values from 0.2 to 0.8
- scale_up: float32 [4096], P(('dp', 'tensor')), may hold values from 0.5 to 2
- scale_gate: float32 [4096], P(('dp', 'tensor')), may hold values from 0.5 to 2
Outputs:
- layer_out: bfloat16 [16, 1024, 1024], P('dp', 'tensor')
- input_grad: bfloat16 [16, 1024, 1024], P('dp', 'tensor')
- grad_query: float32 [1024, 1024], P('dp', 'tensor')
- grad_key: float32 [1024, 1024], P('dp', 'tensor')
- grad_value: float32 [1024, 1024], P('dp', 'tensor')
- grad_output: float32 [1024, 1024], P('tensor', 'dp')
- grad_up: float32 [1024, 4096], P('dp', 'tensor')
- grad_gate: float32 [1024, 4096], P('dp', 'tensor')
- grad_down: float32 [4096, 1024], P('tensor', 'dp')
- grad_scale_qk: float32 [1024], P(('dp', 'tensor'))
- grad_alpha_attn: float32 [1024], P(('dp', 'tensor'))
- grad_alpha_mlp: float32 [1024], P(('dp', 'tensor'))
- grad_scale_up: float32 [4096], P(('dp', 'tensor'))
- grad_scale_gate: float32 [4096], P(('dp', 'tensor'))
The draws below stay inside these ranges and needn't reach their ends.
Inputs may be any that keep to these rules, and one draw needn't show every extreme that they name: `doc_ids`: each sequence packs 3 documents of ids 0 to 2 in order, each of at most 512 tokens.
All inputs are finite; a program needn't handle non-finite values.
Results may differ from the reference program's by a relative error of at most 0.028.
Values may be sent and summed in bfloat16 or wider, within the bound.
A program may use at most 192 MiB of HBM per device.

```python
import math
import jax
import jax.numpy as jnp
import numpy as np
from jax import lax

D = 1024
H = 16
DH = 64
FF = 4096
LEN = 1024
SEQ_MB = 1
BLOCK = 256
DOCS = 3
MB_TOKENS = 1024
MICRO = 16
N_TENSOR = 4


def strengthened(values, stream_key, source, target, parts, factor):
    def block_of(axis_at):
        return (jnp.arange(values.shape[axis_at]) // (values.shape[axis_at] // parts)).reshape((-1,) + (1,) * (values.ndim - 1 - axis_at))

    near = jax.random.permutation(stream_key, parts)[block_of(target)]
    other_side = (block_of(target) + parts // 2) % parts
    return jnp.where((block_of(source) == near) | (block_of(source) == other_side), factor * values, values)


def steps_of(key, shape, shards, low, top_value):
    level = 1.0
    for axis_at, parts in shards:
        draws = jax.random.uniform(jax.random.fold_in(jax.random.fold_in(key, 6), axis_at), (parts,), jnp.float32, low / len(shards), top_value / len(shards))
        level = level * jnp.repeat(jnp.exp(draws), shape[axis_at] // parts).reshape((-1,) + (1,) * (len(shape) - 1 - axis_at))
    return level


def profile(number_of, total, bound, slope):
    loads = [(1 << 20) // math.isqrt(grade ** slope) + 1 for grade in range(2, number_of + 1)]
    surplus, holding = total - bound - (number_of - 1), [1] * (number_of - 1)
    while surplus > 0:
        candidates = [i for i in range(number_of - 1) if holding[i] < bound]
        mass, budget = sum([loads[i] for i in candidates]), surplus
        for i in candidates:
            more = min(bound - holding[i], max(1, budget * loads[i] // mass), surplus)
            holding[i] = holding[i] + more
            surplus = surplus - more
    return np.array([bound] + holding)


def uneven(key, count, total, most, skew):
    if count == 2:
        one = jax.random.randint(key, (), max(1, total - most), min(most, total - 1) + 1)
        return jnp.stack([one, total - one])
    lengths = jnp.asarray(profile(count, total, most, skew), jnp.int32)
    twos = (count - 1) // 2
    source_of, taker = lengths[1:1 + 2 * twos:2], lengths[2:2 + 2 * twos:2]
    room = jnp.minimum(source_of - 1, most - taker)
    passed = jax.random.randint(jax.random.fold_in(key, 1), (twos,), 0, 1 << 20) % (room + 1)
    lengths = lengths.at[1:1 + 2 * twos:2].set(source_of - passed).at[2:2 + 2 * twos:2].set(taker + passed)
    return lengths[jax.random.permutation(jax.random.fold_in(key, 2), count)]


def normal_values(stream_key, shape, width, limit, split=(), kind=jnp.bfloat16):
    array = width * jax.random.normal(stream_key, shape, jnp.float32)
    if split:
        array = array * steps_of(stream_key, shape, split, -0.22, 0.18)
    return jnp.clip(array, -limit, limit).astype(kind)


def bell_draw_with(key, dims, width, most, shards, heavy, held_as=jnp.bfloat16):
    values = width * jax.random.normal(key, dims, jnp.float32)
    if shards:
        values = values * steps_of(key, dims, shards, -0.22, 0.18)
    return jnp.clip(strengthened(values, jax.random.fold_in(key, 3), *heavy), -most, most).astype(held_as)


def setup_inputs(seed: int = 0) -> dict:
    key_of = jax.random.split(jax.random.key(seed), 16)
    hidden_in = bell_draw_with(key_of[0], (MICRO, MB_TOKENS, D), 1.0, 6.0, ((0, 8), (1, 4)), (0, 2, 8, 2.0))
    out_grad = bell_draw_with(key_of[1], (MICRO, MB_TOKENS, D), 1.0, 6.0, ((0, 8), (1, 4)), (0, 2, 8, 2.0))
    doc_ids = jax.vmap(lambda own: jnp.searchsorted(jnp.cumsum(uneven(own, DOCS, LEN, LEN // 2, 0)), jnp.arange(LEN), side="right"))(jax.random.split(key_of[2], MICRO * SEQ_MB)).reshape((MICRO, SEQ_MB, LEN)).astype(jnp.int32)
    w_query = normal_values(key_of[3], (D, D), D ** -0.5, 0.1875, ((0, 8), (1, 4)))
    w_key = normal_values(key_of[4], (D, D), D ** -0.5, 0.1875, ((0, 8), (1, 4)))
    w_value = normal_values(key_of[5], (D, D), D ** -0.5, 0.1875, ((0, 8), (1, 4)))
    w_output = normal_values(key_of[6], (D, D), D ** -0.5, 0.1875, ((0, 4), (1, 8)))
    w_up = normal_values(key_of[7], (D, FF), D ** -0.5, 0.1875, ((0, 8), (1, 4)))
    w_gate = normal_values(key_of[8], (D, FF), D ** -0.5, 0.1875, ((0, 8), (1, 4)))
    w_down = normal_values(key_of[9], (FF, D), FF ** -0.5, 0.09375, ((0, 4), (1, 8)))
    scale_qk = jnp.clip(jnp.exp(math.log(1.6) - 0.6931472 * jax.random.uniform(key_of[10], (D,), jnp.float32) ** steps_of(key_of[10], (D,), ((0, 32),), -0.2, 0.2)), 0.8, 1.6)
    alpha_attn = jnp.clip(0.2 + 0.6 * jax.random.uniform(key_of[11], (D,), jnp.float32) ** steps_of(key_of[11], (D,), ((0, 32),), -0.2, 0.2), 0.2, 0.8)
    alpha_mlp = jnp.clip(0.2 + 0.6 * jax.random.uniform(key_of[12], (D,), jnp.float32) ** steps_of(key_of[12], (D,), ((0, 32),), -0.2, 0.2), 0.2, 0.8)
    scale_up = jnp.clip(jnp.exp(math.log(2.0) - 1.3862944 * jax.random.uniform(key_of[13], (FF,), jnp.float32) ** steps_of(key_of[13], (FF,), ((0, 32),), -0.2, 0.2)), 0.5, 2.0)
    scale_gate = jnp.clip(jnp.exp(math.log(2.0) - 1.3862944 * jax.random.uniform(key_of[14], (FF,), jnp.float32) ** steps_of(key_of[14], (FF,), ((0, 32),), -0.2, 0.2)), 0.5, 2.0)
    return {"hidden_in": hidden_in, "out_grad": out_grad, "doc_ids": doc_ids, "w_query": w_query, "w_key": w_key, "w_value": w_value, "w_output": w_output, "w_up": w_up, "w_gate": w_gate, "w_down": w_down, "scale_qk": scale_qk, "alpha_attn": alpha_attn, "alpha_mlp": alpha_mlp, "scale_up": scale_up, "scale_gate": scale_gate}


@jax.custom_vjp
def low(v):
    return lax.optimization_barrier(v.astype(jnp.bfloat16)).astype(jnp.float32)

@jax.custom_vjp
def low_back(v):
    return v

def low_keep(v):
    return (low(v), None)

def low_pass(kept, grad):
    return (grad,)

def back_keep(v):
    return (v, None)

def back_low(kept, grad):
    return (low(grad),)
low.defvjp(low_keep, low_pass)
low_back.defvjp(back_keep, back_low)

def product(left, right):
    return jnp.dot(left, right, precision=lax.Precision.HIGHEST, preferred_element_type=jnp.float32)

def rms_scale(vals):
    return vals * lax.rsqrt(lax.optimization_barrier(jnp.mean(vals * vals, axis=-1, keepdims=True)) + 1e-06)

def unit_rows(vals):
    return vals * lax.rsqrt(lax.optimization_barrier(jnp.sum(vals * vals, axis=-1, keepdims=True)) + 1e-06)

def rotate(vals, cosine, sine):
    half = vals.shape[-1] // 2
    first = vals[..., :half]
    second = vals[..., half:]
    return jnp.concatenate([first * cosine - second * sine, first * sine + second * cosine], axis=-1)

def prepare(raw, cosine, sine, gain):
    return gain * unit_rows(rotate(raw, cosine, sine))

def doc_places(docs):
    labels = jnp.arange(DOCS, dtype=jnp.int32)
    member = (docs[..., :, None] == labels).astype(jnp.int32)
    counts = lax.optimization_barrier(jnp.sum(member, axis=-2))
    starts = jnp.cumsum(counts, axis=-1) - counts
    first = lax.optimization_barrier(jnp.sum(member * starts[..., None, :], axis=-1))
    return jnp.arange(docs.shape[-1], dtype=jnp.int32) - first

def angles(places):
    steps = jnp.arange(DH // 2, dtype=jnp.float32) / (DH // 2)
    freqs = jnp.exp(-math.log(10000.0) * steps)
    turn = places.astype(jnp.float32)[..., None] * freqs
    return (jnp.cos(turn), jnp.sin(turn))

def grouped_in(rows, weights, span):
    pieces = []
    for group in range(N_TENSOR):
        copy_rows = low_back(rows)
        pieces.append(tuple((product(copy_rows, weight[:, group * span:(group + 1) * span]) for weight in weights)))
    return tuple((jnp.concatenate([piece[index] for piece in pieces], axis=-1) for index in range(len(weights))))

def grouped_out(rows, weight, span):
    total = jnp.zeros((rows.shape[0], weight.shape[1]), jnp.float32)
    for group in range(N_TENSOR):
        total = total + low(product(rows[:, group * span:(group + 1) * span], weight[group * span:(group + 1) * span]))
    return total

def layer(hidden, params, docs):
    w_query, w_key, w_value, w_output, w_up, w_gate, w_down, scale_qk, alpha_attn, alpha_mlp, scale_up, scale_gate = params
    places = doc_places(docs)
    blocks = places // BLOCK
    allowed = (docs[:, None] == docs[None, :]) & (blocks[None, :] <= blocks[:, None])
    cosine, sine = angles(places)
    cosine = cosine[:, None, :]
    sine = sine[:, None, :]
    gain = scale_qk.reshape(H, DH)
    span_attn = D // N_TENSOR
    span_mlp = FF // N_TENSOR
    query_all, key_all, value_all = grouped_in(hidden, (w_query, w_key, w_value), span_attn)
    query_raw = low_back(query_all).reshape(LEN, H, DH)
    key_raw = low_back(key_all).reshape(LEN, H, DH)
    values = low(low_back(value_all)).reshape(LEN, H, DH)
    queries = low(prepare(query_raw, cosine, sine, gain))
    keys = low(prepare(key_raw, cosine, sine, gain))
    scores = low_back(math.sqrt(DH) * jnp.einsum('qhd,khd->hqk', queries, keys, precision=lax.Precision.HIGHEST))
    scores = jnp.where(allowed[None], scores, -1e+30)
    probs = low(jax.nn.softmax(scores, axis=-1))
    mixed = jnp.einsum('hqk,khd->qhd', probs, values, precision=lax.Precision.HIGHEST).reshape(LEN, D)
    mixed = low(low_back(mixed))
    attn = low_back(grouped_out(mixed, w_output, span_attn))
    middle = rms_scale(hidden + alpha_attn * (rms_scale(attn) - hidden))
    middle_low = low(middle)
    up_all, gate_all = grouped_in(middle_low, (w_up, w_gate), span_mlp)
    up_raw = low_back(up_all)
    gate_raw = low_back(gate_all)
    inner = low(scale_up * up_raw * jax.nn.silu(scale_gate * gate_raw))
    mlp = low_back(grouped_out(inner, w_down, span_mlp))
    return rms_scale(middle + alpha_mlp * (rms_scale(mlp) - middle))

def reference(hidden_in, out_grad, doc_ids, w_query, w_key, w_value, w_output, w_up, w_gate, w_down, scale_qk, alpha_attn, alpha_mlp, scale_up, scale_gate):
    params = tuple((item.astype(jnp.float32) for item in (w_query, w_key, w_value, w_output, w_up, w_gate, w_down, scale_qk, alpha_attn, alpha_mlp, scale_up, scale_gate)))
    rows_in = hidden_in.reshape(-1, LEN, D)
    rows_grad = out_grad.reshape(-1, LEN, D)
    rows_doc = doc_ids.reshape(-1, LEN)

    def one_sequence(totals, items):
        hidden, cotangent, docs = items
        result, pull = jax.vjp(lambda inputs, weights: layer(inputs, weights, docs), hidden.astype(jnp.float32), params)
        grad_input, grad_params = pull(cotangent.astype(jnp.float32))
        totals = jax.tree.map(lambda prior, extra: prior + extra, totals, grad_params)
        return (totals, (result.astype(jnp.bfloat16), grad_input.astype(jnp.bfloat16)))
    zeros = jax.tree.map(jnp.zeros_like, params)
    totals, (outputs, grads_in) = lax.scan(one_sequence, zeros, (rows_in, rows_grad, rows_doc))
    return (outputs.reshape(hidden_in.shape), grads_in.reshape(hidden_in.shape), totals[0], totals[1], totals[2], totals[3], totals[4], totals[5], totals[6], totals[7], totals[8], totals[9], totals[10], totals[11])
```

```python
import functools
import math

import jax
import jax.numpy as jnp
from jax import lax
from jax.experimental import pallas as pl
from jax.experimental.pallas import tpu as pltpu
from jax.sharding import PartitionSpec as P

DH = 64
BLOCK = 256
DOCS = 3
DOC_MAX = 512
F32 = jnp.float32
BF16 = jnp.bfloat16
MESH = pl.DeviceIdType.MESH
VMEM_LIMIT = 67043328
LOG2E = 1.4426950408889634
QB = 128
CODE = 8


def doc_places(docs):
    labels = jnp.arange(DOCS, dtype=jnp.int32)
    member = (docs[..., :, None] == labels).astype(jnp.int32)
    counts = jnp.sum(member, axis=-2)
    starts = jnp.cumsum(counts, axis=-1) - counts
    first = jnp.sum(member * starts[..., None, :], axis=-1)
    return jnp.arange(docs.shape[-1], dtype=jnp.int32) - first


def nn(a, b):
    return jnp.dot(a, b, preferred_element_type=F32)


def nt(a, b):
    return lax.dot_general(a, b, (((1,), (1,)), ((), ())), preferred_element_type=F32)


def tn(a, b):
    return lax.dot_general(a, b, (((0,), (0,)), ((), ())), preferred_element_type=F32)


def split_sum(vals, ones):
    high = vals.astype(BF16)
    low = (vals - high.astype(F32)).astype(BF16)
    return nn(high, ones) + nn(low, ones)


def lane_iota(shape):
    return lax.broadcasted_iota(jnp.int32, shape, len(shape) - 1)


def head_ones():
    rows = lax.broadcasted_iota(jnp.int32, (128, 128), 0) // DH
    cols = lax.broadcasted_iota(jnp.int32, (128, 128), 1) // DH
    return jnp.where(rows == cols, 1.0, 0.0).astype(BF16)


def partner(vals):
    low = lane_iota(vals.shape) % DH < DH // 2
    return jnp.where(low, pltpu.roll(vals, 128 - DH // 2, 1), pltpu.roll(vals, DH // 2, 1))


def turns(table):
    lane = lane_iota(table.shape)
    both = jnp.where(lane < DH, table, pltpu.roll(table, DH, 1))
    low = lane % DH < DH // 2
    cosine = jnp.where(low, both, pltpu.roll(both, DH // 2, 1))
    sine = jnp.where(low, -pltpu.roll(both, 128 - DH // 2, 1), both)
    return cosine, sine


class Place:
    def __init__(self, n):
        self.n = n
        self.t = lax.axis_index("tensor")
        self.d = lax.axis_index("dp")
        t, d = self.t, self.d
        self.sib = t + 1 - 2 * (t % 2)
        self.yp = (t + 2) % 4
        self.diag = (self.sib + 2) % 4
        self.xi = d % 2
        self.z = d // 2
        self.nz = n // 2
        self.xn = d + 1 - 2 * (d % 2)
        self.zpeers = [2 * ((self.z + k) % self.nz) + self.xi for k in range(1, self.nz)]
        self.dpeers = [(d + k) % n for k in range(1, n)]
        self.tpeers = [(t + k) % 4 for k in range(1, 4)]

    def barrier(self):
        sem = pltpu.get_barrier_semaphore()
        for peer in self.dpeers:
            pl.semaphore_signal(sem, inc=1, device_id={"dp": peer}, device_id_type=MESH)
        for peer in self.tpeers:
            pl.semaphore_signal(sem, inc=1, device_id={"tensor": peer}, device_id_type=MESH)
        pl.semaphore_wait(sem, self.n + 2)


def remote(src, dst, ssem, rsem, **where):
    return pltpu.make_async_remote_copy(
        src_ref=src, dst_ref=dst, send_sem=ssem, recv_sem=rsem, device_id=where, device_id_type=MESH
    )


class Gather:
    def __init__(self, place, whole, ssem, rsem, rows):
        self.p, self.whole, self.ssem, self.rsem, self.rows = place, whole, ssem, rsem, rows

    def at(self, index):
        return self.whole.at[pl.ds(pl.multiple_of(index * self.rows, self.rows), self.rows)]

    def start(self, own):
        p = self.p
        self.c_yp = remote(own, self.at(p.t), self.ssem.at[1], self.rsem.at[1], tensor=p.yp)
        self.c_sib = remote(own, self.at(p.t), self.ssem.at[0], self.rsem.at[0], tensor=p.sib)
        self.c_yp.start()
        self.c_sib.start()

    def wait(self, step):
        p = self.p
        if step == 1:
            remote(self.at(p.sib), self.at(p.sib), self.ssem.at[0], self.rsem.at[0], tensor=p.sib).wait_recv()
        if step == 2:
            remote(self.at(p.yp), self.at(p.yp), self.ssem.at[1], self.rsem.at[1], tensor=p.yp).wait_recv()
            self.c_fwd = remote(
                self.at(p.yp), self.at(p.yp), self.ssem.at[2], self.rsem.at[2], tensor=p.sib
            )
            self.c_fwd.start()
        if step == 3:
            remote(self.at(p.diag), self.at(p.diag), self.ssem.at[2], self.rsem.at[2], tensor=p.sib).wait_recv()

    def drain(self):
        self.c_yp.wait_send()
        self.c_sib.wait_send()
        self.c_fwd.wait_send()

    def order(self):
        p = self.p
        return (p.t, p.sib, p.yp, p.diag)


class Scatter:
    def __init__(self, place, sbuf, rbuf, ssem, rsem):
        self.p, self.sbuf, self.rbuf, self.ssem, self.rsem = place, sbuf, rbuf, ssem, rsem
        self.copies = []

    def send(self, slot, **where):
        copy = remote(
            self.sbuf.at[slot], self.rbuf.at[slot], self.ssem.at[slot], self.rsem.at[slot], **where
        )
        copy.start()
        self.copies.append(copy)

    def arrive(self, slot):
        remote(
            self.rbuf.at[slot], self.rbuf.at[slot], self.ssem.at[slot], self.rsem.at[slot],
            tensor=self.p.sib,
        ).wait_recv()

    def run(self, part, own):
        p = self.p
        self.sbuf[0] = part(p.diag).astype(BF16)
        self.send(0, tensor=p.sib)
        self.sbuf[1] = part(p.sib).astype(BF16)
        self.send(1, tensor=p.sib)
        across = part(p.yp)
        self.arrive(0)
        self.sbuf[2] = (across + self.rbuf[0].astype(F32)).astype(BF16)
        self.send(2, tensor=p.yp)
        mine = part(p.t)
        self.arrive(1)
        own[...] = mine + self.rbuf[1].astype(F32)

    def finish(self):
        self.arrive(2)
        for copy in self.copies:
            copy.wait_send()


def rows_of(ref, index, rows):
    return ref[pl.ds(pl.multiple_of(index * rows, rows), rows)]


def mean_sq(vals):
    return jnp.mean(vals * vals, axis=-1, keepdims=True)


def fold8(vals):
    total = vals[0:8]
    for k in range(1, vals.shape[0] // 8):
        total = total + vals[8 * k : 8 * k + 8]
    return total


def fwd_kernel(
    n,
    wsh, hid, og, small, table, irow,
    o_out, o_w, o_x, o_q, o_k, o_v, o_rq, o_rk, o_lrow, o_mixed, o_mid, o_up, o_gate, o_inner,
    o_attn, o_gmd, o_gm, o_gm0, o_vec, o_acc,
    w, x, q, k, v, rq, rk, lcol, mixed, mid, up, gate, inner,
    attn, midf, mlp, gmd, gm, gm0, vec, acc, sall, tab, ogv, outv, ir, qm, sbuf, rbuf,
    wsend, wrecv, wloc, small_s, small_r, lsem, agx_s, agx_r, agm_s, agm_r, agg_s, agg_r,
    rsa_s, rsa_r, rsm_s, rsm_r, osem,
):
    p = Place(n)
    nz = p.nz
    mbs, rows, width = hid.shape
    seq = x.shape[1]
    hw = q.shape[2]
    shard = wsh.shape[1]
    heads = hw // DH
    groups = wsh.shape[0]
    hidden = up.shape[2]

    def wat(g, index):
        return w.at[g, pl.ds(pl.multiple_of(index * shard, shard), shard)]

    local = []

    def lcopy(src, dst):
        copy = pltpu.make_async_copy(src, dst, lsem.at[len(local)])
        copy.start()
        local.append(copy)
        return copy

    outs = []

    def ocopy(src, dst):
        copy = pltpu.make_async_copy(src, dst, osem.at[len(outs)])
        copy.start()
        outs.append(copy)

    p.barrier()

    gx = [Gather(p, x.at[m], agx_s.at[m], agx_r.at[m], rows) for m in range(mbs)]
    gmi = [Gather(p, mid.at[m], agm_s.at[m], agm_r.at[m], rows) for m in range(mbs)]
    flat = 4 * p.d + p.t
    small_own = lcopy(small, sall.at[flat])
    small_t = [
        remote(small, sall.at[flat], small_s.at[i], small_r.at[i], tensor=peer)
        for i, peer in enumerate(p.tpeers)
    ]
    for copy in small_t:
        copy.start()
    gx[0].start(hid.at[0])
    sends = []

    def wsend_to(g, i, src, index, peer):
        copy = remote(src, wat(g, index), wsend.at[g, i], wrecv.at[g, index], dp=peer)
        copy.start()
        sends.append(copy)

    def relay(g):
        for i, peer in enumerate(p.zpeers):
            remote(wat(g, peer), wat(g, peer), wsend.at[g, 0], wrecv.at[g, peer], dp=p.xn).wait_recv()
            wsend_to(g, nz + i, wat(g, peer), peer, p.xn)

    wown = []
    for g in range(groups):
        for i, peer in enumerate(p.zpeers):
            wsend_to(g, i, wsh.at[g], p.d, peer)
        if g == 0:
            wsend_to(0, nz - 1, wsh.at[0], p.d, p.xn)
            gx[1].start(hid.at[1])
    for g in range(groups):
        copy = pltpu.make_async_copy(wsh.at[g], wat(g, p.d), wloc.at[g])
        copy.start()
        wown.append(copy)
    xown = [lcopy(hid.at[m], gx[m].at(p.t)) for m in range(mbs)]
    tables = [lcopy(table, tab), lcopy(irow, ir)]
    og_in = lcopy(og, ogv)
    for i, peer in enumerate(p.tpeers):
        src = (p.t + 4 - (i + 1)) % 4
        remote(sall.at[4 * p.d + src], sall.at[4 * p.d + src], small_s.at[i], small_r.at[i], tensor=peer).wait_recv()
    small_own.wait()
    small_d = []
    for i, peer in enumerate(p.dpeers):
        part = sall.at[pl.ds(4 * p.d, 4)]
        copy = remote(part, part, small_s.at[3 + i], small_r.at[3 + i], dp=peer)
        copy.start()
        small_d.append(copy)

    def wready(g):
        remote(wat(g, p.xn), wat(g, p.xn), wsend.at[g, 0], wrecv.at[g, p.xn], dp=p.xn).wait_recv()
        for peer in p.zpeers:
            other = peer + 1 - 2 * p.xi
            remote(wat(g, other), wat(g, other), wsend.at[g, 0], wrecv.at[g, other], dp=p.xn).wait_recv()
        wown[g].wait()
        ocopy(w.at[g], o_w.at[g])

    relay(0)
    for i, peer in enumerate(p.dpeers):
        src = (p.d + n - (i + 1)) % n
        part = sall.at[pl.ds(4 * src, 4)]
        remote(part, part, small_s.at[3 + i], small_r.at[3 + i], dp=peer).wait_recv()
    every = 4 * n

    def gathered(row, base, count, lanes):
        per = count // (lanes // 128)
        for r in range(lanes // 128):
            total = sall[base + r * per, row : row + 1, :]
            for j in range(1, per):
                total = total + sall[base + r * per + j, row : row + 1, :]
            vec[row : row + 1, 128 * r : 128 * r + 128] = total

    gathered(0, p.t * n, n, hw)
    gathered(1, 0, every, width)
    gathered(2, 0, every, width)
    gathered(3, p.t * n, n, hidden)
    gathered(4, p.t * n, n, hidden)
    acc[...] = jnp.zeros_like(acc)
    for copy in tables:
        copy.wait()
    wready(0)
    wsend_to(1, nz - 1, wsh.at[1], p.d, p.xn)

    ones = head_ones()

    def stage_qkv(m):
        for step, index in enumerate(gx[m].order()):
            gx[m].wait(step)
            if step == 0:
                xown[m].wait()
            at = pl.ds(pl.multiple_of(index * rows, rows), rows)
            xb = x[m, at, :]
            cb, sb = turns(tab[m, at, :])
            for which, (dst, rdst) in enumerate(((q, rq), (k, rk))):
                raw = nn(xb, w[0, :, which * hw : (which + 1) * hw])
                for half in range(hw // 128):
                    lanes = slice(128 * half, 128 * half + 128)
                    piece = raw[:, lanes]
                    turned = piece * cb + partner(piece) * sb
                    scale = lax.rsqrt(split_sum(turned * turned, ones) + 1e-06)
                    rdst[m, at, lanes] = scale.astype(BF16)
                    dst[m, at, lanes] = (turned * scale * vec[0:1, lanes]).astype(BF16)
            v[m, at, :] = nn(xb, w[0, :, 2 * hw : 3 * hw]).astype(BF16)

    win = seq - 128
    c_exp = math.sqrt(DH) * LOG2E

    def attend(m):
        def body(b, carry):
            at = pl.ds(pl.multiple_of(b * QB, QB), QB)
            keys = pl.ds(pl.multiple_of(((b + 3) // 8) * 128, 128), win)
            ccol = tab[m, at, DH : DH + 1]
            lcol_ = tab[m, at, DH + 1 : DH + 2]
            crow = ir[m, 0:1, keys]
            bias = jnp.where((crow <= ccol) & (crow >= lcol_), 0.0, -1e30)
            qb = q[m, at, :]
            lane = lane_iota((QB, hw)) // DH
            for h in range(heads):
                qm[h * QB : (h + 1) * QB, :] = jnp.where(lane == h, qb, jnp.zeros_like(qb))
            kb = k[m, keys, :]
            vb = v[m, keys, :]
            total = jnp.zeros((QB, hw), F32)
            lsum = jnp.zeros((QB, 128), F32)
            lane_l = lane_iota((QB, 128))
            for h in range(heads):
                scores = nt(qm[h * QB : (h + 1) * QB, :], kb)
                expo = jnp.exp2(scores * c_exp + bias)
                inv = 1.0 / jnp.sum(expo, axis=-1, keepdims=True)
                part = nn(expo.astype(BF16), vb)
                total = jnp.where(lane == h, part * inv, total)
                lsum = jnp.where(lane_l == h, inv, lsum)
            mixed[m, at, :] = total.astype(BF16)
            lcol[m, at, :] = lsum
            return carry

        lax.fori_loop(0, seq // QB, body, 0)

    sc_a = [Scatter(p, sbuf.at[m], rbuf.at[m], rsa_s.at[m], rsa_r.at[m]) for m in range(mbs)]
    sc_m = [Scatter(p, sbuf.at[m], rbuf.at[m], rsm_s.at[m], rsm_r.at[m]) for m in range(mbs)]

    def stage_o(m):
        sc_a[m].run(
            lambda index: nt(rows_of(mixed.at[m], index, rows), w[0, :, 3 * hw : 3 * hw + hw]),
            attn.at[m],
        )

    chunk = 32

    def stage_mid(m):
        sc_a[m].finish()
        base = p.t * rows

        def body(i, carry):
            at = pl.ds(pl.multiple_of(i * chunk, chunk), chunk)
            own = pl.ds(pl.multiple_of(base + i * chunk, chunk), chunk)
            a = attn[m, at, :] + rbuf[m, 2, at, :].astype(F32)
            attn[m, at, :] = a
            h = x[m, own, :].astype(F32)
            na = a * lax.rsqrt(mean_sq(a) + 1e-06)
            zz = h + vec[1:2, :] * (na - h)
            out = zz * lax.rsqrt(mean_sq(zz) + 1e-06)
            midf[m, at, :] = out
            mid[m, own, :] = out.astype(BF16)
            return carry

        lax.fori_loop(0, rows // chunk, body, 0)
        gmi[m].start(gmi[m].at(p.t))

    cols = 256

    def stage_up(m):
        for step, index in enumerate(gmi[m].order()):
            gmi[m].wait(step)
            at = pl.ds(pl.multiple_of(index * rows, rows), rows)

            def body(c, carry):
                lanes = pl.ds(pl.multiple_of(c * cols, cols), cols)
                mb = mid[m, at, :]
                u = nn(mb, w[1, :, lanes])
                g = nn(mb, w[2, :, lanes])
                up[m, at, lanes] = u.astype(BF16)
                gate[m, at, lanes] = g.astype(BF16)
                gs = g * vec[4:5, lanes]
                inner[m, at, lanes] = ((u * vec[3:4, lanes]) * (gs / (1.0 + jnp.exp(-gs)))).astype(BF16)
                return carry

            lax.fori_loop(0, hidden // cols, body, 0)

    def stage_down(m):
        sc_m[m].run(lambda index: nt(rows_of(inner.at[m], index, rows), w[3]), mlp.at[m])

    gg = Gather(p, gm0, agg_s, agg_r, rows)

    def stage_end(m):
        sc_m[m].finish()

        def body(i, carry):
            at = pl.ds(pl.multiple_of(i * chunk, chunk), chunk)
            a = mlp[m, at, :] + rbuf[m, 2, at, :].astype(F32)
            h = midf[m, at, :]
            ra = lax.rsqrt(mean_sq(a) + 1e-06)
            na = a * ra
            al = vec[2:3, :]
            zz = h + al * (na - h)
            rz = lax.rsqrt(mean_sq(zz) + 1e-06)
            out = zz * rz
            outv[m, at, :] = out.astype(BF16)
            cot = ogv[m, at, :].astype(F32)
            dz = rz * (cot - out * jnp.mean(cot * out, axis=-1, keepdims=True))
            dn = al * dz
            acc[0:8, :] += fold8(dz * (na - h))
            gmd[m, at, :] = dz - dn
            grad = (ra * (dn - na * jnp.mean(dn * na, axis=-1, keepdims=True))).astype(BF16)
            gm[m, at, :] = grad
            if m == 0:
                gm0[pl.ds(pl.multiple_of(p.t * rows + i * chunk, chunk), chunk), :] = grad
            return carry

        lax.fori_loop(0, rows // chunk, body, 0)
        if m == 0:
            gg.start(gg.at(p.t))

    stage_qkv(0)
    attend(0)
    stage_o(0)
    relay(1)
    wsend_to(2, nz - 1, wsh.at[2], p.d, p.xn)
    stage_qkv(1)
    relay(2)
    wsend_to(3, nz - 1, wsh.at[3], p.d, p.xn)
    attend(1)
    relay(3)
    stage_mid(0)
    stage_o(1)
    for m in range(mbs):
        ocopy(x.at[m], o_x.at[m])
        ocopy(q.at[m], o_q.at[m])
        ocopy(k.at[m], o_k.at[m])
        ocopy(v.at[m], o_v.at[m])
        ocopy(rq.at[m], o_rq.at[m])
        ocopy(rk.at[m], o_rk.at[m])
        ocopy(mixed.at[m], o_mixed.at[m])
    ocopy(vec, o_vec)
    wready(1)
    wready(2)
    stage_up(0)
    stage_mid(1)
    wready(3)
    stage_down(0)
    stage_up(1)
    og_in.wait()
    stage_end(0)
    ocopy(mid.at[0], o_mid.at[0])
    ocopy(up.at[0], o_up.at[0])
    ocopy(gate.at[0], o_gate.at[0])
    ocopy(inner.at[0], o_inner.at[0])
    stage_down(1)
    for m in range(mbs):
        lrow = jnp.transpose(lcol[m], (1, 0))
        lcol[m, 0:8, 0:128] = lrow[0:8, 0:128]
        for j in range(1, seq // 128):
            lcol[m, 8 * j : 8 * j + 8, 0:128] = lrow[0:8, 128 * j : 128 * j + 128]
        ocopy(lcol.at[m, pl.ds(0, seq // 16)], o_lrow.at[m])
    ocopy(mid.at[1], o_mid.at[1])
    ocopy(up.at[1], o_up.at[1])
    ocopy(gate.at[1], o_gate.at[1])
    ocopy(inner.at[1], o_inner.at[1])
    ocopy(attn, o_attn)
    for step in range(1, 3):
        gg.wait(step)
    stage_end(1)
    ocopy(outv, o_out)
    ocopy(gmd, o_gmd)
    ocopy(gm, o_gm)
    ocopy(acc, o_acc)
    gg.wait(3)
    ocopy(gm0, o_gm0)
    for gather in gx + gmi + [gg]:
        gather.drain()
    for copy in sends + small_t + small_d:
        copy.wait_send()
    for copy in outs:
        copy.wait()


def bwd_kernel(
    n,
    hid, table, irow, i_w, i_x, i_q, i_k, i_v, i_rq, i_rk, i_lrow, i_mixed, i_mid, i_up, i_gate,
    i_inner, i_attn, i_gmd, i_gm, i_gm0, i_vec, i_acc,
    o_in, o_gq, o_gk, o_gv, o_go, o_gu, o_gg, o_gd, o_tv,
    w, q, k, v, rq, rk, lrow, mixed, up, gate, inner, attn, gmd, gm, ga, vec, acc,
    tab, ir, kt, dqt, dk, dv, outv, xrecv, zrecv, vsend, vrecv, tv, sbuf, rbuf,
    lsem, agg_s, agg_r, aga_s, aga_r, rsm_s, rsm_r, rsi_s, rsi_r, xs, xr, zs, zr, vs, vr, osem,
):
    p = Place(n)
    nz = p.nz
    mbs, rows, width = hid.shape
    seq = q.shape[1]
    hw = q.shape[2]
    heads = hw // DH
    hidden = up.shape[2]
    groups = w.shape[0]
    shard = width // n
    gmix = [inner.at[m, :, pl.ds(0, hw)] for m in range(mbs)]
    pts, dss = (inner.at[m, pl.ds(0, seq - 128), pl.ds(hw, heads * QB)] for m in range(2))
    qs, gs = (
        inner.at[0, pl.ds(i * heads * QB, heads * QB), pl.ds(hw + heads * QB, hw)] for i in range(2)
    )

    local = []

    def lcopy(src, dst):
        copy = pltpu.make_async_copy(src, dst, lsem.at[len(local)])
        copy.start()
        local.append(copy)
        return copy

    outs = []

    def ocopy(src, dst):
        copy = pltpu.make_async_copy(src, dst, osem.at[len(outs)])
        copy.start()
        outs.append(copy)

    l_gm0 = lcopy(i_gm0, gm.at[0])
    l_w3 = lcopy(i_w.at[3], w.at[3])
    l_ug = [[lcopy(i_up.at[m], up.at[m]), lcopy(i_gate.at[m], gate.at[m])] for m in range(mbs)]
    l_vec = [lcopy(i_vec, vec), lcopy(i_acc, acc)]
    p.barrier()
    gg = Gather(p, gm.at[1], agg_s, agg_r, rows)
    gg.start(i_gm.at[1])
    l_gm1 = lcopy(i_gm.at[1], gg.at(p.t))
    l_w12 = [lcopy(i_w.at[1], w.at[1]), lcopy(i_w.at[2], w.at[2])]
    l_inner = [lcopy(i_inner.at[m], inner.at[m]) for m in range(mbs)]
    l_rows = [lcopy(i_attn, attn), lcopy(i_gmd, gmd)]
    l_w0 = lcopy(i_w.at[0], w.at[0])
    l_att = [
        [
            lcopy(src.at[m], dst.at[m])
            for src, dst in ((i_q, q), (i_k, k), (i_v, v), (i_rq, rq), (i_rk, rk), (i_lrow, lrow), (i_mixed, mixed))
        ]
        for m in range(mbs)
    ]
    l_tab = [lcopy(table, tab), lcopy(irow, ir)]

    gga = [Gather(p, ga.at[m], aga_s.at[m], aga_r.at[m], rows) for m in range(mbs)]
    l_hid = [lcopy(hid.at[m], gga[m].at(p.t)) for m in range(mbs)]
    sc_m = [Scatter(p, sbuf.at[m], rbuf.at[m], rsm_s.at[m], rsm_r.at[m]) for m in range(mbs)]
    sc_i = [Scatter(p, sbuf.at[m], rbuf.at[m], rsi_s.at[m], rsi_r.at[m]) for m in range(mbs)]
    cols = 256
    chunk = 32

    def stage_inner(m):
        for step, index in enumerate((p.t, p.sib, p.yp, p.diag)):
            if m == 1:
                gg.wait(step)
                if step == 0:
                    l_gm1.wait()
            at = pl.ds(pl.multiple_of(index * rows, rows), rows)

            def body(c, carry):
                lanes = pl.ds(pl.multiple_of(c * cols, cols), cols)
                gi = nn(gm[m, at, :], w[3, :, lanes])
                u = up[m, at, lanes].astype(F32)
                g = gate[m, at, lanes].astype(F32)
                su = vec[3:4, lanes]
                sg = vec[4:5, lanes]
                gsc = g * sg
                sig = 1.0 / (1.0 + jnp.exp(-gsc))
                gu = gi * (gsc * sig)
                ggs = gi * (u * su) * sig * (1.0 + gsc * (1.0 - sig))
                acc[16:24, lanes] += fold8(gu * u)
                acc[24:32, lanes] += fold8(ggs * g)
                up[m, at, lanes] = (gu * su).astype(BF16)
                gate[m, at, lanes] = (ggs * sg).astype(BF16)
                return carry

            lax.fori_loop(0, hidden // cols, body, 0)

    def stage_back(m):
        sc_m[m].run(
            lambda index: nt(rows_of(up.at[m], index, rows), w[1]) + nt(rows_of(gate.at[m], index, rows), w[2]),
            outv.at[m],
        )

    def stage_attn(m):
        sc_m[m].finish()
        base = p.t * rows

        def body(i, carry):
            at = pl.ds(pl.multiple_of(i * chunk, chunk), chunk)
            own = pl.ds(pl.multiple_of(base + i * chunk, chunk), chunk)
            cot = gmd[m, at, :] + outv[m, at, :] + rbuf[m, 2, at, :].astype(F32)
            a = attn[m, at, :]
            h = ga[m, own, :].astype(F32)
            ra = lax.rsqrt(mean_sq(a) + 1e-06)
            na = a * ra
            al = vec[1:2, :]
            zz = h + al * (na - h)
            rz = lax.rsqrt(mean_sq(zz) + 1e-06)
            out = zz * rz
            dz = rz * (cot - out * jnp.mean(cot * out, axis=-1, keepdims=True))
            dn = al * dz
            acc[8:16, :] += fold8(dz * (na - h))
            gmd[m, at, :] = dz - dn
            ga[m, own, :] = (ra * (dn - na * jnp.mean(dn * na, axis=-1, keepdims=True))).astype(BF16)
            return carry

        lax.fori_loop(0, rows // chunk, body, 0)
        gga[m].start(gga[m].at(p.t))

    def stage_mixed(m):
        for step, index in enumerate(gga[m].order()):
            gga[m].wait(step)
            at = pl.ds(pl.multiple_of(index * rows, rows), rows)
            gmix[m][at, :] = nn(ga[m, at, :], w[0, :, 3 * hw : 4 * hw]).astype(BF16)

    win = seq - 128
    c_exp = math.sqrt(DH) * LOG2E
    ones = head_ones()

    def attend(m):
        kt[...] = jnp.transpose(k[m], (1, 0))
        dk[...] = jnp.zeros_like(dk)
        dv[...] = jnp.zeros_like(dv)

        def body(b, carry):
            at = pl.ds(pl.multiple_of(b * QB, QB), QB)
            keys = pl.ds(pl.multiple_of(((b + 3) // 8) * 128, 128), win)
            crow = ir[m, 0:1, at]
            lrow_ = ir[m, 1:2, at]
            ccol = tab[m, keys, DH : DH + 1]
            bias = jnp.where((ccol <= crow) & (ccol >= lrow_), 0.0, -1e30)
            qb = q[m, at, :]
            gb = gmix[m][at, :]
            lane = lane_iota((QB, hw)) // DH
            for h in range(heads):
                qs[h * QB : (h + 1) * QB, :] = jnp.where(lane == h, qb, jnp.zeros_like(qb))
                gs[h * QB : (h + 1) * QB, :] = jnp.where(lane == h, gb, jnp.zeros_like(gb))
            kb = k[m, keys, :]
            vb = v[m, keys, :]
            for h in range(heads):
                hl = slice(h * QB, (h + 1) * QB)
                scores = nt(kb, qs[hl, :])
                inv = lrow[m, pl.ds(pl.multiple_of(b * 8, 8), 8), :][h : h + 1, :]
                pt = jnp.exp2(scores * c_exp + bias) * inv
                dpt = nt(vb, gs[hl, :])
                delta = jnp.sum(pt * dpt, axis=0, keepdims=True)
                dst = (pt * (dpt - delta)).astype(BF16)
                pts[:, hl] = pt.astype(BF16)
                dss[:, hl] = dst
                dqt[h * DH : (h + 1) * DH, at] = nn(kt[h * DH : (h + 1) * DH, keys], dst)
            dv[keys, :] += nn(pts[...], gs[...])
            dk[keys, :] += nn(dss[...], qs[...])
            return carry

        lax.fori_loop(0, seq // QB, body, 0)

        step = 256

        def after(i, carry):
            at = pl.ds(pl.multiple_of(i * step, step), step)
            cb, sb = turns(tab[m, at, :])
            v[m, at, :] = dv[at, :].astype(BF16)
            for which in range(2):
                src = (q, k)[which]
                rsc = (rq, rk)[which]
                for half in range(hw // 128):
                    lanes = slice(128 * half, 128 * half + 128)
                    if which == 0:
                        grad = jnp.transpose(dqt[lanes, at], (1, 0)) * math.sqrt(DH)
                    else:
                        grad = dk[at, lanes] * math.sqrt(DH)
                    gain = vec[0:1, lanes]
                    unit = src[m, at, lanes].astype(F32) / gain
                    acc[32:40, lanes] += fold8(grad * unit)
                    dn = grad * gain
                    dy = rsc[m, at, lanes].astype(F32) * (dn - unit * split_sum(dn * unit, ones))
                    src[m, at, lanes] = (dy * cb - partner(dy) * sb).astype(BF16)
            return carry

        lax.fori_loop(0, seq // step, after, 0)

    def stage_in(m):
        def part(index):
            at = pl.ds(pl.multiple_of(index * rows, rows), rows)
            return (
                nt(q[m, at, :], w[0, :, 0:hw])
                + nt(k[m, at, :], w[0, :, hw : 2 * hw])
                + nt(v[m, at, :], w[0, :, 2 * hw : 3 * hw])
            )

        sc_i[m].run(part, outv.at[m])

    def stage_out(m):
        sc_i[m].finish()

        def body(i, carry):
            at = pl.ds(pl.multiple_of(i * chunk, chunk), chunk)
            total = gmd[m, at, :] + outv[m, at, :] + rbuf[m, 2, at, :].astype(F32)
            sbuf[m, 0, at, :] = total.astype(BF16)
            return carry

        lax.fori_loop(0, rows // chunk, body, 0)
        ocopy(sbuf.at[m, 0], o_in.at[m])

    def weight_grad(g, left, rights):
        def body(c, carry):
            lanes = pl.ds(pl.multiple_of(c * cols, cols), cols)
            for lo, hi, right in rights:
                total = tn(left[0, :, lanes], right[0])
                for m in range(1, mbs):
                    total = total + tn(left[m, :, lanes], right[m])
                w[g, lanes, lo:hi] = total.astype(BF16)
            return carry

        lax.fori_loop(0, width // cols, body, 0)

    def wrow(g, index):
        return w.at[g, pl.ds(pl.multiple_of(index * shard, shard), shard)]

    gsends = []

    def rs_start(g):
        for kk in range(nz):
            zz = (p.z + kk) % nz
            other = 2 * zz + 1 - p.xi
            copy = remote(wrow(g, other), xrecv.at[g, zz], xs.at[g, kk], xr.at[g, zz], dp=p.xn)
            copy.start()
            gsends.append(copy)

    def rs_mid(g):
        for kk in range(nz - 1, -1, -1):
            zz = (p.z + kk) % nz
            remote(xrecv.at[g, zz], xrecv.at[g, zz], xs.at[g, kk], xr.at[g, zz], dp=p.xn).wait_recv()
            if kk:
                mine = 2 * zz + p.xi
                xrecv[g, zz] = (
                    xrecv[g, zz].astype(F32) + rows_of(w.at[g], mine, shard).astype(F32)
                ).astype(BF16)
                copy = remote(
                    xrecv.at[g, zz], zrecv.at[g, kk - 1], zs.at[g, kk - 1], zr.at[g, kk - 1], dp=mine
                )
                copy.start()
                gsends.append(copy)

    def rs_end(g):
        total = xrecv[g, p.z].astype(F32) + rows_of(w.at[g], p.d, shard).astype(F32)
        for kk in range(1, nz):
            remote(zrecv.at[g, kk - 1], zrecv.at[g, kk - 1], zs.at[g, kk - 1], zr.at[g, kk - 1], dp=p.xn).wait_recv()
            total = total + zrecv[g, kk - 1].astype(F32)
        fin = attn.at[g // 2, pl.ds((g % 2) * shard, shard)]
        fin[...] = total
        if g == 0:
            for i, dst in enumerate((o_gq, o_gk, o_gv, o_go)):
                ocopy(fin.at[:, pl.ds(i * hw, hw)], dst)
        else:
            ocopy(fin, (o_gu, o_gg, o_gd)[g - 1])

    for copy in l_vec + [l_gm0, l_w3] + l_ug[0]:
        copy.wait()
    stage_inner(0)
    for copy in l_w12:
        copy.wait()
    stage_back(0)
    for copy in l_ug[1]:
        copy.wait()
    stage_inner(1)
    stage_back(1)
    for copy in l_inner + l_rows + l_hid:
        copy.wait()
    stage_attn(0)
    weight_grad(3, gm, [(0, hidden, inner)])
    rs_start(3)
    gg.drain()
    l_mid = [lcopy(i_mid.at[m], gm.at[m]) for m in range(mbs)]
    stage_attn(1)
    for copy in l_mid:
        copy.wait()
    weight_grad(1, gm, [(0, hidden, up)])
    rs_start(1)
    l_x = [lcopy(i_x.at[m], up.at[m]) for m in range(mbs)]
    for copy in [l_w0] + l_tab + l_att[0] + l_att[1]:
        copy.wait()
    stage_mixed(0)
    attend(0)
    rs_mid(3)
    stage_in(0)
    stage_mixed(1)
    weight_grad(2, gm, [(0, hidden, gate)])
    rs_start(2)
    rs_mid(1)
    attend(1)
    stage_in(1)
    rs_mid(2)
    for copy in l_x:
        copy.wait()
    weight_grad(0, up, [(0, hw, q), (hw, 2 * hw, k), (2 * hw, 3 * hw, v)])
    weight_grad(0, ga, [(3 * hw, 4 * hw, mixed)])
    rs_start(0)

    per = width // 128
    for r in range(5):
        sums = jnp.sum(acc[8 * r : 8 * r + 8, :], axis=0, keepdims=True)
        for j in range(per):
            vsend[per * r + j : per * r + j + 1, :] = sums[:, 128 * j : 128 * j + 128]
    vcopies = []
    for i, peer in enumerate(p.dpeers):
        copy = remote(vsend, vrecv.at[i], vs.at[i], vr.at[i], dp=peer)
        copy.start()
        vcopies.append(copy)
    stage_out(0)
    stage_out(1)
    rs_end(3)
    rs_end(1)
    total = vsend[...]
    for i in range(n - 1):
        remote(vrecv.at[i], vrecv.at[i], vs.at[i], vr.at[i], dp=p.xn).wait_recv()
        total = total + vrecv[i]
    tv[p.t] = total
    for i, peer in enumerate(p.tpeers):
        copy = remote(tv.at[p.t], tv.at[p.t], vs.at[n - 1 + i], vr.at[n - 1 + i], tensor=peer)
        copy.start()
        vcopies.append(copy)
    rs_mid(0)
    rs_end(2)
    for i, peer in enumerate(p.tpeers):
        src = (p.t + 4 - (i + 1)) % 4
        remote(tv.at[src], tv.at[src], vs.at[n - 1 + i], vr.at[n - 1 + i], tensor=peer).wait_recv()
    ocopy(tv, o_tv)
    rs_end(0)
    for gather in gga:
        gather.drain()
    for copy in gsends + vcopies:
        copy.wait_send()
    for copy in outs:
        copy.wait()


def shards(
    hidden_in, out_grad, doc_ids, w_query, w_key, w_value, w_output, w_up, w_gate, w_down,
    scale_qk, alpha_attn, alpha_mlp, scale_up, scale_gate,
):
    n = lax.axis_size("dp")
    mbs, rows, width = hidden_in.shape
    seq = doc_ids.shape[2]
    hw = w_query.shape[1]
    hidden = w_up.shape[1]
    shard = w_query.shape[0]
    nz = n // 2
    flat = 4 * lax.axis_index("dp") + lax.axis_index("tensor")

    wsh = jnp.stack(
        [
            jnp.concatenate([w_query, w_key, w_value, w_output.T], axis=1),
            w_up,
            w_gate,
            w_down.T,
        ]
    )

    def placed(vals):
        start = (flat * vals.shape[0]) % 128
        return lax.dynamic_update_slice(jnp.zeros((128,), F32), vals, (start,))

    zero = jnp.zeros((128,), F32)
    small = jnp.stack(
        [placed(item) for item in (scale_qk, alpha_attn, alpha_mlp, scale_up, scale_gate)] + [zero] * 3
    )
    docs = doc_ids[:, 0, :]
    places = doc_places(docs)
    steps = jnp.arange(DH // 2, dtype=F32) / (DH // 2)
    freqs = jnp.exp(-math.log(10000.0) * steps)
    turn = places.astype(F32)[..., None] * freqs
    cosine, sine = jnp.cos(turn), jnp.sin(turn)
    code = (docs * CODE + places // BLOCK).astype(F32)
    low = (docs * CODE).astype(F32)
    table = jnp.concatenate(
        [cosine, sine, code[..., None], low[..., None], jnp.zeros(code.shape + (126 - DH,), F32)], axis=-1
    )
    irow = jnp.stack([code, low] + [code] * 6, axis=1)

    any_ = pl.BlockSpec(memory_space=pl.ANY)
    vm = pltpu.VMEM
    dma = pltpu.SemaphoreType.DMA

    def sds(shape, dtype):
        return jax.ShapeDtypeStruct(shape, dtype)

    res_shapes = dict(
        out=((mbs, rows, width), BF16),
        w=((4, width, width), BF16),
        x=((mbs, seq, width), BF16),
        q=((mbs, seq, hw), BF16),
        k=((mbs, seq, hw), BF16),
        v=((mbs, seq, hw), BF16),
        rq=((mbs, seq, hw), BF16),
        rk=((mbs, seq, hw), BF16),
        lrow=((mbs, seq // 16, 128), F32),
        mixed=((mbs, seq, hw), BF16),
        mid=((mbs, seq, width), BF16),
        up=((mbs, seq, hidden), BF16),
        gate=((mbs, seq, hidden), BF16),
        inner=((mbs, seq, hidden), BF16),
        attn=((mbs, rows, width), F32),
        gmd=((mbs, rows, width), F32),
        gm=((mbs, rows, width), BF16),
        gm0=((seq, width), BF16),
        vec=((8, width), F32),
        acc=((40, width), F32),
    )
    r = {key: sds(*val) for key, val in res_shapes.items()}
    s = {key: vm(*val) for key, val in res_shapes.items()}
    tabs = [vm((mbs, seq, 128), F32)]
    infos = [vm((mbs, 8, seq), F32)]
    nvec = 5 * (width // 128)
    own32 = vm((mbs, rows, width), F32)
    scat = [vm((mbs, 3, rows, width), BF16), vm((mbs, 3, rows, width), BF16)]
    heads = hw // DH
    res = pl.pallas_call(
        functools.partial(fwd_kernel, n),
        name="fwd",
        out_shape=tuple(r.values()),
        in_specs=[any_] * 6,
        out_specs=tuple([any_] * len(r)),
        scratch_shapes=[
            s["w"], s["x"], s["q"], s["k"], s["v"], s["rq"], s["rk"],
            vm((mbs, seq, 128), F32),
            s["mixed"], s["mid"], s["up"], s["gate"], s["inner"],
            s["attn"], own32, own32, s["gmd"], s["gm"], s["gm0"], s["vec"], s["acc"],
            vm((4 * n, 8, 128), F32),
            *tabs,
            vm((mbs, rows, width), BF16), vm((mbs, rows, width), BF16),
            *infos,
            vm((heads * QB, hw), BF16),
            *scat,
            dma((4, n)), dma((4, n)), dma((4,)),
            dma((n + 2,)), dma((n + 2,)),
            dma((16,)),
            dma((mbs, 3)), dma((mbs, 3)), dma((mbs, 3)), dma((mbs, 3)), dma((3,)), dma((3,)),
            dma((mbs, 3)), dma((mbs, 3)), dma((mbs, 3)), dma((mbs, 3)),
            dma((40,)),
        ],
        compiler_params=pltpu.CompilerParams(
            collective_id=0, has_side_effects=True, vmem_limit_bytes=VMEM_LIMIT
        ),
    )(wsh, hidden_in, out_grad, small, table, irow)
    r = dict(zip(r, res))

    gshape = sds((shard, hw), F32)
    fshape = sds((shard, hidden), F32)
    grads = pl.pallas_call(
        functools.partial(bwd_kernel, n),
        name="bwd",
        out_shape=(
            sds((mbs, rows, width), BF16), gshape, gshape, gshape, gshape, fshape, fshape, fshape,
            sds((4, nvec, 128), F32),
        ),
        in_specs=[any_] * 22,
        out_specs=tuple([any_] * 9),
        scratch_shapes=[
            s["w"], s["q"], s["k"], s["v"], s["rq"], s["rk"], s["lrow"], s["mixed"],
            s["up"], s["gate"], s["inner"], s["attn"], s["gmd"],
            s["x"], s["x"], s["vec"], s["acc"],
            *tabs, *infos,
            vm((hw, seq), BF16), vm((hw, seq), F32), vm((seq, hw), F32), vm((seq, hw), F32),
            own32,
            vm((4, nz, shard, width), BF16), vm((4, nz - 1, shard, width), BF16),
            vm((nvec, 128), F32), vm((n - 1, nvec, 128), F32), vm((4, nvec, 128), F32),
            *scat,
            dma((48,)), dma((3,)), dma((3,)), dma((mbs, 3)), dma((mbs, 3)),
            dma((mbs, 3)), dma((mbs, 3)), dma((mbs, 3)), dma((mbs, 3)),
            dma((4, nz)), dma((4, nz)), dma((4, nz - 1)), dma((4, nz - 1)),
            dma((n + 2,)), dma((n + 2,)),
            dma((16,)),
        ],
        compiler_params=pltpu.CompilerParams(
            collective_id=1, has_side_effects=True, vmem_limit_bytes=VMEM_LIMIT
        ),
    )(
        hidden_in, table, irow, r["w"], r["x"], r["q"], r["k"], r["v"], r["rq"], r["rk"], r["lrow"],
        r["mixed"], r["mid"], r["up"], r["gate"], r["inner"], r["attn"], r["gmd"], r["gm"], r["gm0"],
        r["vec"], r["acc"],
    )
    g_in, gq, gk, gv, go, gu, gg, gd, tv = grads
    tv = tv.reshape(4, 5, width)
    total = jnp.sum(tv, axis=0)

    def own_part(flat_vals, size):
        return lax.dynamic_slice_in_dim(flat_vals, flat * size, size)

    one = scale_qk.shape[0]
    big = scale_up.shape[0]
    return (
        r["out"], g_in, gq, gk, gv, go.T, gu, gg, gd.T,
        own_part(tv[:, 4, :hw].reshape(-1), one),
        own_part(total[1], one),
        own_part(total[0], one),
        own_part(tv[:, 2, :].reshape(-1), big),
        own_part(tv[:, 3, :].reshape(-1), big),
    )


def solution(mesh):
    rows = P("dp", "tensor", None)
    inward = P("dp", "tensor")
    outward = P("tensor", "dp")
    flat = P(("dp", "tensor"))
    weights = (inward, inward, inward, outward, inward, inward, outward)
    in_specs = (rows, rows, P("dp", None, None)) + weights + (flat,) * 5
    out_specs = (rows, rows) + weights + (flat,) * 5
    return jax.shard_map(shards, mesh=mesh, in_specs=in_specs, out_specs=out_specs, check_vma=False)
```

```python
import functools
import math

import jax
import jax.numpy as jnp
from jax import lax
from jax.experimental import pallas as pl
from jax.experimental.pallas import tpu as pltpu
from jax.sharding import PartitionSpec as P

DH = 64
BLOCK = 256
DOCS = 3
DOC_MAX = 512
F32 = jnp.float32
BF16 = jnp.bfloat16
MESH = pl.DeviceIdType.MESH
VMEM_LIMIT = 67043328
LOG2E = 1.4426950408889634
QB = 128
CODE = 8


def doc_places(docs):
    labels = jnp.arange(DOCS, dtype=jnp.int32)
    member = (docs[..., :, None] == labels).astype(jnp.int32)
    counts = jnp.sum(member, axis=-2)
    starts = jnp.cumsum(counts, axis=-1) - counts
    first = jnp.sum(member * starts[..., None, :], axis=-1)
    return jnp.arange(docs.shape[-1], dtype=jnp.int32) - first


def nn(a, b):
    return jnp.dot(a, b, preferred_element_type=F32)


def nt(a, b):
    return lax.dot_general(a, b, (((1,), (1,)), ((), ())), preferred_element_type=F32)


def tn(a, b):
    return lax.dot_general(a, b, (((0,), (0,)), ((), ())), preferred_element_type=F32)


def split_sum(vals, ones):
    high = vals.astype(BF16)
    low = (vals - high.astype(F32)).astype(BF16)
    return nn(high, ones) + nn(low, ones)


def lane_iota(shape):
    return lax.broadcasted_iota(jnp.int32, shape, len(shape) - 1)


def head_ones():
    rows = lax.broadcasted_iota(jnp.int32, (128, 128), 0) // DH
    cols = lax.broadcasted_iota(jnp.int32, (128, 128), 1) // DH
    return jnp.where(rows == cols, 1.0, 0.0).astype(BF16)


def partner(vals):
    low = lane_iota(vals.shape) % DH < DH // 2
    return jnp.where(low, pltpu.roll(vals, 128 - DH // 2, 1), pltpu.roll(vals, DH // 2, 1))


def turns(table):
    lane = lane_iota(table.shape)
    both = jnp.where(lane < DH, table, pltpu.roll(table, DH, 1))
    low = lane % DH < DH // 2
    cosine = jnp.where(low, both, pltpu.roll(both, DH // 2, 1))
    sine = jnp.where(low, -pltpu.roll(both, 128 - DH // 2, 1), both)
    return cosine, sine


class Place:
    def __init__(self, n):
        self.n = n
        self.t = lax.axis_index("tensor")
        self.d = lax.axis_index("dp")
        t, d = self.t, self.d
        self.sib = t + 1 - 2 * (t % 2)
        self.yp = (t + 2) % 4
        self.diag = (self.sib + 2) % 4
        self.xi = d % 2
        self.z = d // 2
        self.nz = n // 2
        self.xn = d + 1 - 2 * (d % 2)
        self.zpeers = [2 * ((self.z + k) % self.nz) + self.xi for k in range(1, self.nz)]
        self.dpeers = [(d + k) % n for k in range(1, n)]
        self.tpeers = [(t + k) % 4 for k in range(1, 4)]

    def barrier(self):
        sem = pltpu.get_barrier_semaphore()
        for peer in self.dpeers:
            pl.semaphore_signal(sem, inc=1, device_id={"dp": peer}, device_id_type=MESH)
        for peer in self.tpeers:
            pl.semaphore_signal(sem, inc=1, device_id={"tensor": peer}, device_id_type=MESH)
        pl.semaphore_wait(sem, self.n + 2)


def remote(src, dst, ssem, rsem, **where):
    return pltpu.make_async_remote_copy(
        src_ref=src, dst_ref=dst, send_sem=ssem, recv_sem=rsem, device_id=where, device_id_type=MESH
    )


class Gather:
    def __init__(self, place, whole, ssem, rsem, rows):
        self.p, self.whole, self.ssem, self.rsem, self.rows = place, whole, ssem, rsem, rows

    def at(self, index):
        return self.whole.at[pl.ds(pl.multiple_of(index * self.rows, self.rows), self.rows)]

    def start(self, own):
        p = self.p
        self.c_yp = remote(own, self.at(p.t), self.ssem.at[1], self.rsem.at[1], tensor=p.yp)
        self.c_sib = remote(own, self.at(p.t), self.ssem.at[0], self.rsem.at[0], tensor=p.sib)
        self.c_yp.start()
        self.c_sib.start()

    def wait(self, step):
        p = self.p
        if step == 1:
            remote(self.at(p.sib), self.at(p.sib), self.ssem.at[0], self.rsem.at[0], tensor=p.sib).wait_recv()
        if step == 2:
            remote(self.at(p.yp), self.at(p.yp), self.ssem.at[1], self.rsem.at[1], tensor=p.yp).wait_recv()
            self.c_fwd = remote(
                self.at(p.yp), self.at(p.yp), self.ssem.at[2], self.rsem.at[2], tensor=p.sib
            )
            self.c_fwd.start()
        if step == 3:
            remote(self.at(p.diag), self.at(p.diag), self.ssem.at[2], self.rsem.at[2], tensor=p.sib).wait_recv()

    def drain(self):
        self.c_yp.wait_send()
        self.c_sib.wait_send()
        self.c_fwd.wait_send()

    def order(self):
        p = self.p
        return (p.t, p.sib, p.yp, p.diag)


class Scatter:
    def __init__(self, place, sbuf, rbuf, ssem, rsem):
        self.p, self.sbuf, self.rbuf, self.ssem, self.rsem = place, sbuf, rbuf, ssem, rsem
        self.copies = []

    def send(self, slot, **where):
        copy = remote(
            self.sbuf.at[slot], self.rbuf.at[slot], self.ssem.at[slot], self.rsem.at[slot], **where
        )
        copy.start()
        self.copies.append(copy)

    def arrive(self, slot):
        remote(
            self.rbuf.at[slot], self.rbuf.at[slot], self.ssem.at[slot], self.rsem.at[slot],
            tensor=self.p.sib,
        ).wait_recv()

    def run(self, part, own):
        p = self.p
        self.sbuf[0] = part(p.diag).astype(BF16)
        self.send(0, tensor=p.sib)
        self.sbuf[1] = part(p.sib).astype(BF16)
        self.send(1, tensor=p.sib)
        across = part(p.yp)
        self.arrive(0)
        self.sbuf[2] = (across + self.rbuf[0].astype(F32)).astype(BF16)
        self.send(2, tensor=p.yp)
        mine = part(p.t)
        self.arrive(1)
        own[...] = mine + self.rbuf[1].astype(F32)

    def finish(self):
        self.arrive(2)
        for copy in self.copies:
            copy.wait_send()


def rows_of(ref, index, rows):
    return ref[pl.ds(pl.multiple_of(index * rows, rows), rows)]


def mean_sq(vals):
    return jnp.mean(vals * vals, axis=-1, keepdims=True)


def fold8(vals):
    total = vals[0:8]
    for k in range(1, vals.shape[0] // 8):
        total = total + vals[8 * k : 8 * k + 8]
    return total


def fwd_kernel(
    n,
    wsh, hid, og, small, table, irow,
    o_out, o_w, o_x, o_q, o_k, o_v, o_rq, o_rk, o_lrow, o_mixed, o_mid, o_up, o_gate, o_inner,
    o_attn, o_gmd, o_gm, o_gm0, o_vec, o_acc,
    w, x, q, k, v, rq, rk, lcol, mixed, mid, up, gate, inner,
    attn, midf, mlp, gmd, gm, gm0, vec, acc, sall, tab, ogv, outv, ir, qm, sbuf, rbuf,
    wsend, wrecv, wloc, small_s, small_r, lsem, agx_s, agx_r, agm_s, agm_r, agg_s, agg_r,
    rsa_s, rsa_r, rsm_s, rsm_r, osem,
):
    p = Place(n)
    nz = p.nz
    mbs, rows, width = hid.shape
    seq = x.shape[1]
    hw = q.shape[2]
    shard = wsh.shape[1]
    heads = hw // DH
    groups = wsh.shape[0]
    hidden = up.shape[2]

    def wat(g, index):
        return w.at[g, pl.ds(pl.multiple_of(index * shard, shard), shard)]

    local = []

    def lcopy(src, dst):
        copy = pltpu.make_async_copy(src, dst, lsem.at[len(local)])
        copy.start()
        local.append(copy)
        return copy

    outs = []

    def ocopy(src, dst):
        copy = pltpu.make_async_copy(src, dst, osem.at[len(outs)])
        copy.start()
        outs.append(copy)

    p.barrier()

    gx = [Gather(p, x.at[m], agx_s.at[m], agx_r.at[m], rows) for m in range(mbs)]
    gmi = [Gather(p, mid.at[m], agm_s.at[m], agm_r.at[m], rows) for m in range(mbs)]
    slot = p.t * n + p.d
    small_own = lcopy(small, sall.at[slot])
    small_d = [
        remote(small, sall.at[slot], small_s.at[i], small_r.at[i], dp=peer)
        for i, peer in enumerate(p.dpeers)
    ]
    for copy in small_d:
        copy.start()
    gx[0].start(hid.at[0])
    sends = []

    def wsend_to(g, i, src, index, peer):
        copy = remote(src, wat(g, index), wsend.at[g, i], wrecv.at[g, index], dp=peer)
        copy.start()
        sends.append(copy)

    def relay(g):
        for i, peer in reversed(list(enumerate(p.zpeers))):
            remote(wat(g, peer), wat(g, peer), wsend.at[g, 0], wrecv.at[g, peer], dp=p.xn).wait_recv()
            wsend_to(g, nz + i, wat(g, peer), peer, p.xn)

    wown = []
    for g in range(groups):
        for i, peer in enumerate(p.zpeers):
            wsend_to(g, i, wsh.at[g], p.d, peer)
        if g == 0:
            wsend_to(0, nz - 1, wsh.at[0], p.d, p.xn)
    for g in range(groups):
        copy = pltpu.make_async_copy(wsh.at[g], wat(g, p.d), wloc.at[g])
        copy.start()
        wown.append(copy)
    xown = [lcopy(hid.at[m], gx[m].at(p.t)) for m in range(mbs)]
    tables = [lcopy(table, tab), lcopy(irow, ir)]
    og_in = lcopy(og, ogv)
    for i, peer in enumerate(p.dpeers):
        src = p.t * n + (p.d + n - (i + 1)) % n
        remote(sall.at[src], sall.at[src], small_s.at[i], small_r.at[i], dp=peer).wait_recv()
    small_own.wait()
    small_t = []
    for i, peer in enumerate(p.tpeers):
        part = sall.at[pl.ds(p.t * n, n)]
        copy = remote(part, part, small_s.at[n - 1 + i], small_r.at[n - 1 + i], tensor=peer)
        copy.start()
        small_t.append(copy)
    gx[1].start(hid.at[1])

    def wready(g):
        remote(wat(g, p.xn), wat(g, p.xn), wsend.at[g, 0], wrecv.at[g, p.xn], dp=p.xn).wait_recv()
        for peer in p.zpeers:
            other = peer + 1 - 2 * p.xi
            remote(wat(g, other), wat(g, other), wsend.at[g, 0], wrecv.at[g, other], dp=p.xn).wait_recv()
        wown[g].wait()
        ocopy(w.at[g], o_w.at[g])

    relay(0)
    for g in range(1, groups):
        wsend_to(g, nz - 1, wsh.at[g], p.d, p.xn)
    for i, peer in enumerate(p.tpeers):
        part = sall.at[pl.ds((p.t + 4 - (i + 1)) % 4 * n, n)]
        remote(part, part, small_s.at[n - 1 + i], small_r.at[n - 1 + i], tensor=peer).wait_recv()
    every = 4 * n

    def gathered(row, base, count, lanes):
        per = count // (lanes // 128)

        def item(k):
            return sall[k % 4 * n + base + k // 4, row : row + 1, :]

        for r in range(lanes // 128):
            total = item(r * per)
            for j in range(1, per):
                total = total + item(r * per + j)
            vec[row : row + 1, 128 * r : 128 * r + 128] = total

    gathered(0, p.t * (n // 4), n, hw)
    gathered(1, 0, every, width)
    gathered(2, 0, every, width)
    gathered(3, p.t * (n // 4), n, hidden)
    gathered(4, p.t * (n // 4), n, hidden)
    acc[...] = jnp.zeros_like(acc)
    for copy in tables:
        copy.wait()
    wready(0)

    ones = head_ones()

    def stage_qkv(m):
        for step, index in enumerate(gx[m].order()):
            gx[m].wait(step)
            if step == 0:
                xown[m].wait()
            at = pl.ds(pl.multiple_of(index * rows, rows), rows)
            xb = x[m, at, :]
            cb, sb = turns(tab[m, at, :])
            for which, (dst, rdst) in enumerate(((q, rq), (k, rk))):
                raw = nn(xb, w[0, :, which * hw : (which + 1) * hw])
                for half in range(hw // 128):
                    lanes = slice(128 * half, 128 * half + 128)
                    piece = raw[:, lanes]
                    turned = piece * cb + partner(piece) * sb
                    scale = lax.rsqrt(split_sum(turned * turned, ones) + 1e-06)
                    rdst[m, at, lanes] = scale.astype(BF16)
                    dst[m, at, lanes] = (turned * scale * vec[0:1, lanes]).astype(BF16)
            v[m, at, :] = nn(xb, w[0, :, 2 * hw : 3 * hw]).astype(BF16)

    win = seq - 128
    c_exp = math.sqrt(DH) * LOG2E

    def attend(m):
        def body(b, carry):
            at = pl.ds(pl.multiple_of(b * QB, QB), QB)
            keys = pl.ds(pl.multiple_of(((b + 3) // 8) * 128, 128), win)
            ccol = tab[m, at, DH : DH + 1]
            lcol_ = tab[m, at, DH + 1 : DH + 2]
            crow = ir[m, 0:1, keys]
            bias = jnp.where((crow <= ccol) & (crow >= lcol_), 0.0, -1e30)
            qb = q[m, at, :]
            lane = lane_iota((QB, hw)) // DH
            for h in range(heads):
                qm[h * QB : (h + 1) * QB, :] = jnp.where(lane == h, qb, jnp.zeros_like(qb))
            kb = k[m, keys, :]
            vb = v[m, keys, :]
            total = jnp.zeros((QB, hw), F32)
            lsum = jnp.zeros((QB, 128), F32)
            lane_l = lane_iota((QB, 128))
            for h in range(heads):
                scores = nt(qm[h * QB : (h + 1) * QB, :], kb)
                expo = jnp.exp2(scores * c_exp + bias)
                inv = 1.0 / jnp.sum(expo, axis=-1, keepdims=True)
                part = nn(expo.astype(BF16), vb)
                total = jnp.where(lane == h, part * inv, total)
                lsum = jnp.where(lane_l == h, inv, lsum)
            mixed[m, at, :] = total.astype(BF16)
            lcol[m, at, :] = lsum
            return carry

        lax.fori_loop(0, seq // QB, body, 0)

    sc_a = [Scatter(p, sbuf.at[m], rbuf.at[m], rsa_s.at[m], rsa_r.at[m]) for m in range(mbs)]
    sc_m = [Scatter(p, sbuf.at[m], rbuf.at[m], rsm_s.at[m], rsm_r.at[m]) for m in range(mbs)]

    def stage_o(m):
        sc_a[m].run(
            lambda index: nt(rows_of(mixed.at[m], index, rows), w[0, :, 3 * hw : 3 * hw + hw]),
            attn.at[m],
        )

    chunk = 32

    def stage_mid(m):
        sc_a[m].finish()
        base = p.t * rows

        def body(i, carry):
            at = pl.ds(pl.multiple_of(i * chunk, chunk), chunk)
            own = pl.ds(pl.multiple_of(base + i * chunk, chunk), chunk)
            a = attn[m, at, :] + rbuf[m, 2, at, :].astype(F32)
            attn[m, at, :] = a
            h = x[m, own, :].astype(F32)
            na = a * lax.rsqrt(mean_sq(a) + 1e-06)
            zz = h + vec[1:2, :] * (na - h)
            out = zz * lax.rsqrt(mean_sq(zz) + 1e-06)
            midf[m, at, :] = out
            mid[m, own, :] = out.astype(BF16)
            return carry

        lax.fori_loop(0, rows // chunk, body, 0)
        gmi[m].start(gmi[m].at(p.t))

    cols = 256

    def stage_up(m):
        for step, index in enumerate(gmi[m].order()):
            gmi[m].wait(step)
            at = pl.ds(pl.multiple_of(index * rows, rows), rows)

            def body(c, carry):
                lanes = pl.ds(pl.multiple_of(c * cols, cols), cols)
                mb = mid[m, at, :]
                u = nn(mb, w[1, :, lanes])
                g = nn(mb, w[2, :, lanes])
                up[m, at, lanes] = u.astype(BF16)
                gate[m, at, lanes] = g.astype(BF16)
                gs = g * vec[4:5, lanes]
                inner[m, at, lanes] = ((u * vec[3:4, lanes]) * (gs / (1.0 + jnp.exp(-gs)))).astype(BF16)
                return carry

            lax.fori_loop(0, hidden // cols, body, 0)

    def stage_down(m):
        sc_m[m].run(lambda index: nt(rows_of(inner.at[m], index, rows), w[3]), mlp.at[m])

    gg = Gather(p, gm0, agg_s, agg_r, rows)

    def stage_end(m):
        sc_m[m].finish()

        def body(i, carry):
            at = pl.ds(pl.multiple_of(i * chunk, chunk), chunk)
            a = mlp[m, at, :] + rbuf[m, 2, at, :].astype(F32)
            h = midf[m, at, :]
            ra = lax.rsqrt(mean_sq(a) + 1e-06)
            na = a * ra
            al = vec[2:3, :]
            zz = h + al * (na - h)
            rz = lax.rsqrt(mean_sq(zz) + 1e-06)
            out = zz * rz
            outv[m, at, :] = out.astype(BF16)
            cot = ogv[m, at, :].astype(F32)
            dz = rz * (cot - out * jnp.mean(cot * out, axis=-1, keepdims=True))
            dn = al * dz
            acc[0:8, :] += fold8(dz * (na - h))
            gmd[m, at, :] = dz - dn
            grad = (ra * (dn - na * jnp.mean(dn * na, axis=-1, keepdims=True))).astype(BF16)
            gm[m, at, :] = grad
            if m == 0:
                gm0[pl.ds(pl.multiple_of(p.t * rows + i * chunk, chunk), chunk), :] = grad
            return carry

        lax.fori_loop(0, rows // chunk, body, 0)
        if m == 0:
            gg.start(gg.at(p.t))

    stage_qkv(0)
    relay(1)
    attend(0)
    stage_o(0)
    stage_qkv(1)
    relay(2)
    stage_mid(0)
    attend(1)
    stage_o(1)
    relay(3)
    stage_mid(1)
    for m in range(mbs):
        ocopy(x.at[m], o_x.at[m])
        ocopy(q.at[m], o_q.at[m])
        ocopy(k.at[m], o_k.at[m])
        ocopy(v.at[m], o_v.at[m])
        ocopy(rq.at[m], o_rq.at[m])
        ocopy(rk.at[m], o_rk.at[m])
        ocopy(mixed.at[m], o_mixed.at[m])
    ocopy(vec, o_vec)
    wready(1)
    wready(2)
    stage_up(0)
    stage_up(1)
    wready(3)
    stage_down(0)
    stage_down(1)
    og_in.wait()
    stage_end(0)
    ocopy(mid.at[0], o_mid.at[0])
    ocopy(up.at[0], o_up.at[0])
    ocopy(gate.at[0], o_gate.at[0])
    ocopy(inner.at[0], o_inner.at[0])
    for m in range(mbs):
        lrow = jnp.transpose(lcol[m], (1, 0))
        lcol[m, 0:8, 0:128] = lrow[0:8, 0:128]
        for j in range(1, seq // 128):
            lcol[m, 8 * j : 8 * j + 8, 0:128] = lrow[0:8, 128 * j : 128 * j + 128]
        ocopy(lcol.at[m, pl.ds(0, seq // 16)], o_lrow.at[m])
    ocopy(mid.at[1], o_mid.at[1])
    ocopy(up.at[1], o_up.at[1])
    ocopy(gate.at[1], o_gate.at[1])
    ocopy(inner.at[1], o_inner.at[1])
    ocopy(attn, o_attn)
    for step in range(1, 3):
        gg.wait(step)
    stage_end(1)
    ocopy(outv, o_out)
    ocopy(gmd, o_gmd)
    ocopy(gm, o_gm)
    ocopy(acc, o_acc)
    gg.wait(3)
    ocopy(gm0, o_gm0)
    for gather in gx + gmi + [gg]:
        gather.drain()
    for copy in sends + small_t + small_d:
        copy.wait_send()
    for copy in outs:
        copy.wait()


def bwd_kernel(
    n,
    hid, table, irow, i_w, i_x, i_q, i_k, i_v, i_rq, i_rk, i_lrow, i_mixed, i_mid, i_up, i_gate,
    i_inner, i_attn, i_gmd, i_gm, i_gm0, i_vec, i_acc,
    o_in, o_gq, o_gk, o_gv, o_go, o_gu, o_gg, o_gd, o_tv,
    w, q, k, v, rq, rk, lrow, mixed, up, gate, inner, attn, gmd, gm, ga, vec, acc,
    tab, ir, kt, dqt, dk, dv, outv, xrecv, zrecv, vsend, vrecv, tv, sbuf, rbuf,
    lsem, agg_s, agg_r, aga_s, aga_r, rsm_s, rsm_r, rsi_s, rsi_r, xs, xr, zs, zr, vs, vr, osem,
):
    p = Place(n)
    nz = p.nz
    mbs, rows, width = hid.shape
    seq = q.shape[1]
    hw = q.shape[2]
    heads = hw // DH
    hidden = up.shape[2]
    groups = w.shape[0]
    shard = width // n
    gmix = [inner.at[m, :, pl.ds(0, hw)] for m in range(mbs)]
    pts, dss = (inner.at[m, pl.ds(0, seq - 128), pl.ds(hw, heads * QB)] for m in range(2))
    qs, gs = (
        inner.at[0, pl.ds(i * heads * QB, heads * QB), pl.ds(hw + heads * QB, hw)] for i in range(2)
    )

    local = []

    def lcopy(src, dst):
        copy = pltpu.make_async_copy(src, dst, lsem.at[len(local)])
        copy.start()
        local.append(copy)
        return copy

    outs = []

    def ocopy(src, dst):
        copy = pltpu.make_async_copy(src, dst, osem.at[len(outs)])
        copy.start()
        outs.append(copy)

    l_gm0 = lcopy(i_gm0, gm.at[0])
    l_w3 = lcopy(i_w.at[3], w.at[3])
    l_ug = [[lcopy(i_up.at[m], up.at[m]), lcopy(i_gate.at[m], gate.at[m])] for m in range(mbs)]
    l_vec = [lcopy(i_vec, vec), lcopy(i_acc, acc)]
    p.barrier()
    gg = Gather(p, gm.at[1], agg_s, agg_r, rows)
    gg.start(i_gm.at[1])
    l_gm1 = lcopy(i_gm.at[1], gg.at(p.t))
    l_w12 = [lcopy(i_w.at[1], w.at[1]), lcopy(i_w.at[2], w.at[2])]
    l_inner = [lcopy(i_inner.at[m], inner.at[m]) for m in range(mbs)]
    l_rows = [lcopy(i_attn, attn), lcopy(i_gmd, gmd)]
    l_w0 = lcopy(i_w.at[0], w.at[0])
    l_att = [
        [
            lcopy(src.at[m], dst.at[m])
            for src, dst in ((i_q, q), (i_k, k), (i_v, v), (i_rq, rq), (i_rk, rk), (i_lrow, lrow), (i_mixed, mixed))
        ]
        for m in range(mbs)
    ]
    l_tab = [lcopy(table, tab), lcopy(irow, ir)]

    gga = [Gather(p, ga.at[m], aga_s.at[m], aga_r.at[m], rows) for m in range(mbs)]
    l_hid = [lcopy(hid.at[m], gga[m].at(p.t)) for m in range(mbs)]
    sc_m = [Scatter(p, sbuf.at[m], rbuf.at[m], rsm_s.at[m], rsm_r.at[m]) for m in range(mbs)]
    sc_i = [Scatter(p, sbuf.at[m], rbuf.at[m], rsi_s.at[m], rsi_r.at[m]) for m in range(mbs)]
    cols = 256
    chunk = 32

    def stage_inner(m):
        for step, index in enumerate((p.t, p.sib, p.yp, p.diag)):
            if m == 1:
                gg.wait(step)
                if step == 0:
                    l_gm1.wait()
            at = pl.ds(pl.multiple_of(index * rows, rows), rows)

            def body(c, carry):
                lanes = pl.ds(pl.multiple_of(c * cols, cols), cols)
                gi = nn(gm[m, at, :], w[3, :, lanes])
                u = up[m, at, lanes].astype(F32)
                g = gate[m, at, lanes].astype(F32)
                su = vec[3:4, lanes]
                sg = vec[4:5, lanes]
                gsc = g * sg
                sig = 1.0 / (1.0 + jnp.exp(-gsc))
                gu = gi * (gsc * sig)
                ggs = gi * (u * su) * sig * (1.0 + gsc * (1.0 - sig))
                acc[16:24, lanes] += fold8(gu * u)
                acc[24:32, lanes] += fold8(ggs * g)
                up[m, at, lanes] = (gu * su).astype(BF16)
                gate[m, at, lanes] = (ggs * sg).astype(BF16)
                return carry

            lax.fori_loop(0, hidden // cols, body, 0)

    def stage_back(m):
        sc_m[m].run(
            lambda index: nt(rows_of(up.at[m], index, rows), w[1]) + nt(rows_of(gate.at[m], index, rows), w[2]),
            outv.at[m],
        )

    def stage_attn(m):
        sc_m[m].finish()
        base = p.t * rows

        def body(i, carry):
            at = pl.ds(pl.multiple_of(i * chunk, chunk), chunk)
            own = pl.ds(pl.multiple_of(base + i * chunk, chunk), chunk)
            cot = gmd[m, at, :] + outv[m, at, :] + rbuf[m, 2, at, :].astype(F32)
            a = attn[m, at, :]
            h = ga[m, own, :].astype(F32)
            ra = lax.rsqrt(mean_sq(a) + 1e-06)
            na = a * ra
            al = vec[1:2, :]
            zz = h + al * (na - h)
            rz = lax.rsqrt(mean_sq(zz) + 1e-06)
            out = zz * rz
            dz = rz * (cot - out * jnp.mean(cot * out, axis=-1, keepdims=True))
            dn = al * dz
            acc[8:16, :] += fold8(dz * (na - h))
            gmd[m, at, :] = dz - dn
            ga[m, own, :] = (ra * (dn - na * jnp.mean(dn * na, axis=-1, keepdims=True))).astype(BF16)
            return carry

        lax.fori_loop(0, rows // chunk, body, 0)
        gga[m].start(gga[m].at(p.t))

    def stage_mixed(m):
        for step, index in enumerate(gga[m].order()):
            gga[m].wait(step)
            at = pl.ds(pl.multiple_of(index * rows, rows), rows)
            gmix[m][at, :] = nn(ga[m, at, :], w[0, :, 3 * hw : 4 * hw]).astype(BF16)

    win = seq - 128
    c_exp = math.sqrt(DH) * LOG2E
    ones = head_ones()

    def attend(m):
        kt[...] = jnp.transpose(k[m], (1, 0))
        dk[...] = jnp.zeros_like(dk)
        dv[...] = jnp.zeros_like(dv)

        def body(b, carry):
            at = pl.ds(pl.multiple_of(b * QB, QB), QB)
            keys = pl.ds(pl.multiple_of(((b + 3) // 8) * 128, 128), win)
            crow = ir[m, 0:1, at]
            lrow_ = ir[m, 1:2, at]
            ccol = tab[m, keys, DH : DH + 1]
            bias = jnp.where((ccol <= crow) & (ccol >= lrow_), 0.0, -1e30)
            qb = q[m, at, :]
            gb = gmix[m][at, :]
            lane = lane_iota((QB, hw)) // DH
            for h in range(heads):
                qs[h * QB : (h + 1) * QB, :] = jnp.where(lane == h, qb, jnp.zeros_like(qb))
                gs[h * QB : (h + 1) * QB, :] = jnp.where(lane == h, gb, jnp.zeros_like(gb))
            kb = k[m, keys, :]
            vb = v[m, keys, :]
            for h in range(heads):
                hl = slice(h * QB, (h + 1) * QB)
                scores = nt(kb, qs[hl, :])
                inv = lrow[m, pl.ds(pl.multiple_of(b * 8, 8), 8), :][h : h + 1, :]
                pt = jnp.exp2(scores * c_exp + bias) * inv
                dpt = nt(vb, gs[hl, :])
                delta = jnp.sum(pt * dpt, axis=0, keepdims=True)
                dst = (pt * (dpt - delta)).astype(BF16)
                pts[:, hl] = pt.astype(BF16)
                dss[:, hl] = dst
                dqt[h * DH : (h + 1) * DH, at] = nn(kt[h * DH : (h + 1) * DH, keys], dst)
            dv[keys, :] += nn(pts[...], gs[...])
            dk[keys, :] += nn(dss[...], qs[...])
            return carry

        lax.fori_loop(0, seq // QB, body, 0)

        step = 256

        def after(i, carry):
            at = pl.ds(pl.multiple_of(i * step, step), step)
            cb, sb = turns(tab[m, at, :])
            v[m, at, :] = dv[at, :].astype(BF16)
            for which in range(2):
                src = (q, k)[which]
                rsc = (rq, rk)[which]
                for half in range(hw // 128):
                    lanes = slice(128 * half, 128 * half + 128)
                    if which == 0:
                        grad = jnp.transpose(dqt[lanes, at], (1, 0)) * math.sqrt(DH)
                    else:
                        grad = dk[at, lanes] * math.sqrt(DH)
                    gain = vec[0:1, lanes]
                    unit = src[m, at, lanes].astype(F32) / gain
                    acc[32:40, lanes] += fold8(grad * unit)
                    dn = grad * gain
                    dy = rsc[m, at, lanes].astype(F32) * (dn - unit * split_sum(dn * unit, ones))
                    src[m, at, lanes] = (dy * cb - partner(dy) * sb).astype(BF16)
            return carry

        lax.fori_loop(0, seq // step, after, 0)

    def stage_in(m):
        def part(index):
            at = pl.ds(pl.multiple_of(index * rows, rows), rows)
            return (
                nt(q[m, at, :], w[0, :, 0:hw])
                + nt(k[m, at, :], w[0, :, hw : 2 * hw])
                + nt(v[m, at, :], w[0, :, 2 * hw : 3 * hw])
            )

        sc_i[m].run(part, outv.at[m])

    def stage_out(m):
        sc_i[m].finish()

        def body(i, carry):
            at = pl.ds(pl.multiple_of(i * chunk, chunk), chunk)
            total = gmd[m, at, :] + outv[m, at, :] + rbuf[m, 2, at, :].astype(F32)
            sbuf[m, 0, at, :] = total.astype(BF16)
            return carry

        lax.fori_loop(0, rows // chunk, body, 0)
        ocopy(sbuf.at[m, 0], o_in.at[m])

    pieces = {
        3: (w.at[3], 3, 0, width),
        1: (w.at[1], 1, 0, width),
        2: (w.at[2], 2, 0, width),
        0: (gm.at[0], 0, 0, 3 * hw),
        4: (gm.at[0], 0, 3 * hw, 4 * hw),
    }

    def weight_grad(key, left, rights):
        into = pieces[key][0]

        def body(c, carry):
            lanes = pl.ds(pl.multiple_of(c * cols, cols), cols)
            for lo, hi, right in rights:
                total = tn(left[0, :, lanes], right[0])
                for m in range(1, mbs):
                    total = total + tn(left[m, :, lanes], right[m])
                into[lanes, lo:hi] = total.astype(BF16)
            return carry

        lax.fori_loop(0, width // cols, body, 0)

    def wrow(key, index):
        ref, _, lo, hi = pieces[key]
        return ref.at[pl.ds(pl.multiple_of(index * shard, shard), shard), pl.ds(lo, hi - lo)]

    def held(buf, key, index):
        _, g, lo, hi = pieces[key]
        return buf.at[g, index, :, pl.ds(lo, hi - lo)]

    gsends = []

    def rs_start(key):
        for kk in list(range(1, nz)) + [0]:
            zz = (p.z + kk) % nz
            other = 2 * zz + 1 - p.xi
            copy = remote(wrow(key, other), held(xrecv, key, zz), xs.at[key, kk], xr.at[key, zz], dp=p.xn)
            copy.start()
            gsends.append(copy)

    def rs_arrive(key, kk):
        zz = (p.z + kk) % nz
        got = held(xrecv, key, zz)
        remote(got, got, xs.at[key, kk], xr.at[key, zz], dp=p.xn).wait_recv()
        return got, zz

    def rs_mid(key):
        for kk in range(1, nz):
            got, zz = rs_arrive(key, kk)
            mine = 2 * zz + p.xi
            got[...] = (got[...].astype(F32) + wrow(key, mine)[...].astype(F32)).astype(BF16)
            copy = remote(got, held(zrecv, key, kk - 1), zs.at[key, kk - 1], zr.at[key, kk - 1], dp=mine)
            copy.start()
            gsends.append(copy)

    def rs_end(key):
        _, g, lo, hi = pieces[key]
        got, _ = rs_arrive(key, 0)
        total = got[...].astype(F32) + wrow(key, p.d)[...].astype(F32)
        for kk in range(1, nz):
            got = held(zrecv, key, kk - 1)
            remote(got, got, zs.at[key, kk - 1], zr.at[key, kk - 1], dp=p.xn).wait_recv()
            total = total + got[...].astype(F32)
        fin = attn.at[g // 2, pl.ds((g % 2) * shard, shard)]
        fin[:, lo:hi] = total
        if g == 0:
            for i, dst in enumerate((o_gq, o_gk, o_gv, o_go)):
                if lo <= i * hw < hi:
                    ocopy(fin.at[:, pl.ds(i * hw, hw)], dst)
        else:
            ocopy(fin, (o_gu, o_gg, o_gd)[g - 1])

    for copy in l_vec + [l_gm0, l_w3] + l_ug[0]:
        copy.wait()
    stage_inner(0)
    for copy in l_w12:
        copy.wait()
    stage_back(0)
    for copy in l_ug[1]:
        copy.wait()
    stage_inner(1)
    for copy in l_inner + l_rows + l_hid:
        copy.wait()
    weight_grad(3, gm, [(0, hidden, inner)])
    rs_start(3)
    gg.drain()
    l_mid = [lcopy(i_mid.at[m], gm.at[m]) for m in range(mbs)]
    stage_back(1)
    stage_attn(0)
    for copy in l_mid:
        copy.wait()
    weight_grad(1, gm, [(0, hidden, up)])
    rs_start(1)
    l_x = [lcopy(i_x.at[m], up.at[m]) for m in range(mbs)]
    stage_attn(1)
    weight_grad(2, gm, [(0, hidden, gate)])
    rs_start(2)
    for copy in [l_w0] + l_tab + l_att[0] + l_att[1]:
        copy.wait()
    stage_mixed(0)
    rs_mid(3)
    attend(0)
    stage_in(0)
    rs_mid(1)
    stage_mixed(1)
    weight_grad(4, ga, [(3 * hw, 4 * hw, mixed)])
    rs_start(4)
    attend(1)
    rs_mid(2)

    per = width // 128
    for r in range(5):
        sums = jnp.sum(acc[8 * r : 8 * r + 8, :], axis=0, keepdims=True)
        for j in range(per):
            vsend[per * r + j : per * r + j + 1, :] = sums[:, 128 * j : 128 * j + 128]
    vcopies = []
    for i, peer in enumerate(p.dpeers):
        copy = remote(vsend, vrecv.at[i], vs.at[i], vr.at[i], dp=peer)
        copy.start()
        vcopies.append(copy)
    for copy in l_x:
        copy.wait()
    weight_grad(0, up, [(0, hw, q), (hw, 2 * hw, k), (2 * hw, 3 * hw, v)])
    rs_start(0)
    rs_mid(4)
    stage_in(1)
    stage_out(0)
    rs_mid(0)
    total = vsend[...]
    for i in range(n - 1):
        remote(vrecv.at[i], vrecv.at[i], vs.at[i], vr.at[i], dp=p.xn).wait_recv()
        total = total + vrecv[i]
    tv[p.t] = total
    for i, peer in enumerate(p.tpeers):
        copy = remote(tv.at[p.t], tv.at[p.t], vs.at[n - 1 + i], vr.at[n - 1 + i], tensor=peer)
        copy.start()
        vcopies.append(copy)
    rs_end(3)
    rs_end(1)
    rs_end(2)
    stage_out(1)
    for i, peer in enumerate(p.tpeers):
        src = (p.t + 4 - (i + 1)) % 4
        remote(tv.at[src], tv.at[src], vs.at[n - 1 + i], vr.at[n - 1 + i], tensor=peer).wait_recv()
    ocopy(tv, o_tv)
    rs_end(4)
    rs_end(0)
    for gather in gga:
        gather.drain()
    for copy in gsends + vcopies:
        copy.wait_send()
    for copy in outs:
        copy.wait()


def shards(
    hidden_in, out_grad, doc_ids, w_query, w_key, w_value, w_output, w_up, w_gate, w_down,
    scale_qk, alpha_attn, alpha_mlp, scale_up, scale_gate,
):
    n = lax.axis_size("dp")
    mbs, rows, width = hidden_in.shape
    seq = doc_ids.shape[2]
    hw = w_query.shape[1]
    hidden = w_up.shape[1]
    shard = w_query.shape[0]
    nz = n // 2
    flat = 4 * lax.axis_index("dp") + lax.axis_index("tensor")

    wsh = jnp.stack(
        [
            jnp.concatenate([w_query, w_key, w_value, w_output.T], axis=1),
            w_up,
            w_gate,
            w_down.T,
        ]
    )

    def placed(vals):
        start = (flat * vals.shape[0]) % 128
        return lax.dynamic_update_slice(jnp.zeros((128,), F32), vals, (start,))

    zero = jnp.zeros((128,), F32)
    small = jnp.stack(
        [placed(item) for item in (scale_qk, alpha_attn, alpha_mlp, scale_up, scale_gate)] + [zero] * 3
    )
    docs = doc_ids[:, 0, :]
    places = doc_places(docs)
    steps = jnp.arange(DH // 2, dtype=F32) / (DH // 2)
    freqs = jnp.exp(-math.log(10000.0) * steps)
    turn = places.astype(F32)[..., None] * freqs
    cosine, sine = jnp.cos(turn), jnp.sin(turn)
    code = (docs * CODE + places // BLOCK).astype(F32)
    low = (docs * CODE).astype(F32)
    table = jnp.concatenate(
        [cosine, sine, code[..., None], low[..., None], jnp.zeros(code.shape + (126 - DH,), F32)], axis=-1
    )
    irow = jnp.stack([code, low] + [code] * 6, axis=1)

    any_ = pl.BlockSpec(memory_space=pl.ANY)
    vm = pltpu.VMEM
    dma = pltpu.SemaphoreType.DMA

    def sds(shape, dtype):
        return jax.ShapeDtypeStruct(shape, dtype)

    res_shapes = dict(
        out=((mbs, rows, width), BF16),
        w=((4, width, width), BF16),
        x=((mbs, seq, width), BF16),
        q=((mbs, seq, hw), BF16),
        k=((mbs, seq, hw), BF16),
        v=((mbs, seq, hw), BF16),
        rq=((mbs, seq, hw), BF16),
        rk=((mbs, seq, hw), BF16),
        lrow=((mbs, seq // 16, 128), F32),
        mixed=((mbs, seq, hw), BF16),
        mid=((mbs, seq, width), BF16),
        up=((mbs, seq, hidden), BF16),
        gate=((mbs, seq, hidden), BF16),
        inner=((mbs, seq, hidden), BF16),
        attn=((mbs, rows, width), F32),
        gmd=((mbs, rows, width), F32),
        gm=((mbs, rows, width), BF16),
        gm0=((seq, width), BF16),
        vec=((8, width), F32),
        acc=((40, width), F32),
    )
    r = {key: sds(*val) for key, val in res_shapes.items()}
    s = {key: vm(*val) for key, val in res_shapes.items()}
    tabs = [vm((mbs, seq, 128), F32)]
    infos = [vm((mbs, 8, seq), F32)]
    nvec = 5 * (width // 128)
    own32 = vm((mbs, rows, width), F32)
    scat = [vm((mbs, 3, rows, width), BF16), vm((mbs, 3, rows, width), BF16)]
    heads = hw // DH
    res = pl.pallas_call(
        functools.partial(fwd_kernel, n),
        name="fwd",
        out_shape=tuple(r.values()),
        in_specs=[any_] * 6,
        out_specs=tuple([any_] * len(r)),
        scratch_shapes=[
            s["w"], s["x"], s["q"], s["k"], s["v"], s["rq"], s["rk"],
            vm((mbs, seq, 128), F32),
            s["mixed"], s["mid"], s["up"], s["gate"], s["inner"],
            s["attn"], own32, own32, s["gmd"], s["gm"], s["gm0"], s["vec"], s["acc"],
            vm((4 * n, 8, 128), F32),
            *tabs,
            vm((mbs, rows, width), BF16), vm((mbs, rows, width), BF16),
            *infos,
            vm((heads * QB, hw), BF16),
            *scat,
            dma((4, n)), dma((4, n)), dma((4,)),
            dma((n + 2,)), dma((n + 2,)),
            dma((16,)),
            dma((mbs, 3)), dma((mbs, 3)), dma((mbs, 3)), dma((mbs, 3)), dma((3,)), dma((3,)),
            dma((mbs, 3)), dma((mbs, 3)), dma((mbs, 3)), dma((mbs, 3)),
            dma((40,)),
        ],
        compiler_params=pltpu.CompilerParams(
            collective_id=0, has_side_effects=True, vmem_limit_bytes=VMEM_LIMIT
        ),
    )(wsh, hidden_in, out_grad, small, table, irow)
    r = dict(zip(r, res))

    gshape = sds((shard, hw), F32)
    fshape = sds((shard, hidden), F32)
    grads = pl.pallas_call(
        functools.partial(bwd_kernel, n),
        name="bwd",
        out_shape=(
            sds((mbs, rows, width), BF16), gshape, gshape, gshape, gshape, fshape, fshape, fshape,
            sds((4, nvec, 128), F32),
        ),
        in_specs=[any_] * 22,
        out_specs=tuple([any_] * 9),
        scratch_shapes=[
            s["w"], s["q"], s["k"], s["v"], s["rq"], s["rk"], s["lrow"], s["mixed"],
            s["up"], s["gate"], s["inner"], s["attn"], s["gmd"],
            s["x"], s["x"], s["vec"], s["acc"],
            *tabs, *infos,
            vm((hw, seq), BF16), vm((hw, seq), F32), vm((seq, hw), F32), vm((seq, hw), F32),
            own32,
            vm((4, nz, shard, width), BF16), vm((4, nz - 1, shard, width), BF16),
            vm((nvec, 128), F32), vm((n - 1, nvec, 128), F32), vm((4, nvec, 128), F32),
            *scat,
            dma((48,)), dma((3,)), dma((3,)), dma((mbs, 3)), dma((mbs, 3)),
            dma((mbs, 3)), dma((mbs, 3)), dma((mbs, 3)), dma((mbs, 3)),
            dma((5, nz)), dma((5, nz)), dma((5, nz - 1)), dma((5, nz - 1)),
            dma((n + 2,)), dma((n + 2,)),
            dma((16,)),
        ],
        compiler_params=pltpu.CompilerParams(
            collective_id=1, has_side_effects=True, vmem_limit_bytes=VMEM_LIMIT
        ),
    )(
        hidden_in, table, irow, r["w"], r["x"], r["q"], r["k"], r["v"], r["rq"], r["rk"], r["lrow"],
        r["mixed"], r["mid"], r["up"], r["gate"], r["inner"], r["attn"], r["gmd"], r["gm"], r["gm0"],
        r["vec"], r["acc"],
    )
    g_in, gq, gk, gv, go, gu, gg, gd, tv = grads
    tv = tv.reshape(4, 5, width)
    total = jnp.sum(tv, axis=0)

    def own_part(flat_vals, size):
        return lax.dynamic_slice_in_dim(flat_vals, flat * size, size)

    one = scale_qk.shape[0]
    big = scale_up.shape[0]
    return (
        r["out"], g_in, gq, gk, gv, go.T, gu, gg, gd.T,
        own_part(tv[:, 4, :hw].reshape(-1), one),
        own_part(total[1], one),
        own_part(total[0], one),
        own_part(tv[:, 2, :].reshape(-1), big),
        own_part(tv[:, 3, :].reshape(-1), big),
    )


def solution(mesh):
    rows = P("dp", "tensor", None)
    inward = P("dp", "tensor")
    outward = P("tensor", "dp")
    flat = P(("dp", "tensor"))
    weights = (inward, inward, inward, outward, inward, inward, outward)
    in_specs = (rows, rows, P("dp", None, None)) + weights + (flat,) * 5
    out_specs = (rows, rows) + weights + (flat,) * 5
    return jax.shard_map(shards, mesh=mesh, in_specs=in_specs, out_specs=out_specs, check_vma=False)
```

```python
import functools
import math

import jax
import jax.numpy as jnp
from jax import lax
from jax.experimental import pallas as pl
from jax.experimental.pallas import tpu as pltpu
from jax.sharding import PartitionSpec as P

DH = 64
BLOCK = 256
DOCS = 3
DOC_MAX = 512
F32 = jnp.float32
BF16 = jnp.bfloat16
MESH = pl.DeviceIdType.MESH
VMEM_LIMIT = 67043328
LOG2E = 1.4426950408889634
QB = 128
COLS = 256
CODE = 8


def nn(a, b):
    return jnp.dot(a, b, preferred_element_type=F32)


def nt(a, b):
    return lax.dot_general(a, b, (((1,), (1,)), ((), ())), preferred_element_type=F32)


def tn(a, b):
    return lax.dot_general(a, b, (((0,), (0,)), ((), ())), preferred_element_type=F32)


def split_sum(vals, ones):
    high = vals.astype(BF16)
    low = (vals - high.astype(F32)).astype(BF16)
    return nn(high, ones) + nn(low, ones)


def lane_iota(shape):
    return lax.broadcasted_iota(jnp.int32, shape, len(shape) - 1)


def head_ones():
    rows = lax.broadcasted_iota(jnp.int32, (128, 128), 0) // DH
    cols = lax.broadcasted_iota(jnp.int32, (128, 128), 1) // DH
    return jnp.where(rows == cols, 1.0, 0.0).astype(BF16)


def partner(vals):
    low = lane_iota(vals.shape) % DH < DH // 2
    return jnp.where(low, pltpu.roll(vals, 128 - DH // 2, 1), pltpu.roll(vals, DH // 2, 1))


def turns(table):
    lane = lane_iota(table.shape)
    both = jnp.where(lane < DH, table, pltpu.roll(table, DH, 1))
    low = lane % DH < DH // 2
    cosine = jnp.where(low, both, pltpu.roll(both, DH // 2, 1))
    sine = jnp.where(low, -pltpu.roll(both, 128 - DH // 2, 1), both)
    return cosine, sine


class Place:
    def __init__(self, n):
        self.n = n
        self.t = lax.axis_index("tensor")
        self.d = lax.axis_index("dp")
        t, d = self.t, self.d
        self.sib = t + 1 - 2 * (t % 2)
        self.yp = (t + 2) % 4
        self.diag = (self.sib + 2) % 4
        self.xi = d % 2
        self.z = d // 2
        self.nz = n // 2
        self.xn = d + 1 - 2 * (d % 2)
        self.zpeers = [2 * ((self.z + k) % self.nz) + self.xi for k in range(1, self.nz)]
        self.dpeers = [(d + k) % n for k in range(1, n)]
        self.tpeers = [(t + k) % 4 for k in range(1, 4)]

    def barrier(self):
        sem = pltpu.get_barrier_semaphore()
        for peer in self.dpeers:
            pl.semaphore_signal(sem, inc=1, device_id={"dp": peer}, device_id_type=MESH)
        for peer in self.tpeers:
            pl.semaphore_signal(sem, inc=1, device_id={"tensor": peer}, device_id_type=MESH)
        pl.semaphore_wait(sem, self.n + 2)


def remote(src, dst, ssem, rsem, **where):
    return pltpu.make_async_remote_copy(
        src_ref=src, dst_ref=dst, send_sem=ssem, recv_sem=rsem, device_id=where, device_id_type=MESH
    )


class Gather:
    def __init__(self, place, whole, ssem, rsem, rows):
        self.p, self.whole, self.ssem, self.rsem, self.rows = place, whole, ssem, rsem, rows

    def at(self, index):
        return self.whole.at[pl.ds(pl.multiple_of(index * self.rows, self.rows), self.rows)]

    def start(self, own):
        p = self.p
        self.c_yp = remote(own, self.at(p.t), self.ssem.at[1], self.rsem.at[1], tensor=p.yp)
        self.c_sib = remote(own, self.at(p.t), self.ssem.at[0], self.rsem.at[0], tensor=p.sib)
        self.c_yp.start()
        self.c_sib.start()

    def wait(self, step):
        p = self.p
        if step == 1:
            remote(self.at(p.sib), self.at(p.sib), self.ssem.at[0], self.rsem.at[0], tensor=p.sib).wait_recv()
        if step == 2:
            remote(self.at(p.yp), self.at(p.yp), self.ssem.at[1], self.rsem.at[1], tensor=p.yp).wait_recv()
            self.forward().start()
        if step == 3:
            remote(self.at(p.diag), self.at(p.diag), self.ssem.at[2], self.rsem.at[2], tensor=p.sib).wait_recv()

    def forward(self):
        p = self.p
        return remote(self.at(p.yp), self.at(p.yp), self.ssem.at[2], self.rsem.at[2], tensor=p.sib)

    def drain(self):
        self.c_yp.wait_send()
        self.c_sib.wait_send()
        self.forward().wait_send()

    def each(self, work):
        blocks(self.p, work, self.wait)


def blocks(p, work, wait=None):
    def body(i, carry):
        for step in range(1, 4):
            if wait is not None:
                pl.when(i == step)(functools.partial(wait, step))
        work((p.t // 2 + i // 2) % 2 * 2 + (p.t + i) % 2)
        return carry

    lax.fori_loop(0, 4, body, 0)


class Scatter:
    def __init__(self, place, sbuf, rbuf, ssem, rsem):
        self.p, self.sbuf, self.rbuf, self.ssem, self.rsem = place, sbuf, rbuf, ssem, rsem
        self.copies = []

    def send(self, slot, **where):
        copy = remote(
            self.sbuf.at[slot], self.rbuf.at[slot], self.ssem.at[slot], self.rsem.at[slot], **where
        )
        copy.start()
        self.copies.append(copy)

    def arrive(self, slot):
        remote(
            self.rbuf.at[slot], self.rbuf.at[slot], self.ssem.at[slot], self.rsem.at[slot],
            tensor=self.p.sib,
        ).wait_recv()

    def run(self, part, own):
        p = self.p
        width = own.shape[1]

        def fill(index, put):
            def body(c, carry):
                lanes = pl.ds(pl.multiple_of(c * COLS, COLS), COLS)
                put(lanes, part(index, lanes))
                return carry

            lax.fori_loop(0, width // COLS, body, 0)

        def first(slot):
            def put(lanes, vals):
                self.sbuf[slot, :, lanes] = vals.astype(BF16)

            return put

        def across(lanes, vals):
            self.sbuf[2, :, lanes] = (vals + self.rbuf[0, :, lanes].astype(F32)).astype(BF16)

        def mine(lanes, vals):
            own[:, lanes] = vals

        fill(p.diag, first(0))
        self.send(0, tensor=p.sib)
        fill(p.sib, first(1))
        self.send(1, tensor=p.sib)
        self.arrive(0)
        fill(p.yp, across)
        self.send(2, tensor=p.yp)
        fill(p.t, mine)

    def finish(self):
        self.arrive(1)
        self.arrive(2)
        for copy in self.copies:
            copy.wait_send()


def rows_of(ref, index, rows):
    return ref[pl.ds(pl.multiple_of(index * rows, rows), rows)]


def mean_sq(vals):
    return jnp.mean(vals * vals, axis=-1, keepdims=True)


def fold8(vals):
    total = vals[0:8]
    for k in range(1, vals.shape[0] // 8):
        total = total + vals[8 * k : 8 * k + 8]
    return total


def fwd_kernel(
    n,
    wq, wk, wv, wo, wu, wg, wd, hid, og, small, docs,
    o_out, o_w, o_x, o_q, o_k, o_v, o_rq, o_rk, o_lrow, o_mixed, o_mid, o_up, o_gate, o_inner,
    o_attn, o_gmd, o_gm, o_gm0, o_vec, o_acc, o_tab, o_ir,
    w, x, q, k, v, rq, rk, lcol, mixed, mid, up, gate, inner,
    attn, midf, mlp, gmd, gm, gm0, vec, acc, tab, ir, sall, docv, ogv, outv, qm, sbuf, rbuf,
    wsend, wrecv, small_s, small_r, lsem, agx_s, agx_r, agm_s, agm_r, agg_s, agg_r,
    rsa_s, rsa_r, rsm_s, rsm_r, osem,
):
    p = Place(n)
    nz = p.nz
    mbs, rows, width = hid.shape
    seq = x.shape[1]
    hw = q.shape[2]
    shard = wq.shape[0]
    heads = hw // DH
    groups = w.shape[0]
    hidden = up.shape[2]

    def wat(g, index):
        return w.at[g, pl.ds(pl.multiple_of(index * shard, shard), shard)]

    local = []

    def lcopy(src, dst):
        copy = pltpu.make_async_copy(src, dst, lsem.at[len(local)])
        copy.start()
        local.append(copy)
        return copy

    outs = []

    def ocopy(src, dst):
        copy = pltpu.make_async_copy(src, dst, osem.at[len(outs)])
        copy.start()
        outs.append(copy)

    own_w = pl.ds(pl.multiple_of(p.d * shard, shard), shard)
    w_in = [lcopy(src, w.at[0, own_w, pl.ds(i * hw, hw)]) for i, src in enumerate((wq, wk, wv, wo))]
    w_in += [lcopy(src, w.at[i + 1, own_w]) for i, src in enumerate((wu, wg, wd))]
    docs_in = lcopy(docs, docv)
    p.barrier()

    gx = [Gather(p, x.at[m], agx_s.at[m], agx_r.at[m], rows) for m in range(mbs)]
    gmi = [Gather(p, mid.at[m], agm_s.at[m], agm_r.at[m], rows) for m in range(mbs)]
    slot = p.t * n + p.d
    small_own = lcopy(small, sall.at[slot])
    small_d = [
        remote(small, sall.at[slot], small_s.at[i], small_r.at[i], dp=peer)
        for i, peer in enumerate(p.dpeers)
    ]
    for copy in small_d:
        copy.start()
    gx[0].start(hid.at[0])
    sends = []

    def wsend_to(g, i, src, index, peer):
        copy = remote(src, wat(g, index), wsend.at[g, i], wrecv.at[g, index], dp=peer)
        copy.start()
        sends.append(copy)

    def relay(g):
        for i, peer in reversed(list(enumerate(p.zpeers))):
            remote(wat(g, peer), wat(g, peer), wsend.at[g, 0], wrecv.at[g, peer], dp=p.xn).wait_recv()
            wsend_to(g, nz + i, wat(g, peer), peer, p.xn)

    for copy in w_in:
        copy.wait()
    for g in range(groups):
        for i, peer in enumerate(p.zpeers):
            wsend_to(g, i, wat(g, p.d), p.d, peer)
        if g == 0:
            wsend_to(0, nz - 1, wat(0, p.d), p.d, p.xn)
    xown = [lcopy(hid.at[m], gx[m].at(p.t)) for m in range(mbs)]
    og_in = lcopy(og, ogv)
    for i, peer in enumerate(p.dpeers):
        src = p.t * n + (p.d + n - (i + 1)) % n
        remote(sall.at[src], sall.at[src], small_s.at[i], small_r.at[i], dp=peer).wait_recv()
    small_own.wait()
    small_t = []
    for i, peer in enumerate(p.tpeers):
        part = sall.at[pl.ds(p.t * n, n)]
        copy = remote(part, part, small_s.at[n - 1 + i], small_r.at[n - 1 + i], tensor=peer)
        copy.start()
        small_t.append(copy)
    gx[1].start(hid.at[1])

    def wready(g):
        remote(wat(g, p.xn), wat(g, p.xn), wsend.at[g, 0], wrecv.at[g, p.xn], dp=p.xn).wait_recv()
        for peer in p.zpeers:
            other = peer + 1 - 2 * p.xi
            remote(wat(g, other), wat(g, other), wsend.at[g, 0], wrecv.at[g, other], dp=p.xn).wait_recv()
        ocopy(w.at[g], o_w.at[g])

    docs_in.wait()
    for m in range(mbs):
        doc = docv[m]
        count = [jnp.sum(jnp.where(doc == i, 1.0, 0.0), axis=1, keepdims=True) for i in range(DOCS - 1)]
        first = jnp.zeros(doc.shape, F32)
        for i in range(DOCS - 1):
            first = first + jnp.where(doc > i, count[i], 0.0)
        place = lane_iota(doc.shape).astype(F32) - first
        low = doc.astype(F32) * CODE
        code = low + jnp.floor(place * (1.0 / BLOCK))
        line = lax.broadcasted_iota(jnp.int32, (8, seq), 0)
        ir[m] = jnp.where(line == 0, code, jnp.where(line == 1, low, place))
        line = lax.broadcasted_iota(jnp.int32, (128, seq), 0)
        every_row = jnp.where(line == DH, code, jnp.where(line == DH + 1, low, place))
        tab[m] = jnp.transpose(every_row, (1, 0))

    def turn_rows(i, carry):
        at = pl.ds(pl.multiple_of(i % (seq // 64) * 64, 64), 64)
        m = i // (seq // 64)
        lane = lane_iota((1, 128))
        freq = jnp.exp((lane % (DH // 2)).astype(F32) * (-math.log(10000.0) / (DH // 2)))
        shift = jnp.where(lane < DH // 2, 0.5 * math.pi, 0.0)
        old = tab[m, at, :]
        tab[m, at, :] = jnp.where(lane < DH, jnp.sin(old[:, 0:1] * freq + shift), old)
        return carry

    lax.fori_loop(0, mbs * (seq // 64), turn_rows, 0)
    acc[...] = jnp.zeros_like(acc)

    relay(0)
    for g in range(1, groups):
        wsend_to(g, nz - 1, wat(g, p.d), p.d, p.xn)
    for i, peer in enumerate(p.tpeers):
        part = sall.at[pl.ds((p.t + 4 - (i + 1)) % 4 * n, n)]
        remote(part, part, small_s.at[n - 1 + i], small_r.at[n - 1 + i], tensor=peer).wait_recv()
    every = 4 * n

    def gathered(row, base, count, lanes):
        per = count // (lanes // 128)

        def item(k):
            part = sall[k % 4 * n + base + k // 4, row : row + 1, :]
            turn = k % per * (128 // per)
            return pltpu.roll(part, turn, 1) if turn else part

        for r in range(lanes // 128):
            total = item(r * per)
            for j in range(1, per):
                total = total + item(r * per + j)
            vec[row : row + 1, 128 * r : 128 * r + 128] = total

    gathered(0, p.t * (n // 4), n, hw)
    gathered(1, 0, every, width)
    gathered(2, 0, every, width)
    gathered(3, p.t * (n // 4), n, hidden)
    gathered(4, p.t * (n // 4), n, hidden)
    wready(0)

    ones = head_ones()

    def stage_qkv(m):
        xown[m].wait()

        def work(index):
            at = pl.ds(pl.multiple_of(index * rows, rows), rows)
            xb = x[m, at, :]
            cb, sb = turns(tab[m, at, :])
            for which, (dst, rdst) in enumerate(((q, rq), (k, rk))):
                raw = nn(xb, w[0, :, which * hw : (which + 1) * hw])
                for half in range(hw // 128):
                    lanes = slice(128 * half, 128 * half + 128)
                    piece = raw[:, lanes]
                    turned = piece * cb + partner(piece) * sb
                    scale = lax.rsqrt(split_sum(turned * turned, ones) + 1e-06)
                    rdst[m, at, lanes] = scale.astype(BF16)
                    dst[m, at, lanes] = (turned * scale * vec[0:1, lanes]).astype(BF16)
            v[m, at, :] = nn(xb, w[0, :, 2 * hw : 3 * hw]).astype(BF16)

        gx[m].each(work)

    win = seq - 128
    c_exp = math.sqrt(DH) * LOG2E

    def attend(m):
        def body(b, carry):
            at = pl.ds(pl.multiple_of(b * QB, QB), QB)
            keys = pl.ds(pl.multiple_of(((b + 3) // 8) * 128, 128), win)
            ccol = tab[m, at, DH : DH + 1]
            lcol_ = tab[m, at, DH + 1 : DH + 2]
            crow = ir[m, 0:1, keys]
            bias = jnp.where((crow <= ccol) & (crow >= lcol_), 0.0, -1e30)
            qb = q[m, at, :]
            lane = lane_iota((QB, hw)) // DH
            for h in range(heads):
                qm[h * QB : (h + 1) * QB, :] = jnp.where(lane == h, qb, jnp.zeros_like(qb))
            kb = k[m, keys, :]
            vb = v[m, keys, :]
            total = jnp.zeros((QB, hw), F32)
            lsum = jnp.zeros((QB, 128), F32)
            lane_l = lane_iota((QB, 128))
            for h in range(heads):
                scores = nt(qm[h * QB : (h + 1) * QB, :], kb)
                expo = jnp.exp2(scores * c_exp + bias)
                inv = 1.0 / jnp.sum(expo, axis=-1, keepdims=True)
                part = nn(expo.astype(BF16), vb)
                total = jnp.where(lane == h, part * inv, total)
                lsum = jnp.where(lane_l == h, inv, lsum)
            mixed[m, at, :] = total.astype(BF16)
            lcol[m, at, :] = lsum
            return carry

        lax.fori_loop(0, seq // QB, body, 0)

    sc_a = [Scatter(p, sbuf.at[m], rbuf.at[m], rsa_s.at[m], rsa_r.at[m]) for m in range(mbs)]
    sc_m = [Scatter(p, sbuf.at[m], rbuf.at[m], rsm_s.at[m], rsm_r.at[m]) for m in range(mbs)]

    def stage_o(m):
        sc_a[m].run(
            lambda index, cols: nt(rows_of(mixed.at[m], index, rows), w[0, cols, 3 * hw : 3 * hw + hw]),
            attn.at[m],
        )

    chunk = 32

    def stage_mid(m):
        sc_a[m].finish()
        base = p.t * rows

        def body(i, carry):
            at = pl.ds(pl.multiple_of(i * chunk, chunk), chunk)
            own = pl.ds(pl.multiple_of(base + i * chunk, chunk), chunk)
            a = attn[m, at, :] + rbuf[m, 1, at, :].astype(F32) + rbuf[m, 2, at, :].astype(F32)
            attn[m, at, :] = a
            h = x[m, own, :].astype(F32)
            na = a * lax.rsqrt(mean_sq(a) + 1e-06)
            zz = h + vec[1:2, :] * (na - h)
            out = zz * lax.rsqrt(mean_sq(zz) + 1e-06)
            midf[m, at, :] = out
            mid[m, own, :] = out.astype(BF16)
            return carry

        lax.fori_loop(0, rows // chunk, body, 0)
        gmi[m].start(gmi[m].at(p.t))

    cols = 256

    def stage_up(m):
        def work(index):
            at = pl.ds(pl.multiple_of(index * rows, rows), rows)

            def body(c, carry):
                lanes = pl.ds(pl.multiple_of(c * cols, cols), cols)
                mb = mid[m, at, :]
                u = nn(mb, w[1, :, lanes])
                g = nn(mb, w[2, :, lanes])
                up[m, at, lanes] = u.astype(BF16)
                gate[m, at, lanes] = g.astype(BF16)
                gs = g * vec[4:5, lanes]
                inner[m, at, lanes] = ((u * vec[3:4, lanes]) * (gs / (1.0 + jnp.exp(-gs)))).astype(BF16)
                return carry

            lax.fori_loop(0, hidden // cols, body, 0)

        gmi[m].each(work)

    def stage_down(m):
        sc_m[m].run(lambda index, cols: nt(rows_of(inner.at[m], index, rows), w[3, cols, :]), mlp.at[m])

    gg = Gather(p, gm0, agg_s, agg_r, rows)

    def stage_end(m):
        sc_m[m].finish()

        def body(i, carry):
            at = pl.ds(pl.multiple_of(i * chunk, chunk), chunk)
            a = mlp[m, at, :] + rbuf[m, 1, at, :].astype(F32) + rbuf[m, 2, at, :].astype(F32)
            h = midf[m, at, :]
            ra = lax.rsqrt(mean_sq(a) + 1e-06)
            na = a * ra
            al = vec[2:3, :]
            zz = h + al * (na - h)
            rz = lax.rsqrt(mean_sq(zz) + 1e-06)
            out = zz * rz
            outv[m, at, :] = out.astype(BF16)
            cot = ogv[m, at, :].astype(F32)
            dz = rz * (cot - out * jnp.mean(cot * out, axis=-1, keepdims=True))
            dn = al * dz
            acc[0:8, :] += fold8(dz * (na - h))
            gmd[m, at, :] = dz - dn
            grad = (ra * (dn - na * jnp.mean(dn * na, axis=-1, keepdims=True))).astype(BF16)
            gm[m, at, :] = grad
            if m == 0:
                gm0[pl.ds(pl.multiple_of(p.t * rows + i * chunk, chunk), chunk), :] = grad
            return carry

        lax.fori_loop(0, rows // chunk, body, 0)
        if m == 0:
            gg.start(gg.at(p.t))

    stage_qkv(0)
    attend(0)
    relay(1)
    stage_o(0)
    stage_qkv(1)
    attend(1)
    stage_mid(0)
    stage_o(1)
    relay(2)
    for m in range(mbs):
        ocopy(x.at[m], o_x.at[m])
        ocopy(q.at[m], o_q.at[m])
        ocopy(k.at[m], o_k.at[m])
        ocopy(v.at[m], o_v.at[m])
        ocopy(rq.at[m], o_rq.at[m])
        ocopy(rk.at[m], o_rk.at[m])
        ocopy(mixed.at[m], o_mixed.at[m])
    ocopy(vec, o_vec)
    ocopy(tab, o_tab)
    ocopy(ir, o_ir)
    relay(3)
    wready(1)
    wready(2)
    stage_up(0)
    stage_mid(1)
    wready(3)
    stage_down(0)
    stage_up(1)
    stage_down(1)
    og_in.wait()
    stage_end(0)
    ocopy(mid.at[0], o_mid.at[0])
    ocopy(up.at[0], o_up.at[0])
    ocopy(gate.at[0], o_gate.at[0])
    ocopy(inner.at[0], o_inner.at[0])
    for m in range(mbs):
        lrow = jnp.transpose(lcol[m], (1, 0))
        lcol[m, 0:8, 0:128] = lrow[0:8, 0:128]
        for j in range(1, seq // 128):
            lcol[m, 8 * j : 8 * j + 8, 0:128] = lrow[0:8, 128 * j : 128 * j + 128]
        ocopy(lcol.at[m, pl.ds(0, seq // 16)], o_lrow.at[m])
    ocopy(mid.at[1], o_mid.at[1])
    ocopy(up.at[1], o_up.at[1])
    ocopy(gate.at[1], o_gate.at[1])
    ocopy(inner.at[1], o_inner.at[1])
    ocopy(attn, o_attn)
    for step in range(1, 3):
        gg.wait(step)
    stage_end(1)
    ocopy(outv, o_out)
    ocopy(gmd, o_gmd)
    ocopy(gm, o_gm)
    ocopy(acc, o_acc)
    gg.wait(3)
    ocopy(gm0, o_gm0)
    for gather in gx + gmi + [gg]:
        gather.drain()
    for copy in sends + small_t + small_d:
        copy.wait_send()
    for copy in outs:
        copy.wait()


def bwd_kernel(
    n,
    hid, i_w, i_x, i_q, i_k, i_v, i_rq, i_rk, i_lrow, i_mixed, i_mid, i_up, i_gate,
    i_inner, i_attn, i_gmd, i_gm, i_gm0, i_vec, i_acc, i_tab, i_ir,
    o_in, o_gq, o_gk, o_gv, o_go, o_gu, o_gg, o_gd, o_tv,
    w, q, k, v, rq, rk, lrow, mixed, up, gate, inner, attn, gmd, gm, ga, vec, acc,
    tab, ir, kt, dqt, dk, dv, outv, xrecv, zrecv, vsend, vrecv, tv, sbuf, rbuf,
    lsem, agg_s, agg_r, aga_s, aga_r, rsm_s, rsm_r, rsi_s, rsi_r, xs, xr, zs, zr, vs, vr, osem,
):
    p = Place(n)
    nz = p.nz
    mbs, rows, width = hid.shape
    seq = q.shape[1]
    hw = q.shape[2]
    heads = hw // DH
    hidden = up.shape[2]
    groups = w.shape[0]
    shard = width // n
    gmix = [inner.at[m, :, pl.ds(0, hw)] for m in range(mbs)]
    pts, dss = (inner.at[m, pl.ds(0, seq - 128), pl.ds(hw, heads * QB)] for m in range(2))
    qs, gs = (
        inner.at[0, pl.ds(i * heads * QB, heads * QB), pl.ds(hw + heads * QB, hw)] for i in range(2)
    )

    local = []

    def lcopy(src, dst):
        copy = pltpu.make_async_copy(src, dst, lsem.at[len(local)])
        copy.start()
        local.append(copy)
        return copy

    outs = []

    def ocopy(src, dst):
        copy = pltpu.make_async_copy(src, dst, osem.at[len(outs)])
        copy.start()
        outs.append(copy)

    l_gm0 = lcopy(i_gm0, gm.at[0])
    l_w3 = lcopy(i_w.at[3], w.at[3])
    l_ug = [[lcopy(i_up.at[m], up.at[m]), lcopy(i_gate.at[m], gate.at[m])] for m in range(mbs)]
    l_vec = [lcopy(i_vec, vec), lcopy(i_acc, acc)]
    p.barrier()
    gg = Gather(p, gm.at[1], agg_s, agg_r, rows)
    gg.start(i_gm.at[1])
    l_gm1 = lcopy(i_gm.at[1], gg.at(p.t))
    l_w12 = [lcopy(i_w.at[1], w.at[1]), lcopy(i_w.at[2], w.at[2])]
    l_inner = [lcopy(i_inner.at[m], inner.at[m]) for m in range(mbs)]
    l_rows = [lcopy(i_attn, attn), lcopy(i_gmd, gmd)]
    l_w0 = lcopy(i_w.at[0], w.at[0])
    l_att = [
        [
            lcopy(src.at[m], dst.at[m])
            for src, dst in ((i_q, q), (i_k, k), (i_v, v), (i_rq, rq), (i_rk, rk), (i_lrow, lrow), (i_mixed, mixed))
        ]
        for m in range(mbs)
    ]
    l_tab = [lcopy(i_tab, tab), lcopy(i_ir, ir)]

    gga = [Gather(p, ga.at[m], aga_s.at[m], aga_r.at[m], rows) for m in range(mbs)]
    l_hid = [lcopy(hid.at[m], gga[m].at(p.t)) for m in range(mbs)]
    sc_m = [Scatter(p, sbuf.at[m], rbuf.at[m], rsm_s.at[m], rsm_r.at[m]) for m in range(mbs)]
    sc_i = [Scatter(p, sbuf.at[m], rbuf.at[m], rsi_s.at[m], rsi_r.at[m]) for m in range(mbs)]
    cols = 256
    chunk = 32

    def stage_inner(m):
        if m == 1:
            l_gm1.wait()

        def work(index):
            at = pl.ds(pl.multiple_of(index * rows, rows), rows)

            def body(c, carry):
                lanes = pl.ds(pl.multiple_of(c * cols, cols), cols)
                gi = nn(gm[m, at, :], w[3, :, lanes])
                u = up[m, at, lanes].astype(F32)
                g = gate[m, at, lanes].astype(F32)
                su = vec[3:4, lanes]
                sg = vec[4:5, lanes]
                gsc = g * sg
                sig = 1.0 / (1.0 + jnp.exp(-gsc))
                gu = gi * (gsc * sig)
                ggs = gi * (u * su) * sig * (1.0 + gsc * (1.0 - sig))
                acc[16:24, lanes] += fold8(gu * u)
                acc[24:32, lanes] += fold8(ggs * g)
                up[m, at, lanes] = (gu * su).astype(BF16)
                gate[m, at, lanes] = (ggs * sg).astype(BF16)
                return carry

            lax.fori_loop(0, hidden // cols, body, 0)

        blocks(p, work, gg.wait if m == 1 else None)

    def stage_back(m):
        sc_m[m].run(
            lambda index, cols: nt(rows_of(up.at[m], index, rows), w[1, cols, :])
            + nt(rows_of(gate.at[m], index, rows), w[2, cols, :]),
            outv.at[m],
        )

    def stage_attn(m):
        sc_m[m].finish()
        base = p.t * rows

        def body(i, carry):
            at = pl.ds(pl.multiple_of(i * chunk, chunk), chunk)
            own = pl.ds(pl.multiple_of(base + i * chunk, chunk), chunk)
            part = outv[m, at, :] + rbuf[m, 1, at, :].astype(F32)
            cot = gmd[m, at, :] + part + rbuf[m, 2, at, :].astype(F32)
            a = attn[m, at, :]
            h = ga[m, own, :].astype(F32)
            ra = lax.rsqrt(mean_sq(a) + 1e-06)
            na = a * ra
            al = vec[1:2, :]
            zz = h + al * (na - h)
            rz = lax.rsqrt(mean_sq(zz) + 1e-06)
            out = zz * rz
            dz = rz * (cot - out * jnp.mean(cot * out, axis=-1, keepdims=True))
            dn = al * dz
            acc[8:16, :] += fold8(dz * (na - h))
            gmd[m, at, :] = dz - dn
            ga[m, own, :] = (ra * (dn - na * jnp.mean(dn * na, axis=-1, keepdims=True))).astype(BF16)
            return carry

        lax.fori_loop(0, rows // chunk, body, 0)
        gga[m].start(gga[m].at(p.t))

    def stage_mixed(m):
        def work(index):
            at = pl.ds(pl.multiple_of(index * rows, rows), rows)
            gmix[m][at, :] = nn(ga[m, at, :], w[0, :, 3 * hw : 4 * hw]).astype(BF16)

        gga[m].each(work)

    win = seq - 128
    c_exp = math.sqrt(DH) * LOG2E
    ones = head_ones()

    def attend(m):
        kt[...] = jnp.transpose(k[m], (1, 0))
        dk[...] = jnp.zeros_like(dk)
        dv[...] = jnp.zeros_like(dv)

        def body(b, carry):
            at = pl.ds(pl.multiple_of(b * QB, QB), QB)
            keys = pl.ds(pl.multiple_of(((b + 3) // 8) * 128, 128), win)
            crow = ir[m, 0:1, at]
            lrow_ = ir[m, 1:2, at]
            ccol = tab[m, keys, DH : DH + 1]
            bias = jnp.where((ccol <= crow) & (ccol >= lrow_), 0.0, -1e30)
            qb = q[m, at, :]
            gb = gmix[m][at, :]
            lane = lane_iota((QB, hw)) // DH
            for h in range(heads):
                qs[h * QB : (h + 1) * QB, :] = jnp.where(lane == h, qb, jnp.zeros_like(qb))
                gs[h * QB : (h + 1) * QB, :] = jnp.where(lane == h, gb, jnp.zeros_like(gb))
            kb = k[m, keys, :]
            vb = v[m, keys, :]
            for h in range(heads):
                hl = slice(h * QB, (h + 1) * QB)
                scores = nt(kb, qs[hl, :])
                inv = lrow[m, pl.ds(pl.multiple_of(b * 8, 8), 8), :][h : h + 1, :]
                pt = jnp.exp2(scores * c_exp + bias) * inv
                dpt = nt(vb, gs[hl, :])
                delta = jnp.sum(pt * dpt, axis=0, keepdims=True)
                dst = (pt * (dpt - delta)).astype(BF16)
                pts[:, hl] = pt.astype(BF16)
                dss[:, hl] = dst
                dqt[h * DH : (h + 1) * DH, at] = nn(kt[h * DH : (h + 1) * DH, keys], dst)
            dv[keys, :] += nn(pts[...], gs[...])
            dk[keys, :] += nn(dss[...], qs[...])
            return carry

        lax.fori_loop(0, seq // QB, body, 0)

        step = 256

        def after(i, carry):
            at = pl.ds(pl.multiple_of(i * step, step), step)
            cb, sb = turns(tab[m, at, :])
            v[m, at, :] = dv[at, :].astype(BF16)
            for which in range(2):
                src = (q, k)[which]
                rsc = (rq, rk)[which]
                for half in range(hw // 128):
                    lanes = slice(128 * half, 128 * half + 128)
                    if which == 0:
                        grad = jnp.transpose(dqt[lanes, at], (1, 0)) * math.sqrt(DH)
                    else:
                        grad = dk[at, lanes] * math.sqrt(DH)
                    gain = vec[0:1, lanes]
                    unit = src[m, at, lanes].astype(F32) / gain
                    acc[32:40, lanes] += fold8(grad * unit)
                    dn = grad * gain
                    dy = rsc[m, at, lanes].astype(F32) * (dn - unit * split_sum(dn * unit, ones))
                    src[m, at, lanes] = (dy * cb - partner(dy) * sb).astype(BF16)
            return carry

        lax.fori_loop(0, seq // step, after, 0)

    def stage_in(m):
        def part(index, cols):
            at = pl.ds(pl.multiple_of(index * rows, rows), rows)
            return (
                nt(q[m, at, :], w[0, cols, 0:hw])
                + nt(k[m, at, :], w[0, cols, hw : 2 * hw])
                + nt(v[m, at, :], w[0, cols, 2 * hw : 3 * hw])
            )

        sc_i[m].run(part, outv.at[m])

    def stage_out(m):
        sc_i[m].finish()

        def body(i, carry):
            at = pl.ds(pl.multiple_of(i * chunk, chunk), chunk)
            part = outv[m, at, :] + rbuf[m, 1, at, :].astype(F32)
            total = gmd[m, at, :] + part + rbuf[m, 2, at, :].astype(F32)
            sbuf[m, 0, at, :] = total.astype(BF16)
            return carry

        lax.fori_loop(0, rows // chunk, body, 0)
        ocopy(sbuf.at[m, 0], o_in.at[m])

    pieces = {
        3: (w.at[3], 3, 0, width),
        1: (w.at[1], 1, 0, width),
        2: (w.at[2], 2, 0, width),
        0: (gm.at[0], 0, 0, 3 * hw),
        4: (gm.at[0], 0, 3 * hw, 4 * hw),
    }

    def weight_grad(key, left, rights):
        into = pieces[key][0]

        def body(c, carry):
            lanes = pl.ds(pl.multiple_of(c * cols, cols), cols)
            for lo, hi, right in rights:
                total = tn(left[0, :, lanes], right[0])
                for m in range(1, mbs):
                    total = total + tn(left[m, :, lanes], right[m])
                into[lanes, lo:hi] = total.astype(BF16)
            return carry

        lax.fori_loop(0, width // cols, body, 0)

    def wrow(key, index):
        ref, _, lo, hi = pieces[key]
        return ref.at[pl.ds(pl.multiple_of(index * shard, shard), shard), pl.ds(lo, hi - lo)]

    def held(buf, key, index):
        _, g, lo, hi = pieces[key]
        return buf.at[g, index, :, pl.ds(lo, hi - lo)]

    gsends = []

    def rs_start(key):
        for kk in list(range(1, nz)) + [0]:
            zz = (p.z + kk) % nz
            other = 2 * zz + 1 - p.xi
            copy = remote(wrow(key, other), held(xrecv, key, zz), xs.at[key, kk], xr.at[key, zz], dp=p.xn)
            copy.start()
            gsends.append(copy)

    def rs_arrive(key, kk):
        zz = (p.z + kk) % nz
        got = held(xrecv, key, zz)
        remote(got, got, xs.at[key, kk], xr.at[key, zz], dp=p.xn).wait_recv()
        return got, zz

    def rs_mid(key):
        for kk in range(1, nz):
            got, zz = rs_arrive(key, kk)
            mine = 2 * zz + p.xi
            got[...] = (got[...].astype(F32) + wrow(key, mine)[...].astype(F32)).astype(BF16)
            copy = remote(got, held(zrecv, key, kk - 1), zs.at[key, kk - 1], zr.at[key, kk - 1], dp=mine)
            copy.start()
            gsends.append(copy)

    def rs_end(key):
        _, g, lo, hi = pieces[key]
        got, _ = rs_arrive(key, 0)
        total = got[...].astype(F32) + wrow(key, p.d)[...].astype(F32)
        for kk in range(1, nz):
            got = held(zrecv, key, kk - 1)
            remote(got, got, zs.at[key, kk - 1], zr.at[key, kk - 1], dp=p.xn).wait_recv()
            total = total + got[...].astype(F32)
        fin = attn.at[g // 2, pl.ds((g % 2) * shard, shard)]
        fin[:, lo:hi] = total
        if g == 0:
            for i, dst in enumerate((o_gq, o_gk, o_gv, o_go)):
                if lo <= i * hw < hi:
                    ocopy(fin.at[:, pl.ds(i * hw, hw)], dst)
        else:
            ocopy(fin, (o_gu, o_gg, o_gd)[g - 1])

    for copy in l_vec + [l_gm0, l_w3] + l_ug[0]:
        copy.wait()
    stage_inner(0)
    for copy in l_w12:
        copy.wait()
    stage_back(0)
    for copy in l_ug[1]:
        copy.wait()
    stage_inner(1)
    for copy in l_inner + l_rows + l_hid:
        copy.wait()
    weight_grad(3, gm, [(0, hidden, inner)])
    rs_start(3)
    gg.drain()
    l_mid = [lcopy(i_mid.at[m], gm.at[m]) for m in range(mbs)]
    stage_attn(0)
    stage_back(1)
    for copy in l_mid:
        copy.wait()
    weight_grad(1, gm, [(0, hidden, up)])
    rs_start(1)
    l_x = [lcopy(i_x.at[m], up.at[m]) for m in range(mbs)]
    for copy in [l_w0] + l_tab + l_att[0] + l_att[1]:
        copy.wait()
    stage_mixed(0)
    rs_mid(3)
    attend(0)
    stage_attn(1)
    stage_in(0)
    weight_grad(2, gm, [(0, hidden, gate)])
    rs_start(2)
    rs_mid(1)
    stage_mixed(1)
    weight_grad(4, ga, [(3 * hw, 4 * hw, mixed)])
    rs_start(4)
    attend(1)
    rs_mid(2)

    per = width // 128
    for r in range(5):
        sums = jnp.sum(acc[8 * r : 8 * r + 8, :], axis=0, keepdims=True)
        for j in range(per):
            vsend[per * r + j : per * r + j + 1, :] = sums[:, 128 * j : 128 * j + 128]
    vcopies = []
    for i, peer in enumerate(p.dpeers):
        copy = remote(vsend, vrecv.at[i], vs.at[i], vr.at[i], dp=peer)
        copy.start()
        vcopies.append(copy)
    for copy in l_x:
        copy.wait()
    weight_grad(0, up, [(0, hw, q), (hw, 2 * hw, k), (2 * hw, 3 * hw, v)])
    rs_start(0)
    rs_mid(4)
    stage_in(1)
    stage_out(0)
    rs_mid(0)
    total = vsend[...]
    for i in range(n - 1):
        remote(vrecv.at[i], vrecv.at[i], vs.at[i], vr.at[i], dp=p.xn).wait_recv()
        total = total + vrecv[i]
    tv[p.t] = total
    for i, peer in enumerate(p.tpeers):
        copy = remote(tv.at[p.t], tv.at[p.t], vs.at[n - 1 + i], vr.at[n - 1 + i], tensor=peer)
        copy.start()
        vcopies.append(copy)
    rs_end(3)
    rs_end(1)
    rs_end(2)
    stage_out(1)
    for i, peer in enumerate(p.tpeers):
        src = (p.t + 4 - (i + 1)) % 4
        remote(tv.at[src], tv.at[src], vs.at[n - 1 + i], vr.at[n - 1 + i], tensor=peer).wait_recv()
    ocopy(tv, o_tv)
    rs_end(4)
    rs_end(0)
    for gather in gga:
        gather.drain()
    for copy in gsends + vcopies:
        copy.wait_send()
    for copy in outs:
        copy.wait()


def out_kernel(turned, hw, i_tv, *refs):
    count = (len(refs) - 8 - turned) // 3
    ins, outs, vecs = refs[:count], refs[count : 2 * count], refs[2 * count : 2 * count + 5]
    tv, isem, osem = refs[2 * count + 5], refs[-2], refs[-1]
    bufs = refs[2 * count + 6 : -2]
    tv_in = pltpu.make_async_copy(i_tv, tv, isem.at[count])
    tv_in.start()
    loads = [pltpu.make_async_copy(ins[i], bufs[i], isem.at[i]) for i in range(count)]
    for copy in loads:
        copy.start()
    stores = []
    for i, copy in enumerate(loads):
        copy.wait()
        buf = bufs[i]
        if i >= count - turned:
            buf = bufs[turned + i]
            buf[...] = jnp.transpose(bufs[i][...], (1, 0))
        stores.append(pltpu.make_async_copy(buf, outs[i], osem.at[i]))
        stores[-1].start()
    tv_in.wait()
    flat = 4 * lax.axis_index("dp") + lax.axis_index("tensor")
    per = tv.shape[1] // 5
    for ref, row, whole in zip(vecs, (4, 1, 0, 2, 3), (hw, 0, 0, per * 128, per * 128)):
        size = ref.shape[1]
        start = flat * size
        if whole:
            line = per * row + start % whole // 128
            part = tv[start // whole, pl.ds(line, 1), :]
        else:
            line = per * row + start // 128
            part = tv[0, pl.ds(line, 1), :]
            for a in range(1, tv.shape[0]):
                part = part + tv[a, pl.ds(line, 1), :]
        part = pltpu.roll(jnp.broadcast_to(part, (8, 128)), (128 - start % 128) % 128, 1)
        ref[...] = part[0:1, :size]
    for copy in stores:
        copy.wait()


def shards(
    hidden_in, out_grad, doc_ids, w_query, w_key, w_value, w_output, w_up, w_gate, w_down,
    scale_qk, alpha_attn, alpha_mlp, scale_up, scale_gate,
):
    n = lax.axis_size("dp")
    mbs, rows, width = hidden_in.shape
    seq = doc_ids.shape[2]
    hw = w_query.shape[1]
    hidden = w_up.shape[1]
    shard = w_query.shape[0]
    nz = n // 2
    flat = 4 * lax.axis_index("dp") + lax.axis_index("tensor")

    small = jnp.stack(
        [jnp.pad(item, (0, 128 - item.shape[0])) for item in (scale_qk, alpha_attn, alpha_mlp, scale_up, scale_gate)]
        + [jnp.zeros((128,), F32)] * 3
    )

    any_ = pl.BlockSpec(memory_space=pl.ANY)
    vm = pltpu.VMEM
    dma = pltpu.SemaphoreType.DMA

    def sds(shape, dtype):
        return jax.ShapeDtypeStruct(shape, dtype)

    res_shapes = dict(
        out=((mbs, rows, width), BF16),
        w=((4, width, width), BF16),
        x=((mbs, seq, width), BF16),
        q=((mbs, seq, hw), BF16),
        k=((mbs, seq, hw), BF16),
        v=((mbs, seq, hw), BF16),
        rq=((mbs, seq, hw), BF16),
        rk=((mbs, seq, hw), BF16),
        lrow=((mbs, seq // 16, 128), F32),
        mixed=((mbs, seq, hw), BF16),
        mid=((mbs, seq, width), BF16),
        up=((mbs, seq, hidden), BF16),
        gate=((mbs, seq, hidden), BF16),
        inner=((mbs, seq, hidden), BF16),
        attn=((mbs, rows, width), F32),
        gmd=((mbs, rows, width), F32),
        gm=((mbs, rows, width), BF16),
        gm0=((seq, width), BF16),
        vec=((8, width), F32),
        acc=((40, width), F32),
        tab=((mbs, seq, 128), F32),
        ir=((mbs, 8, seq), F32),
    )
    r = {key: sds(*val) for key, val in res_shapes.items()}
    s = {key: vm(*val) for key, val in res_shapes.items()}
    nvec = 5 * (width // 128)
    own32 = vm((mbs, rows, width), F32)
    scat = [vm((mbs, 3, rows, width), BF16), vm((mbs, 3, rows, width), BF16)]
    heads = hw // DH
    res = pl.pallas_call(
        functools.partial(fwd_kernel, n),
        name="fwd",
        out_shape=tuple(r.values()),
        in_specs=[any_] * 11,
        out_specs=tuple([any_] * len(r)),
        scratch_shapes=[
            s["w"], s["x"], s["q"], s["k"], s["v"], s["rq"], s["rk"],
            vm((mbs, seq, 128), F32),
            s["mixed"], s["mid"], s["up"], s["gate"], s["inner"],
            s["attn"], own32, own32, s["gmd"], s["gm"], s["gm0"], s["vec"], s["acc"],
            s["tab"], s["ir"],
            vm((4 * n, 8, 128), F32),
            vm((mbs, 1, seq), jnp.int32),
            vm((mbs, rows, width), BF16), vm((mbs, rows, width), BF16),
            vm((heads * QB, hw), BF16),
            *scat,
            dma((4, n)), dma((4, n)),
            dma((n + 2,)), dma((n + 2,)),
            dma((16,)),
            dma((mbs, 3)), dma((mbs, 3)), dma((mbs, 3)), dma((mbs, 3)), dma((3,)), dma((3,)),
            dma((mbs, 3)), dma((mbs, 3)), dma((mbs, 3)), dma((mbs, 3)),
            dma((40,)),
        ],
        compiler_params=pltpu.CompilerParams(
            collective_id=0, has_side_effects=True, vmem_limit_bytes=VMEM_LIMIT
        ),
    )(w_query, w_key, w_value, w_output.T, w_up, w_gate, w_down.T, hidden_in, out_grad, small, doc_ids)
    r = dict(zip(r, res))

    gshape = sds((shard, hw), F32)
    fshape = sds((shard, hidden), F32)
    grads = pl.pallas_call(
        functools.partial(bwd_kernel, n),
        name="bwd",
        out_shape=(
            sds((mbs, rows, width), BF16), gshape, gshape, gshape, gshape, fshape, fshape, fshape,
            sds((4, nvec, 128), F32),
        ),
        in_specs=[any_] * 22,
        out_specs=tuple([any_] * 9),
        scratch_shapes=[
            s["w"], s["q"], s["k"], s["v"], s["rq"], s["rk"], s["lrow"], s["mixed"],
            s["up"], s["gate"], s["inner"], s["attn"], s["gmd"],
            s["x"], s["x"], s["vec"], s["acc"],
            s["tab"], s["ir"],
            vm((hw, seq), BF16), vm((hw, seq), F32), vm((seq, hw), F32), vm((seq, hw), F32),
            own32,
            vm((4, nz, shard, width), BF16), vm((4, nz - 1, shard, width), BF16),
            vm((nvec, 128), F32), vm((n - 1, nvec, 128), F32), vm((4, nvec, 128), F32),
            *scat,
            dma((48,)), dma((3,)), dma((3,)), dma((mbs, 3)), dma((mbs, 3)),
            dma((mbs, 3)), dma((mbs, 3)), dma((mbs, 3)), dma((mbs, 3)),
            dma((5, nz)), dma((5, nz)), dma((5, nz - 1)), dma((5, nz - 1)),
            dma((n + 2,)), dma((n + 2,)),
            dma((16,)),
        ],
        compiler_params=pltpu.CompilerParams(
            collective_id=1, has_side_effects=True, vmem_limit_bytes=VMEM_LIMIT
        ),
    )(
        hidden_in, r["w"], r["x"], r["q"], r["k"], r["v"], r["rq"], r["rk"], r["lrow"],
        r["mixed"], r["mid"], r["up"], r["gate"], r["inner"], r["attn"], r["gmd"], r["gm"], r["gm0"],
        r["vec"], r["acc"], r["tab"], r["ir"],
    )
    g_in, gq, gk, gv, go, gu, gg, gd, tv = grads
    results = [gq, gk, gv, gu, gg, r["out"], g_in, go, gd]
    turned = 2 if shard % 128 == 0 else 0
    if not turned:
        results = results[:-2]
    finals = [sds(item.shape, item.dtype) for item in results]
    for i in range(len(results) - turned, len(results)):
        finals[i] = sds(finals[i].shape[::-1], F32)
    ones = [scale_qk, alpha_attn, alpha_mlp, scale_up, scale_gate]
    done = pl.pallas_call(
        functools.partial(out_kernel, turned, hw),
        name="results",
        out_shape=tuple(finals) + tuple(sds((1, item.shape[0]), F32) for item in ones),
        in_specs=[any_] * (len(results) + 1),
        out_specs=(any_,) * len(finals) + (pl.BlockSpec(memory_space=vm),) * 5,
        scratch_shapes=[
            vm(tv.shape, F32),
            *[vm(item.shape, item.dtype) for item in results],
            *[vm(item.shape, item.dtype) for item in finals[len(results) - turned :]],
            dma((len(results) + 1,)), dma((len(results),)),
        ],
        compiler_params=pltpu.CompilerParams(vmem_limit_bytes=VMEM_LIMIT // 2),
    )(tv, *results)
    vecs = [item.reshape(-1) for item in done[len(finals) :]]
    gq, gk, gv, gu, gg, out, g_in = done[:7]
    go, gd = done[7:9] if turned else (go.T, gd.T)
    return (out, g_in, gq, gk, gv, go, gu, gg, gd, *vecs)


def solution(mesh):
    rows = P("dp", "tensor", None)
    inward = P("dp", "tensor")
    outward = P("tensor", "dp")
    flat = P(("dp", "tensor"))
    weights = (inward, inward, inward, outward, inward, inward, outward)
    in_specs = (rows, rows, P("dp", None, None)) + weights + (flat,) * 5
    out_specs = (rows, rows) + weights + (flat,) * 5
    return jax.shard_map(shards, mesh=mesh, in_specs=in_specs, out_specs=out_specs, check_vma=False)
```

```python
import functools
import math

import jax
import jax.numpy as jnp
from jax import lax
from jax.experimental import pallas as pl
from jax.experimental.pallas import tpu as pltpu
from jax.sharding import PartitionSpec as P

DH = 64
BLOCK = 256
DOCS = 3
DOC_MAX = 512
F32 = jnp.float32
BF16 = jnp.bfloat16
MESH = pl.DeviceIdType.MESH
VMEM_LIMIT = 67043328
LOG2E = 1.4426950408889634
QB = 128
WIDE = 512
CODE = 8


def nn(a, b):
    return jnp.dot(a, b, preferred_element_type=F32)


def nt(a, b):
    return lax.dot_general(a, b, (((1,), (1,)), ((), ())), preferred_element_type=F32)


def tn(a, b):
    return lax.dot_general(a, b, (((0,), (0,)), ((), ())), preferred_element_type=F32)


def split_sum(vals, ones):
    high = vals.astype(BF16)
    low = (vals - high.astype(F32)).astype(BF16)
    return nn(high, ones) + nn(low, ones)


def lane_iota(shape):
    return lax.broadcasted_iota(jnp.int32, shape, len(shape) - 1)


def head_ones():
    rows = lax.broadcasted_iota(jnp.int32, (128, 128), 0) // DH
    cols = lax.broadcasted_iota(jnp.int32, (128, 128), 1) // DH
    return jnp.where(rows == cols, 1.0, 0.0).astype(BF16)


def partner(vals):
    low = lane_iota(vals.shape) % DH < DH // 2
    return jnp.where(low, pltpu.roll(vals, 128 - DH // 2, 1), pltpu.roll(vals, DH // 2, 1))


def turns(table):
    lane = lane_iota(table.shape)
    both = jnp.where(lane < DH, table, pltpu.roll(table, DH, 1))
    low = lane % DH < DH // 2
    cosine = jnp.where(low, both, pltpu.roll(both, DH // 2, 1))
    sine = jnp.where(low, -pltpu.roll(both, 128 - DH // 2, 1), both)
    return cosine, sine


class Place:
    def __init__(self, n):
        self.n = n
        self.t = lax.axis_index("tensor")
        self.d = lax.axis_index("dp")
        t, d = self.t, self.d
        self.sib = t + 1 - 2 * (t % 2)
        self.yp = (t + 2) % 4
        self.diag = (self.sib + 2) % 4
        self.xi = d % 2
        self.z = d // 2
        self.nz = n // 2
        self.xn = d + 1 - 2 * (d % 2)
        self.zpeers = [2 * ((self.z + k) % self.nz) + self.xi for k in range(1, self.nz)]
        self.dpeers = [(d + k) % n for k in range(1, n)]
        self.tpeers = [(t + k) % 4 for k in range(1, 4)]

    def barrier(self):
        sem = pltpu.get_barrier_semaphore()
        for peer in self.dpeers:
            pl.semaphore_signal(sem, inc=1, device_id={"dp": peer}, device_id_type=MESH)
        for peer in self.tpeers:
            pl.semaphore_signal(sem, inc=1, device_id={"tensor": peer}, device_id_type=MESH)
        pl.semaphore_wait(sem, self.n + 2)


def remote(src, dst, ssem, rsem, **where):
    return pltpu.make_async_remote_copy(
        src_ref=src, dst_ref=dst, send_sem=ssem, recv_sem=rsem, device_id=where, device_id_type=MESH
    )


class Gather:
    def __init__(self, place, whole, ssem, rsem, rows):
        self.p, self.whole, self.ssem, self.rsem, self.rows = place, whole, ssem, rsem, rows

    def at(self, index):
        return self.whole.at[pl.ds(pl.multiple_of(index * self.rows, self.rows), self.rows)]

    def start(self, own):
        p = self.p
        self.c_yp = remote(own, self.at(p.t), self.ssem.at[1], self.rsem.at[1], tensor=p.yp)
        self.c_sib = remote(own, self.at(p.t), self.ssem.at[0], self.rsem.at[0], tensor=p.sib)
        self.c_yp.start()
        self.c_sib.start()

    def wait(self, step):
        p = self.p
        if step == 1:
            remote(self.at(p.sib), self.at(p.sib), self.ssem.at[0], self.rsem.at[0], tensor=p.sib).wait_recv()
        if step == 2:
            remote(self.at(p.yp), self.at(p.yp), self.ssem.at[1], self.rsem.at[1], tensor=p.yp).wait_recv()
            self.forward().start()
        if step == 3:
            remote(self.at(p.diag), self.at(p.diag), self.ssem.at[2], self.rsem.at[2], tensor=p.sib).wait_recv()

    def forward(self):
        p = self.p
        return remote(self.at(p.yp), self.at(p.yp), self.ssem.at[2], self.rsem.at[2], tensor=p.sib)

    def drain(self):
        self.c_yp.wait_send()
        self.c_sib.wait_send()
        self.forward().wait_send()

    def each(self, work):
        blocks(self.p, work, self.wait)


def blocks(p, work, wait=None):
    def body(i, carry):
        for step in range(1, 4):
            if wait is not None:
                pl.when(i == step)(functools.partial(wait, step))
        work((p.t // 2 + i // 2) % 2 * 2 + (p.t + i) % 2)
        return carry

    lax.fori_loop(0, 4, body, 0)


class Scatter:
    def __init__(self, place, sbuf, rbuf, ssem, rsem):
        self.p, self.sbuf, self.rbuf, self.ssem, self.rsem = place, sbuf, rbuf, ssem, rsem

    def copy(self, slot):
        where = self.p.yp if slot == 2 else self.p.sib
        return remote(self.sbuf.at[slot], self.rbuf.at[slot], self.ssem.at[slot], self.rsem.at[slot], tensor=where)

    def arrive(self, slot):
        self.copy(slot).wait_recv()

    def run(self, part, own):
        p = self.p

        def send(slot):
            vals = own[...]
            if slot == 2:
                self.arrive(0)
                vals = vals + self.rbuf[0].astype(F32)
            self.sbuf[slot] = vals.astype(BF16)
            self.copy(slot).start()

        def body(i, carry):
            own[...] = part((p.t // 2 + (i + 1) % 2) % 2 * 2 + (p.t + 1 - i // 2) % 2)
            for slot in range(3):
                pl.when(i == slot)(functools.partial(send, slot))
            return carry

        lax.fori_loop(0, 4, body, 0)

    def finish(self):
        self.arrive(1)
        self.arrive(2)
        for slot in range(3):
            self.copy(slot).wait_send()


def rows_of(ref, index, rows):
    return ref[pl.ds(pl.multiple_of(index * rows, rows), rows)]


def mean_sq(vals):
    return jnp.mean(vals * vals, axis=-1, keepdims=True)


def fold8(vals):
    total = vals[0:8]
    for k in range(1, vals.shape[0] // 8):
        total = total + vals[8 * k : 8 * k + 8]
    return total


def fwd_kernel(
    n,
    wq, wk, wv, wo, wu, wg, wd, hid, og, small, docs,
    o_out, o_w, o_x, o_q, o_k, o_v, o_rq, o_rk, o_lrow, o_mixed, o_mid, o_up, o_gate, o_inner,
    o_attn, o_gmd, o_gm, o_gm0, o_vec, o_acc, o_tab, o_ir,
    w, x, q, k, v, rq, rk, lcol, mixed, mid, up, gate, inner,
    attn, midf, mlp, gmd, gm, gm0, vec, acc, tab, ir, sall, docv, ogv, outv, qm, sbuf, rbuf,
    wsend, wrecv, small_s, small_r, lsem, agx_s, agx_r, agm_s, agm_r, agg_s, agg_r,
    rsa_s, rsa_r, rsm_s, rsm_r, osem,
):
    p = Place(n)
    nz = p.nz
    mbs, rows, width = hid.shape
    seq = x.shape[1]
    hw = q.shape[2]
    shard = wq.shape[0]
    heads = hw // DH
    groups = w.shape[0]
    hidden = up.shape[2]

    pieces = ((0, 0, 3 * hw), (0, 3 * hw, 4 * hw), (1, 0, hidden), (2, 0, hidden), (3, 0, hidden))

    def wat(key, index):
        g, lo, hi = pieces[key]
        return w.at[g, pl.ds(pl.multiple_of(index * shard, shard), shard), pl.ds(lo, hi - lo)]

    local = []

    def lcopy(src, dst):
        copy = pltpu.make_async_copy(src, dst, lsem.at[len(local)])
        copy.start()
        local.append(copy)
        return copy

    outs = []

    def ocopy(src, dst):
        copy = pltpu.make_async_copy(src, dst, osem.at[len(outs)])
        copy.start()
        outs.append(copy)

    own_w = pl.ds(pl.multiple_of(p.d * shard, shard), shard)
    w_in = [lcopy(src, w.at[0, own_w, pl.ds(i * hw, hw)]) for i, src in enumerate((wq, wk, wv, wo))]
    w_in += [lcopy(src, w.at[i + 1, own_w]) for i, src in enumerate((wu, wg, wd))]
    docs_in = lcopy(docs, docv)
    p.barrier()

    gx = [Gather(p, x.at[m], agx_s.at[m], agx_r.at[m], rows) for m in range(mbs)]
    gmi = [Gather(p, mid.at[m], agm_s.at[m], agm_r.at[m], rows) for m in range(mbs)]
    slot = p.t * n + p.d
    small_own = lcopy(small, sall.at[slot])
    small_d = [
        remote(small, sall.at[slot], small_s.at[i], small_r.at[i], dp=peer)
        for i, peer in enumerate(p.dpeers)
    ]
    for copy in small_d:
        copy.start()
    gx[0].start(hid.at[0])
    sends = []

    def wsend_to(g, i, src, index, peer):
        copy = remote(src, wat(g, index), wsend.at[g, i], wrecv.at[g, index], dp=peer)
        copy.start()
        sends.append(copy)

    def relay(g):
        for i, peer in reversed(list(enumerate(p.zpeers))):
            remote(wat(g, peer), wat(g, peer), wsend.at[g, 0], wrecv.at[g, peer], dp=p.xn).wait_recv()
            wsend_to(g, nz + i, wat(g, peer), peer, p.xn)

    for copy in w_in:
        copy.wait()
    for g in range(len(pieces)):
        for i, peer in enumerate(p.zpeers):
            wsend_to(g, i, wat(g, p.d), p.d, peer)
        if g == 0:
            wsend_to(0, nz - 1, wat(0, p.d), p.d, p.xn)
    xown = [lcopy(hid.at[m], gx[m].at(p.t)) for m in range(mbs)]
    og_in = lcopy(og, ogv)
    for i, peer in enumerate(p.dpeers):
        src = p.t * n + (p.d + n - (i + 1)) % n
        remote(sall.at[src], sall.at[src], small_s.at[i], small_r.at[i], dp=peer).wait_recv()
    small_own.wait()
    small_t = []
    for i, peer in enumerate(p.tpeers):
        part = sall.at[pl.ds(p.t * n, n)]
        copy = remote(part, part, small_s.at[n - 1 + i], small_r.at[n - 1 + i], tensor=peer)
        copy.start()
        small_t.append(copy)
    gx[1].start(hid.at[1])

    def wready(g):
        remote(wat(g, p.xn), wat(g, p.xn), wsend.at[g, 0], wrecv.at[g, p.xn], dp=p.xn).wait_recv()
        for peer in p.zpeers:
            other = peer + 1 - 2 * p.xi
            remote(wat(g, other), wat(g, other), wsend.at[g, 0], wrecv.at[g, other], dp=p.xn).wait_recv()
        if g:
            g, _, _ = pieces[g]
            ocopy(w.at[g], o_w.at[g])

    docs_in.wait()
    for m in range(mbs):
        doc = docv[m]
        count = [jnp.sum(jnp.where(doc == i, 1.0, 0.0), axis=1, keepdims=True) for i in range(DOCS - 1)]
        first = jnp.zeros(doc.shape, F32)
        for i in range(DOCS - 1):
            first = first + jnp.where(doc > i, count[i], 0.0)
        place = lane_iota(doc.shape).astype(F32) - first
        low = doc.astype(F32) * CODE
        code = low + jnp.floor(place * (1.0 / BLOCK))
        line = lax.broadcasted_iota(jnp.int32, (8, seq), 0)
        ir[m] = jnp.where(line == 0, code, jnp.where(line == 1, low, place))
        line = lax.broadcasted_iota(jnp.int32, (128, seq), 0)
        every_row = jnp.where(line == DH, code, jnp.where(line == DH + 1, low, place))
        tab[m] = jnp.transpose(every_row, (1, 0))

    def turn_rows(i, carry):
        at = pl.ds(pl.multiple_of(i % (seq // 64) * 64, 64), 64)
        m = i // (seq // 64)
        lane = lane_iota((1, 128))
        freq = jnp.exp((lane % (DH // 2)).astype(F32) * (-math.log(10000.0) / (DH // 2)))
        shift = jnp.where(lane < DH // 2, 0.5 * math.pi, 0.0)
        old = tab[m, at, :]
        tab[m, at, :] = jnp.where(lane < DH, jnp.sin(old[:, 0:1] * freq + shift), old)
        return carry

    lax.fori_loop(0, mbs * (seq // 64), turn_rows, 0)
    acc[...] = jnp.zeros_like(acc)

    relay(0)
    for g in range(1, len(pieces)):
        wsend_to(g, nz - 1, wat(g, p.d), p.d, p.xn)
    for i, peer in enumerate(p.tpeers):
        part = sall.at[pl.ds((p.t + 4 - (i + 1)) % 4 * n, n)]
        remote(part, part, small_s.at[n - 1 + i], small_r.at[n - 1 + i], tensor=peer).wait_recv()
    every = 4 * n

    def gathered(row, base, count, lanes):
        per = count // (lanes // 128)

        def item(k):
            part = sall[k % 4 * n + base + k // 4, row : row + 1, :]
            turn = k % per * (128 // per)
            return pltpu.roll(part, turn, 1) if turn else part

        for r in range(lanes // 128):
            total = item(r * per)
            for j in range(1, per):
                total = total + item(r * per + j)
            vec[row : row + 1, 128 * r : 128 * r + 128] = total

    gathered(0, p.t * (n // 4), n, hw)
    gathered(1, 0, every, width)
    gathered(2, 0, every, width)
    gathered(3, p.t * (n // 4), n, hidden)
    gathered(4, p.t * (n // 4), n, hidden)
    wready(0)

    ones = head_ones()

    def stage_qkv(m):
        xown[m].wait()

        def work(index):
            at = pl.ds(pl.multiple_of(index * rows, rows), rows)
            xb = x[m, at, :]
            cb, sb = turns(tab[m, at, :])
            for which, (dst, rdst) in enumerate(((q, rq), (k, rk))):
                raw = nn(xb, w[0, :, which * hw : (which + 1) * hw])
                for half in range(hw // 128):
                    lanes = slice(128 * half, 128 * half + 128)
                    piece = raw[:, lanes]
                    turned = piece * cb + partner(piece) * sb
                    scale = lax.rsqrt(split_sum(turned * turned, ones) + 1e-06)
                    rdst[m, at, lanes] = scale.astype(BF16)
                    dst[m, at, lanes] = (turned * scale * vec[0:1, lanes]).astype(BF16)
            v[m, at, :] = nn(xb, w[0, :, 2 * hw : 3 * hw]).astype(BF16)

        gx[m].each(work)

    win = seq - 128
    c_exp = math.sqrt(DH) * LOG2E

    def attend(m):
        def body(b, carry):
            at = pl.ds(pl.multiple_of(b * QB, QB), QB)
            keys = pl.ds(pl.multiple_of(((b + 3) // 8) * 128, 128), win)
            ccol = tab[m, at, DH : DH + 1]
            lcol_ = tab[m, at, DH + 1 : DH + 2]
            crow = ir[m, 0:1, keys]
            bias = jnp.where((crow <= ccol) & (crow >= lcol_), 0.0, -1e30)
            qb = q[m, at, :]
            lane = lane_iota((QB, hw)) // DH
            for h in range(heads):
                qm[h * QB : (h + 1) * QB, :] = jnp.where(lane == h, qb, jnp.zeros_like(qb))
            kb = k[m, keys, :]
            vb = v[m, keys, :]
            total = jnp.zeros((QB, hw), F32)
            lsum = jnp.zeros((QB, 128), F32)
            lane_l = lane_iota((QB, 128))
            for h in range(heads):
                scores = nt(qm[h * QB : (h + 1) * QB, :], kb)
                expo = jnp.exp2(scores * c_exp + bias)
                inv = 1.0 / jnp.sum(expo, axis=-1, keepdims=True)
                part = nn(expo.astype(BF16), vb)
                total = jnp.where(lane == h, part * inv, total)
                lsum = jnp.where(lane_l == h, inv, lsum)
            mixed[m, at, :] = total.astype(BF16)
            lcol[m, at, :] = lsum
            return carry

        lax.fori_loop(0, seq // QB, body, 0)

    sc_a = [Scatter(p, sbuf.at[m], rbuf.at[m], rsa_s.at[m], rsa_r.at[m]) for m in range(mbs)]
    sc_m = [Scatter(p, sbuf.at[m], rbuf.at[m], rsm_s.at[m], rsm_r.at[m]) for m in range(mbs)]

    def stage_o(m):
        sc_a[m].run(
            lambda index: nt(rows_of(mixed.at[m], index, rows), w[0, :, 3 * hw : 3 * hw + hw]),
            attn.at[m],
        )

    chunk = 32

    def stage_mid(m):
        sc_a[m].finish()
        base = p.t * rows

        def body(i, carry):
            at = pl.ds(pl.multiple_of(i * chunk, chunk), chunk)
            own = pl.ds(pl.multiple_of(base + i * chunk, chunk), chunk)
            a = attn[m, at, :] + rbuf[m, 1, at, :].astype(F32) + rbuf[m, 2, at, :].astype(F32)
            attn[m, at, :] = a
            h = x[m, own, :].astype(F32)
            na = a * lax.rsqrt(mean_sq(a) + 1e-06)
            zz = h + vec[1:2, :] * (na - h)
            out = zz * lax.rsqrt(mean_sq(zz) + 1e-06)
            midf[m, at, :] = out
            mid[m, own, :] = out.astype(BF16)
            return carry

        lax.fori_loop(0, rows // chunk, body, 0)
        gmi[m].start(gmi[m].at(p.t))


    def stage_up(m):
        def work(index):
            at = pl.ds(pl.multiple_of(index * rows, rows), rows)

            def body(c, carry):
                lanes = pl.ds(pl.multiple_of(c * WIDE, WIDE), WIDE)
                mb = mid[m, at, :]
                u = nn(mb, w[1, :, lanes])
                g = nn(mb, w[2, :, lanes])
                up[m, at, lanes] = u.astype(BF16)
                gate[m, at, lanes] = g.astype(BF16)
                gs = g * vec[4:5, lanes]
                inner[m, at, lanes] = ((u * vec[3:4, lanes]) * (gs / (1.0 + jnp.exp(-gs)))).astype(BF16)
                return carry

            lax.fori_loop(0, hidden // WIDE, body, 0)

        gmi[m].each(work)

    def stage_down(m):
        sc_m[m].run(lambda index: nt(rows_of(inner.at[m], index, rows), w[3]), mlp.at[m])

    gg = Gather(p, gm0, agg_s, agg_r, rows)

    def stage_end(m):
        sc_m[m].finish()

        def body(i, carry):
            at = pl.ds(pl.multiple_of(i * chunk, chunk), chunk)
            a = mlp[m, at, :] + rbuf[m, 1, at, :].astype(F32) + rbuf[m, 2, at, :].astype(F32)
            h = midf[m, at, :]
            ra = lax.rsqrt(mean_sq(a) + 1e-06)
            na = a * ra
            al = vec[2:3, :]
            zz = h + al * (na - h)
            rz = lax.rsqrt(mean_sq(zz) + 1e-06)
            out = zz * rz
            outv[m, at, :] = out.astype(BF16)
            cot = ogv[m, at, :].astype(F32)
            dz = rz * (cot - out * jnp.mean(cot * out, axis=-1, keepdims=True))
            dn = al * dz
            acc[0:8, :] += fold8(dz * (na - h))
            gmd[m, at, :] = dz - dn
            grad = (ra * (dn - na * jnp.mean(dn * na, axis=-1, keepdims=True))).astype(BF16)
            gm[m, at, :] = grad
            if m == 0:
                gm0[pl.ds(pl.multiple_of(p.t * rows + i * chunk, chunk), chunk), :] = grad
            return carry

        lax.fori_loop(0, rows // chunk, body, 0)
        if m == 0:
            gg.start(gg.at(p.t))

    stage_qkv(0)
    relay(1)
    attend(0)
    relay(2)
    wready(1)
    stage_o(0)
    stage_qkv(1)
    attend(1)
    stage_mid(0)
    relay(3)
    stage_o(1)
    for m in range(mbs):
        ocopy(x.at[m], o_x.at[m])
        ocopy(q.at[m], o_q.at[m])
        ocopy(k.at[m], o_k.at[m])
        ocopy(v.at[m], o_v.at[m])
        ocopy(rq.at[m], o_rq.at[m])
        ocopy(rk.at[m], o_rk.at[m])
        ocopy(mixed.at[m], o_mixed.at[m])
    ocopy(vec, o_vec)
    ocopy(tab, o_tab)
    ocopy(ir, o_ir)
    relay(4)
    wready(2)
    wready(3)
    stage_up(0)
    stage_mid(1)
    wready(4)
    stage_down(0)
    stage_up(1)
    stage_down(1)
    og_in.wait()
    stage_end(0)
    ocopy(mid.at[0], o_mid.at[0])
    ocopy(up.at[0], o_up.at[0])
    ocopy(gate.at[0], o_gate.at[0])
    ocopy(inner.at[0], o_inner.at[0])
    for m in range(mbs):
        lrow = jnp.transpose(lcol[m], (1, 0))
        lcol[m, 0:8, 0:128] = lrow[0:8, 0:128]
        for j in range(1, seq // 128):
            lcol[m, 8 * j : 8 * j + 8, 0:128] = lrow[0:8, 128 * j : 128 * j + 128]
        ocopy(lcol.at[m, pl.ds(0, seq // 16)], o_lrow.at[m])
    ocopy(mid.at[1], o_mid.at[1])
    ocopy(up.at[1], o_up.at[1])
    ocopy(gate.at[1], o_gate.at[1])
    ocopy(inner.at[1], o_inner.at[1])
    ocopy(attn, o_attn)
    for step in range(1, 3):
        gg.wait(step)
    stage_end(1)
    ocopy(outv, o_out)
    ocopy(gmd, o_gmd)
    ocopy(gm, o_gm)
    ocopy(acc, o_acc)
    gg.wait(3)
    ocopy(gm0, o_gm0)
    for gather in gx + gmi + [gg]:
        gather.drain()
    for copy in sends + small_t + small_d:
        copy.wait_send()
    for copy in outs:
        copy.wait()


def bwd_kernel(
    n,
    hid, i_w, i_x, i_q, i_k, i_v, i_rq, i_rk, i_lrow, i_mixed, i_mid, i_up, i_gate,
    i_inner, i_attn, i_gmd, i_gm, i_gm0, i_vec, i_acc, i_tab, i_ir,
    o_in, o_gq, o_gk, o_gv, o_go, o_gu, o_gg, o_gd, o_tv,
    w, q, k, v, rq, rk, lrow, mixed, up, gate, inner, attn, gmd, gm, ga, vec, acc,
    tab, ir, kt, dqt, dk, dv, outv, xrecv, zrecv, vsend, vrecv, tv, sbuf, rbuf,
    lsem, agg_s, agg_r, aga_s, aga_r, rsm_s, rsm_r, rsi_s, rsi_r, xs, xr, zs, zr, vs, vr, osem,
):
    p = Place(n)
    nz = p.nz
    mbs, rows, width = hid.shape
    seq = q.shape[1]
    hw = q.shape[2]
    heads = hw // DH
    hidden = up.shape[2]
    groups = w.shape[0]
    shard = width // n
    gmix = [inner.at[m, :, pl.ds(0, hw)] for m in range(mbs)]
    pts, dss = (inner.at[m, pl.ds(0, seq - 128), pl.ds(hw, heads * QB)] for m in range(2))
    qs, gs = (
        inner.at[0, pl.ds(i * heads * QB, heads * QB), pl.ds(hw + heads * QB, hw)] for i in range(2)
    )

    local = []

    def lcopy(src, dst):
        copy = pltpu.make_async_copy(src, dst, lsem.at[len(local)])
        copy.start()
        local.append(copy)
        return copy

    outs = []

    def ocopy(src, dst):
        copy = pltpu.make_async_copy(src, dst, osem.at[len(outs)])
        copy.start()
        outs.append(copy)

    l_gm0 = lcopy(i_gm0, gm.at[0])
    l_w3 = lcopy(i_w.at[3], w.at[3])
    l_ug = [[lcopy(i_up.at[m], up.at[m]), lcopy(i_gate.at[m], gate.at[m])] for m in range(mbs)]
    l_vec = [lcopy(i_vec, vec), lcopy(i_acc, acc)]
    p.barrier()
    gg = Gather(p, gm.at[1], agg_s, agg_r, rows)
    gg.start(i_gm.at[1])
    l_gm1 = lcopy(i_gm.at[1], gg.at(p.t))
    l_w12 = [lcopy(i_w.at[1], w.at[1]), lcopy(i_w.at[2], w.at[2])]
    l_inner = [lcopy(i_inner.at[m], inner.at[m]) for m in range(mbs)]
    l_rows = [lcopy(i_attn, attn), lcopy(i_gmd, gmd)]
    l_w0 = lcopy(i_w.at[0], w.at[0])
    l_att = [
        [
            lcopy(src.at[m], dst.at[m])
            for src, dst in ((i_q, q), (i_k, k), (i_v, v), (i_rq, rq), (i_rk, rk), (i_lrow, lrow), (i_mixed, mixed))
        ]
        for m in range(mbs)
    ]
    l_tab = [lcopy(i_tab, tab), lcopy(i_ir, ir)]

    gga = [Gather(p, ga.at[m], aga_s.at[m], aga_r.at[m], rows) for m in range(mbs)]
    l_hid = [lcopy(hid.at[m], gga[m].at(p.t)) for m in range(mbs)]
    sc_m = [Scatter(p, sbuf.at[m], rbuf.at[m], rsm_s.at[m], rsm_r.at[m]) for m in range(mbs)]
    sc_i = [Scatter(p, sbuf.at[m], rbuf.at[m], rsi_s.at[m], rsi_r.at[m]) for m in range(mbs)]
    cols = 256
    chunk = 32

    def stage_inner(m):
        if m == 1:
            l_gm1.wait()

        def work(index):
            at = pl.ds(pl.multiple_of(index * rows, rows), rows)

            def body(c, carry):
                lanes = pl.ds(pl.multiple_of(c * WIDE, WIDE), WIDE)
                gi = nn(gm[m, at, :], w[3, :, lanes])
                u = up[m, at, lanes].astype(F32)
                g = gate[m, at, lanes].astype(F32)
                su = vec[3:4, lanes]
                sg = vec[4:5, lanes]
                gsc = g * sg
                sig = 1.0 / (1.0 + jnp.exp(-gsc))
                gu = gi * (gsc * sig)
                ggs = gi * (u * su) * sig * (1.0 + gsc * (1.0 - sig))
                acc[16:24, lanes] += fold8(gu * u)
                acc[24:32, lanes] += fold8(ggs * g)
                up[m, at, lanes] = (gu * su).astype(BF16)
                gate[m, at, lanes] = (ggs * sg).astype(BF16)
                return carry

            lax.fori_loop(0, hidden // WIDE, body, 0)

        blocks(p, work, gg.wait if m == 1 else None)

    def stage_back(m):
        sc_m[m].run(
            lambda index: nt(rows_of(up.at[m], index, rows), w[1])
            + nt(rows_of(gate.at[m], index, rows), w[2]),
            outv.at[m],
        )

    def stage_attn(m):
        sc_m[m].finish()
        base = p.t * rows

        def body(i, carry):
            at = pl.ds(pl.multiple_of(i * chunk, chunk), chunk)
            own = pl.ds(pl.multiple_of(base + i * chunk, chunk), chunk)
            part = outv[m, at, :] + rbuf[m, 1, at, :].astype(F32)
            cot = gmd[m, at, :] + part + rbuf[m, 2, at, :].astype(F32)
            a = attn[m, at, :]
            h = ga[m, own, :].astype(F32)
            ra = lax.rsqrt(mean_sq(a) + 1e-06)
            na = a * ra
            al = vec[1:2, :]
            zz = h + al * (na - h)
            rz = lax.rsqrt(mean_sq(zz) + 1e-06)
            out = zz * rz
            dz = rz * (cot - out * jnp.mean(cot * out, axis=-1, keepdims=True))
            dn = al * dz
            acc[8:16, :] += fold8(dz * (na - h))
            gmd[m, at, :] = dz - dn
            ga[m, own, :] = (ra * (dn - na * jnp.mean(dn * na, axis=-1, keepdims=True))).astype(BF16)
            return carry

        lax.fori_loop(0, rows // chunk, body, 0)
        gga[m].start(gga[m].at(p.t))

    def stage_mixed(m):
        def work(index):
            at = pl.ds(pl.multiple_of(index * rows, rows), rows)
            gmix[m][at, :] = nn(ga[m, at, :], w[0, :, 3 * hw : 4 * hw]).astype(BF16)

        gga[m].each(work)

    win = seq - 128
    c_exp = math.sqrt(DH) * LOG2E
    ones = head_ones()

    def attend(m):
        kt[...] = jnp.transpose(k[m], (1, 0))
        dk[...] = jnp.zeros_like(dk)
        dv[...] = jnp.zeros_like(dv)

        def body(b, carry):
            at = pl.ds(pl.multiple_of(b * QB, QB), QB)
            keys = pl.ds(pl.multiple_of(((b + 3) // 8) * 128, 128), win)
            crow = ir[m, 0:1, at]
            lrow_ = ir[m, 1:2, at]
            ccol = tab[m, keys, DH : DH + 1]
            bias = jnp.where((ccol <= crow) & (ccol >= lrow_), 0.0, -1e30)
            qb = q[m, at, :]
            gb = gmix[m][at, :]
            lane = lane_iota((QB, hw)) // DH
            for h in range(heads):
                qs[h * QB : (h + 1) * QB, :] = jnp.where(lane == h, qb, jnp.zeros_like(qb))
                gs[h * QB : (h + 1) * QB, :] = jnp.where(lane == h, gb, jnp.zeros_like(gb))
            kb = k[m, keys, :]
            vb = v[m, keys, :]
            for h in range(heads):
                hl = slice(h * QB, (h + 1) * QB)
                scores = nt(kb, qs[hl, :])
                inv = lrow[m, pl.ds(pl.multiple_of(b * 8, 8), 8), :][h : h + 1, :]
                pt = jnp.exp2(scores * c_exp + bias) * inv
                dpt = nt(vb, gs[hl, :])
                delta = jnp.sum(pt * dpt, axis=0, keepdims=True)
                dst = (pt * (dpt - delta)).astype(BF16)
                pts[:, hl] = pt.astype(BF16)
                dss[:, hl] = dst
                dqt[h * DH : (h + 1) * DH, at] = nn(kt[h * DH : (h + 1) * DH, keys], dst)
            dv[keys, :] += nn(pts[...], gs[...])
            dk[keys, :] += nn(dss[...], qs[...])
            return carry

        lax.fori_loop(0, seq // QB, body, 0)

        step = 256

        def after(i, carry):
            at = pl.ds(pl.multiple_of(i * step, step), step)
            cb, sb = turns(tab[m, at, :])
            v[m, at, :] = dv[at, :].astype(BF16)
            for which in range(2):
                src = (q, k)[which]
                rsc = (rq, rk)[which]
                for half in range(hw // 128):
                    lanes = slice(128 * half, 128 * half + 128)
                    if which == 0:
                        grad = jnp.transpose(dqt[lanes, at], (1, 0)) * math.sqrt(DH)
                    else:
                        grad = dk[at, lanes] * math.sqrt(DH)
                    gain = vec[0:1, lanes]
                    unit = src[m, at, lanes].astype(F32) / gain
                    acc[32:40, lanes] += fold8(grad * unit)
                    dn = grad * gain
                    dy = rsc[m, at, lanes].astype(F32) * (dn - unit * split_sum(dn * unit, ones))
                    src[m, at, lanes] = (dy * cb - partner(dy) * sb).astype(BF16)
            return carry

        lax.fori_loop(0, seq // step, after, 0)

    def stage_in(m):
        def part(index):
            at = pl.ds(pl.multiple_of(index * rows, rows), rows)
            return (
                nt(q[m, at, :], w[0, :, 0:hw])
                + nt(k[m, at, :], w[0, :, hw : 2 * hw])
                + nt(v[m, at, :], w[0, :, 2 * hw : 3 * hw])
            )

        sc_i[m].run(part, outv.at[m])

    def stage_out(m):
        sc_i[m].finish()

        def body(i, carry):
            at = pl.ds(pl.multiple_of(i * chunk, chunk), chunk)
            part = outv[m, at, :] + rbuf[m, 1, at, :].astype(F32)
            total = gmd[m, at, :] + part + rbuf[m, 2, at, :].astype(F32)
            sbuf[m, 0, at, :] = total.astype(BF16)
            return carry

        lax.fori_loop(0, rows // chunk, body, 0)
        ocopy(sbuf.at[m, 0], o_in.at[m])

    pieces = {
        3: (w.at[3], 3, 0, width),
        1: (w.at[1], 1, 0, width),
        2: (w.at[2], 2, 0, width),
        0: (gm.at[0], 0, 0, 3 * hw),
        4: (gm.at[0], 0, 3 * hw, 4 * hw),
    }

    def weight_grad(key, left, rights):
        into = pieces[key][0]

        def body(c, carry):
            lanes = pl.ds(pl.multiple_of(c * cols, cols), cols)
            for lo, hi, right in rights:
                total = tn(left[0, :, lanes], right[0])
                for m in range(1, mbs):
                    total = total + tn(left[m, :, lanes], right[m])
                into[lanes, lo:hi] = total.astype(BF16)
            return carry

        lax.fori_loop(0, width // cols, body, 0)

    def wrow(key, index):
        ref, _, lo, hi = pieces[key]
        return ref.at[pl.ds(pl.multiple_of(index * shard, shard), shard), pl.ds(lo, hi - lo)]

    def held(buf, key, index):
        _, g, lo, hi = pieces[key]
        return buf.at[g, index, :, pl.ds(lo, hi - lo)]

    gsends = []

    def rs_start(key):
        for kk in list(range(1, nz)) + [0]:
            zz = (p.z + kk) % nz
            other = 2 * zz + 1 - p.xi
            copy = remote(wrow(key, other), held(xrecv, key, zz), xs.at[key, kk], xr.at[key, zz], dp=p.xn)
            copy.start()
            gsends.append(copy)

    def rs_arrive(key, kk):
        zz = (p.z + kk) % nz
        got = held(xrecv, key, zz)
        remote(got, got, xs.at[key, kk], xr.at[key, zz], dp=p.xn).wait_recv()
        return got, zz

    def rs_mid(key):
        for kk in range(1, nz):
            got, zz = rs_arrive(key, kk)
            mine = 2 * zz + p.xi
            got[...] = (got[...].astype(F32) + wrow(key, mine)[...].astype(F32)).astype(BF16)
            copy = remote(got, held(zrecv, key, kk - 1), zs.at[key, kk - 1], zr.at[key, kk - 1], dp=mine)
            copy.start()
            gsends.append(copy)

    def rs_end(key):
        _, g, lo, hi = pieces[key]
        got, _ = rs_arrive(key, 0)
        total = got[...].astype(F32) + wrow(key, p.d)[...].astype(F32)
        for kk in range(1, nz):
            got = held(zrecv, key, kk - 1)
            remote(got, got, zs.at[key, kk - 1], zr.at[key, kk - 1], dp=p.xn).wait_recv()
            total = total + got[...].astype(F32)
        fin = attn.at[g // 2, pl.ds((g % 2) * shard, shard)]
        fin[:, lo:hi] = total
        if g == 0:
            for i, dst in enumerate((o_gq, o_gk, o_gv, o_go)):
                if lo <= i * hw < hi:
                    ocopy(fin.at[:, pl.ds(i * hw, hw)], dst)
        else:
            ocopy(fin, (o_gu, o_gg, o_gd)[g - 1])

    for copy in l_vec + [l_gm0, l_w3] + l_ug[0]:
        copy.wait()
    stage_inner(0)
    for copy in l_w12:
        copy.wait()
    stage_back(0)
    for copy in l_ug[1]:
        copy.wait()
    stage_inner(1)
    for copy in l_inner + l_rows + l_hid:
        copy.wait()
    weight_grad(3, gm, [(0, hidden, inner)])
    rs_start(3)
    gg.drain()
    l_mid = [lcopy(i_mid.at[m], gm.at[m]) for m in range(mbs)]
    stage_attn(0)
    stage_back(1)
    for copy in l_mid:
        copy.wait()
    weight_grad(1, gm, [(0, hidden, up)])
    rs_start(1)
    l_x = [lcopy(i_x.at[m], up.at[m]) for m in range(mbs)]
    for copy in [l_w0] + l_tab + l_att[0] + l_att[1]:
        copy.wait()
    stage_mixed(0)
    rs_mid(3)
    attend(0)
    stage_attn(1)
    stage_in(0)
    weight_grad(2, gm, [(0, hidden, gate)])
    rs_start(2)
    rs_mid(1)
    stage_mixed(1)
    weight_grad(4, ga, [(3 * hw, 4 * hw, mixed)])
    rs_start(4)
    attend(1)
    rs_mid(2)

    per = width // 128
    for r in range(5):
        sums = jnp.sum(acc[8 * r : 8 * r + 8, :], axis=0, keepdims=True)
        for j in range(per):
            vsend[per * r + j : per * r + j + 1, :] = sums[:, 128 * j : 128 * j + 128]
    vcopies = []
    for i, peer in enumerate(p.dpeers):
        copy = remote(vsend, vrecv.at[i], vs.at[i], vr.at[i], dp=peer)
        copy.start()
        vcopies.append(copy)
    for copy in l_x:
        copy.wait()
    weight_grad(0, up, [(0, hw, q), (hw, 2 * hw, k), (2 * hw, 3 * hw, v)])
    rs_start(0)
    rs_mid(4)
    stage_in(1)
    stage_out(0)
    rs_mid(0)
    total = vsend[...]
    for i in range(n - 1):
        remote(vrecv.at[i], vrecv.at[i], vs.at[i], vr.at[i], dp=p.xn).wait_recv()
        total = total + vrecv[i]
    tv[p.t] = total
    for i, peer in enumerate(p.tpeers):
        copy = remote(tv.at[p.t], tv.at[p.t], vs.at[n - 1 + i], vr.at[n - 1 + i], tensor=peer)
        copy.start()
        vcopies.append(copy)
    rs_end(3)
    rs_end(1)
    rs_end(2)
    stage_out(1)
    for i, peer in enumerate(p.tpeers):
        src = (p.t + 4 - (i + 1)) % 4
        remote(tv.at[src], tv.at[src], vs.at[n - 1 + i], vr.at[n - 1 + i], tensor=peer).wait_recv()
    ocopy(tv, o_tv)
    rs_end(4)
    rs_end(0)
    for gather in gga:
        gather.drain()
    for copy in gsends + vcopies:
        copy.wait_send()
    for copy in outs:
        copy.wait()


def out_kernel(turned, hw, i_tv, *refs):
    count = (len(refs) - 8 - turned) // 3
    ins, outs, vecs = refs[:count], refs[count : 2 * count], refs[2 * count : 2 * count + 5]
    tv, isem, osem = refs[2 * count + 5], refs[-2], refs[-1]
    bufs = refs[2 * count + 6 : -2]
    tv_in = pltpu.make_async_copy(i_tv, tv, isem.at[count])
    tv_in.start()
    loads = [pltpu.make_async_copy(ins[i], bufs[i], isem.at[i]) for i in range(count)]
    for copy in loads:
        copy.start()
    stores = []
    for i, copy in enumerate(loads):
        copy.wait()
        buf = bufs[i]
        if i >= count - turned:
            buf = bufs[turned + i]
            buf[...] = jnp.transpose(bufs[i][...], (1, 0))
        stores.append(pltpu.make_async_copy(buf, outs[i], osem.at[i]))
        stores[-1].start()
    tv_in.wait()
    flat = 4 * lax.axis_index("dp") + lax.axis_index("tensor")
    per = tv.shape[1] // 5
    for ref, row, whole in zip(vecs, (4, 1, 0, 2, 3), (hw, 0, 0, per * 128, per * 128)):
        size = ref.shape[1]
        start = flat * size
        if whole:
            line = per * row + start % whole // 128
            part = tv[start // whole, pl.ds(line, 1), :]
        else:
            line = per * row + start // 128
            part = tv[0, pl.ds(line, 1), :]
            for a in range(1, tv.shape[0]):
                part = part + tv[a, pl.ds(line, 1), :]
        part = pltpu.roll(jnp.broadcast_to(part, (8, 128)), (128 - start % 128) % 128, 1)
        ref[...] = part[0:1, :size]
    for copy in stores:
        copy.wait()


def shards(
    hidden_in, out_grad, doc_ids, w_query, w_key, w_value, w_output, w_up, w_gate, w_down,
    scale_qk, alpha_attn, alpha_mlp, scale_up, scale_gate,
):
    n = lax.axis_size("dp")
    mbs, rows, width = hidden_in.shape
    seq = doc_ids.shape[2]
    hw = w_query.shape[1]
    hidden = w_up.shape[1]
    shard = w_query.shape[0]
    nz = n // 2
    flat = 4 * lax.axis_index("dp") + lax.axis_index("tensor")

    small = jnp.stack(
        [jnp.pad(item, (0, 128 - item.shape[0])) for item in (scale_qk, alpha_attn, alpha_mlp, scale_up, scale_gate)]
        + [jnp.zeros((128,), F32)] * 3
    )

    any_ = pl.BlockSpec(memory_space=pl.ANY)
    vm = pltpu.VMEM
    dma = pltpu.SemaphoreType.DMA

    def sds(shape, dtype):
        return jax.ShapeDtypeStruct(shape, dtype)

    res_shapes = dict(
        out=((mbs, rows, width), BF16),
        w=((4, width, width), BF16),
        x=((mbs, seq, width), BF16),
        q=((mbs, seq, hw), BF16),
        k=((mbs, seq, hw), BF16),
        v=((mbs, seq, hw), BF16),
        rq=((mbs, seq, hw), BF16),
        rk=((mbs, seq, hw), BF16),
        lrow=((mbs, seq // 16, 128), F32),
        mixed=((mbs, seq, hw), BF16),
        mid=((mbs, seq, width), BF16),
        up=((mbs, seq, hidden), BF16),
        gate=((mbs, seq, hidden), BF16),
        inner=((mbs, seq, hidden), BF16),
        attn=((mbs, rows, width), F32),
        gmd=((mbs, rows, width), F32),
        gm=((mbs, rows, width), BF16),
        gm0=((seq, width), BF16),
        vec=((8, width), F32),
        acc=((40, width), F32),
        tab=((mbs, seq, 128), F32),
        ir=((mbs, 8, seq), F32),
    )
    r = {key: sds(*val) for key, val in res_shapes.items()}
    s = {key: vm(*val) for key, val in res_shapes.items()}
    nvec = 5 * (width // 128)
    own32 = vm((mbs, rows, width), F32)
    scat = [vm((mbs, 3, rows, width), BF16), vm((mbs, 3, rows, width), BF16)]
    heads = hw // DH
    res = pl.pallas_call(
        functools.partial(fwd_kernel, n),
        name="fwd",
        out_shape=tuple(r.values()),
        in_specs=[any_] * 11,
        out_specs=tuple([any_] * len(r)),
        scratch_shapes=[
            s["w"], s["x"], s["q"], s["k"], s["v"], s["rq"], s["rk"],
            vm((mbs, seq, 128), F32),
            s["mixed"], s["mid"], s["up"], s["gate"], s["inner"],
            s["attn"], own32, own32, s["gmd"], s["gm"], s["gm0"], s["vec"], s["acc"],
            s["tab"], s["ir"],
            vm((4 * n, 8, 128), F32),
            vm((mbs, 1, seq), jnp.int32),
            vm((mbs, rows, width), BF16), vm((mbs, rows, width), BF16),
            vm((heads * QB, hw), BF16),
            *scat,
            dma((5, n)), dma((5, n)),
            dma((n + 2,)), dma((n + 2,)),
            dma((16,)),
            dma((mbs, 3)), dma((mbs, 3)), dma((mbs, 3)), dma((mbs, 3)), dma((3,)), dma((3,)),
            dma((mbs, 3)), dma((mbs, 3)), dma((mbs, 3)), dma((mbs, 3)),
            dma((40,)),
        ],
        compiler_params=pltpu.CompilerParams(
            collective_id=0, has_side_effects=True, vmem_limit_bytes=VMEM_LIMIT
        ),
    )(w_query, w_key, w_value, w_output.T, w_up, w_gate, w_down.T, hidden_in, out_grad, small, doc_ids)
    r = dict(zip(r, res))

    gshape = sds((shard, hw), F32)
    fshape = sds((shard, hidden), F32)
    grads = pl.pallas_call(
        functools.partial(bwd_kernel, n),
        name="bwd",
        out_shape=(
            sds((mbs, rows, width), BF16), gshape, gshape, gshape, gshape, fshape, fshape, fshape,
            sds((4, nvec, 128), F32),
        ),
        in_specs=[any_] * 22,
        out_specs=tuple([any_] * 9),
        scratch_shapes=[
            s["w"], s["q"], s["k"], s["v"], s["rq"], s["rk"], s["lrow"], s["mixed"],
            s["up"], s["gate"], s["inner"], s["attn"], s["gmd"],
            s["x"], s["x"], s["vec"], s["acc"],
            s["tab"], s["ir"],
            vm((hw, seq), BF16), vm((hw, seq), F32), vm((seq, hw), F32), vm((seq, hw), F32),
            own32,
            vm((4, nz, shard, width), BF16), vm((4, nz - 1, shard, width), BF16),
            vm((nvec, 128), F32), vm((n - 1, nvec, 128), F32), vm((4, nvec, 128), F32),
            *scat,
            dma((48,)), dma((3,)), dma((3,)), dma((mbs, 3)), dma((mbs, 3)),
            dma((mbs, 3)), dma((mbs, 3)), dma((mbs, 3)), dma((mbs, 3)),
            dma((5, nz)), dma((5, nz)), dma((5, nz - 1)), dma((5, nz - 1)),
            dma((n + 2,)), dma((n + 2,)),
            dma((16,)),
        ],
        compiler_params=pltpu.CompilerParams(
            collective_id=1, has_side_effects=True, vmem_limit_bytes=VMEM_LIMIT
        ),
    )(
        hidden_in, r["w"], r["x"], r["q"], r["k"], r["v"], r["rq"], r["rk"], r["lrow"],
        r["mixed"], r["mid"], r["up"], r["gate"], r["inner"], r["attn"], r["gmd"], r["gm"], r["gm0"],
        r["vec"], r["acc"], r["tab"], r["ir"],
    )
    g_in, gq, gk, gv, go, gu, gg, gd, tv = grads
    results = [gq, gk, gv, gu, gg, r["out"], g_in, go, gd]
    turned = 2 if shard % 128 == 0 else 0
    if not turned:
        results = results[:-2]
    finals = [sds(item.shape, item.dtype) for item in results]
    for i in range(len(results) - turned, len(results)):
        finals[i] = sds(finals[i].shape[::-1], F32)
    ones = [scale_qk, alpha_attn, alpha_mlp, scale_up, scale_gate]
    done = pl.pallas_call(
        functools.partial(out_kernel, turned, hw),
        name="results",
        out_shape=tuple(finals) + tuple(sds((1, item.shape[0]), F32) for item in ones),
        in_specs=[any_] * (len(results) + 1),
        out_specs=(any_,) * len(finals) + (pl.BlockSpec(memory_space=vm),) * 5,
        scratch_shapes=[
            vm(tv.shape, F32),
            *[vm(item.shape, item.dtype) for item in results],
            *[vm(item.shape, item.dtype) for item in finals[len(results) - turned :]],
            dma((len(results) + 1,)), dma((len(results),)),
        ],
        compiler_params=pltpu.CompilerParams(vmem_limit_bytes=VMEM_LIMIT),
    )(tv, *results)
    vecs = [item.reshape(-1) for item in done[len(finals) :]]
    gq, gk, gv, gu, gg, out, g_in = done[:7]
    go, gd = done[7:9] if turned else (go.T, gd.T)
    return (out, g_in, gq, gk, gv, go, gu, gg, gd, *vecs)


def solution(mesh):
    rows = P("dp", "tensor", None)
    inward = P("dp", "tensor")
    outward = P("tensor", "dp")
    flat = P(("dp", "tensor"))
    weights = (inward, inward, inward, outward, inward, inward, outward)
    in_specs = (rows, rows, P("dp", None, None)) + weights + (flat,) * 5
    out_specs = (rows, rows) + weights + (flat,) * 5
    return jax.shard_map(shards, mesh=mesh, in_specs=in_specs, out_specs=out_specs, check_vma=False)
```

```python
import functools
import math

import jax
import jax.numpy as jnp
from jax import lax
from jax.experimental import pallas as pl
from jax.experimental.pallas import tpu as pltpu
from jax.sharding import PartitionSpec as P

DH = 64
BLOCK = 256
DOCS = 3
DOC_MAX = 512
F32 = jnp.float32
BF16 = jnp.bfloat16
MESH = pl.DeviceIdType.MESH
VMEM_LIMIT = 67043328
LOG2E = 1.4426950408889634
QB = 128
WIDE = 512
CODE = 8


def nn(a, b):
    return jnp.dot(a, b, preferred_element_type=F32)


def nt(a, b):
    return lax.dot_general(a, b, (((1,), (1,)), ((), ())), preferred_element_type=F32)


def tn(a, b):
    return lax.dot_general(a, b, (((0,), (0,)), ((), ())), preferred_element_type=F32)


def split_sum(vals, ones):
    high = vals.astype(BF16)
    low = (vals - high.astype(F32)).astype(BF16)
    return nn(high, ones) + nn(low, ones)


def lane_iota(shape):
    return lax.broadcasted_iota(jnp.int32, shape, len(shape) - 1)


def head_ones():
    rows = lax.broadcasted_iota(jnp.int32, (128, 128), 0) // DH
    cols = lax.broadcasted_iota(jnp.int32, (128, 128), 1) // DH
    return jnp.where(rows == cols, 1.0, 0.0).astype(BF16)


def partner(vals):
    low = lane_iota(vals.shape) % DH < DH // 2
    return jnp.where(low, pltpu.roll(vals, 128 - DH // 2, 1), pltpu.roll(vals, DH // 2, 1))


def turns(table):
    lane = lane_iota(table.shape)
    both = jnp.where(lane < DH, table, pltpu.roll(table, DH, 1))
    low = lane % DH < DH // 2
    cosine = jnp.where(low, both, pltpu.roll(both, DH // 2, 1))
    sine = jnp.where(low, -pltpu.roll(both, 128 - DH // 2, 1), both)
    return cosine, sine


class Place:
    def __init__(self, n):
        self.n = n
        self.t = lax.axis_index("tensor")
        self.d = lax.axis_index("dp")
        t, d = self.t, self.d
        self.sib = t + 1 - 2 * (t % 2)
        self.yp = (t + 2) % 4
        self.diag = (self.sib + 2) % 4
        self.xi = d % 2
        self.z = d // 2
        self.nz = n // 2
        self.xn = d + 1 - 2 * (d % 2)
        self.zpeers = [2 * ((self.z + k) % self.nz) + self.xi for k in range(1, self.nz)]
        self.dpeers = [(d + k) % n for k in range(1, n)]
        self.tpeers = [(t + k) % 4 for k in range(1, 4)]

    def barrier(self):
        sem = pltpu.get_barrier_semaphore()
        for peer in self.dpeers:
            pl.semaphore_signal(sem, inc=1, device_id={"dp": peer}, device_id_type=MESH)
        for peer in self.tpeers:
            pl.semaphore_signal(sem, inc=1, device_id={"tensor": peer}, device_id_type=MESH)
        pl.semaphore_wait(sem, self.n + 2)


def remote(src, dst, ssem, rsem, **where):
    return pltpu.make_async_remote_copy(
        src_ref=src, dst_ref=dst, send_sem=ssem, recv_sem=rsem, device_id=where, device_id_type=MESH
    )


class Gather:
    def __init__(self, place, whole, ssem, rsem, rows):
        self.p, self.whole, self.ssem, self.rsem, self.rows = place, whole, ssem, rsem, rows

    def at(self, index):
        return self.whole.at[pl.ds(pl.multiple_of(index * self.rows, self.rows), self.rows)]

    def start(self, own):
        p = self.p
        self.c_yp = remote(own, self.at(p.t), self.ssem.at[1], self.rsem.at[1], tensor=p.yp)
        self.c_sib = remote(own, self.at(p.t), self.ssem.at[0], self.rsem.at[0], tensor=p.sib)
        self.c_yp.start()
        self.c_sib.start()

    def wait(self, step):
        p = self.p
        if step == 1:
            remote(self.at(p.sib), self.at(p.sib), self.ssem.at[0], self.rsem.at[0], tensor=p.sib).wait_recv()
        if step == 2:
            remote(self.at(p.yp), self.at(p.yp), self.ssem.at[1], self.rsem.at[1], tensor=p.yp).wait_recv()
            self.forward().start()
        if step == 3:
            remote(self.at(p.diag), self.at(p.diag), self.ssem.at[2], self.rsem.at[2], tensor=p.sib).wait_recv()

    def forward(self):
        p = self.p
        return remote(self.at(p.yp), self.at(p.yp), self.ssem.at[2], self.rsem.at[2], tensor=p.sib)

    def drain(self):
        self.c_yp.wait_send()
        self.c_sib.wait_send()
        self.forward().wait_send()

    def each(self, work):
        blocks(self.p, work, self.wait)


def blocks(p, work, wait=None):
    def body(i, carry):
        for step in range(1, 4):
            if wait is not None:
                pl.when(i == step)(functools.partial(wait, step))
        work((p.t // 2 + i // 2) % 2 * 2 + (p.t + i) % 2)
        return carry

    lax.fori_loop(0, 4, body, 0)


class Scatter:
    def __init__(self, place, sbuf, rbuf, ssem, rsem):
        self.p, self.sbuf, self.rbuf, self.ssem, self.rsem = place, sbuf, rbuf, ssem, rsem

    def copy(self, slot):
        where = self.p.yp if slot == 2 else self.p.sib
        return remote(self.sbuf.at[slot], self.rbuf.at[slot], self.ssem.at[slot], self.rsem.at[slot], tensor=where)

    def arrive(self, slot):
        self.copy(slot).wait_recv()

    def run(self, part, own):
        p = self.p

        def send(slot):
            vals = own[...]
            if slot == 2:
                self.arrive(0)
                vals = vals + self.rbuf[0].astype(F32)
            self.sbuf[slot] = vals.astype(BF16)
            self.copy(slot).start()

        def body(i, carry):
            own[...] = part((p.t // 2 + (i + 1) % 2) % 2 * 2 + (p.t + 1 - i // 2) % 2)
            for slot in range(3):
                pl.when(i == slot)(functools.partial(send, slot))
            return carry

        lax.fori_loop(0, 4, body, 0)

    def finish(self):
        self.arrive(1)
        self.arrive(2)
        for slot in range(3):
            self.copy(slot).wait_send()


def rows_of(ref, index, rows):
    return ref[pl.ds(pl.multiple_of(index * rows, rows), rows)]


def mean_sq(vals):
    return jnp.mean(vals * vals, axis=-1, keepdims=True)


def fold8(vals):
    total = vals[0:8]
    for k in range(1, vals.shape[0] // 8):
        total = total + vals[8 * k : 8 * k + 8]
    return total


def layer_kernel(
    n,
    wq, wk, wv, wo, wu, wg, wd, hid, og, small, docs,
    o_out, o_x, o_mid, o_in, o_gq, o_gk, o_gv, o_go, o_gu, o_gg, o_gd, o_tv,
    w, x, q, k, v, rqk, lrow, mixed, mid, up, gate, inner, attn, midf, mlp, gmd, vec, acc, tab, ir,
    docv, ogv, qm, sbuf, rbuf, kt, dk, dv, xrecv, zrecv, vsend, vrecv, tv,
    wsend, wrecv, small_s, small_r, lsem, agx_s, agx_r, agm_s, agm_r, agg_s, agg_r, aga_s, aga_r,
    rsa_s, rsa_r, rsm_s, rsm_r, rsb_s, rsb_r, rsi_s, rsi_r, xs, xr, zs, zr, vs, vr, osem,
):
    p = Place(n)
    nz = p.nz
    mbs, rows, width = hid.shape
    seq = x.shape[1]
    hw = q.shape[2]
    shard = wq.shape[0]
    heads = hw // DH
    groups = w.shape[0]
    hidden = up.shape[2]

    pieces = ((0, 0, 3 * hw), (0, 3 * hw, 4 * hw), (1, 0, hidden), (2, 0, hidden), (3, 0, hidden))

    def wat(key, index):
        g, lo, hi = pieces[key]
        return w.at[g, pl.ds(pl.multiple_of(index * shard, shard), shard), pl.ds(lo, hi - lo)]

    ga, gm, back, dqt = x, mid, midf, mlp.at[0]
    gmix = [inner.at[m, :, pl.ds(0, hw)] for m in range(mbs)]
    pts, dss = (inner.at[m, pl.ds(0, seq - 128), pl.ds(hw, heads * QB)] for m in range(2))
    qs, gs = (
        inner.at[0, pl.ds(i * heads * QB, heads * QB), pl.ds(hw + heads * QB, hw)] for i in range(2)
    )

    local = []

    def lcopy(src, dst):
        copy = pltpu.make_async_copy(src, dst, lsem.at[len(local)])
        copy.start()
        local.append(copy)
        return copy

    outs = []

    def ocopy(src, dst):
        copy = pltpu.make_async_copy(src, dst, osem.at[len(outs)])
        copy.start()
        outs.append(copy)

    own_w = pl.ds(pl.multiple_of(p.d * shard, shard), shard)
    w_in = [lcopy(src, w.at[0, own_w, pl.ds(i * hw, hw)]) for i, src in enumerate((wq, wk, wv, wo))]
    w_in += [lcopy(src, w.at[i + 1, own_w]) for i, src in enumerate((wu, wg, wd))]
    docs_in = lcopy(docs, docv)
    p.barrier()

    gx = [Gather(p, x.at[m], agx_s.at[m], agx_r.at[m], rows) for m in range(mbs)]
    gmi = [Gather(p, mid.at[m], agm_s.at[m], agm_r.at[m], rows) for m in range(mbs)]
    def seat(t, d):
        line = pl.ds(pl.multiple_of(t * n + d // 8 * 8, 8), 8)
        return midf.at[0, line, pl.ds(pl.multiple_of(d % 8 * 128, 128), 128)]

    small_own = lcopy(small, seat(p.t, p.d))
    small_d = [
        remote(small, seat(p.t, p.d), small_s.at[i], small_r.at[i], dp=peer)
        for i, peer in enumerate(p.dpeers)
    ]
    for copy in small_d:
        copy.start()
    gx[0].start(hid.at[0])
    sends = []

    def wsend_to(g, i, src, index, peer):
        copy = remote(src, wat(g, index), wsend.at[g, i], wrecv.at[g, index], dp=peer)
        copy.start()
        sends.append(copy)

    def relay(g):
        for i, peer in reversed(list(enumerate(p.zpeers))):
            remote(wat(g, peer), wat(g, peer), wsend.at[g, 0], wrecv.at[g, peer], dp=p.xn).wait_recv()
            wsend_to(g, nz + i, wat(g, peer), peer, p.xn)

    for copy in w_in:
        copy.wait()
    for g in range(len(pieces)):
        for i, peer in enumerate(p.zpeers):
            wsend_to(g, i, wat(g, p.d), p.d, peer)
        if g == 0:
            wsend_to(0, nz - 1, wat(0, p.d), p.d, p.xn)
    xown = [lcopy(hid.at[m], gx[m].at(p.t)) for m in range(mbs)]
    og_in = lcopy(og, ogv)
    for i, peer in enumerate(p.dpeers):
        src = seat(p.t, (p.d + n - (i + 1)) % n)
        remote(src, src, small_s.at[i], small_r.at[i], dp=peer).wait_recv()
    small_own.wait()
    small_t = []
    for i, peer in enumerate(p.tpeers):
        part = midf.at[0, pl.ds(pl.multiple_of(p.t * n, n), n)]
        copy = remote(part, part, small_s.at[n - 1 + i], small_r.at[n - 1 + i], tensor=peer)
        copy.start()
        small_t.append(copy)
    gx[1].start(hid.at[1])

    def wready(g):
        remote(wat(g, p.xn), wat(g, p.xn), wsend.at[g, 0], wrecv.at[g, p.xn], dp=p.xn).wait_recv()
        for peer in p.zpeers:
            other = peer + 1 - 2 * p.xi
            remote(wat(g, other), wat(g, other), wsend.at[g, 0], wrecv.at[g, other], dp=p.xn).wait_recv()

    docs_in.wait()
    for m in range(mbs):
        doc = docv[m]
        count = [jnp.sum(jnp.where(doc == i, 1.0, 0.0), axis=1, keepdims=True) for i in range(DOCS - 1)]
        first = jnp.zeros(doc.shape, F32)
        for i in range(DOCS - 1):
            first = first + jnp.where(doc > i, count[i], 0.0)
        place = lane_iota(doc.shape).astype(F32) - first
        low = doc.astype(F32) * CODE
        code = low + jnp.floor(place * (1.0 / BLOCK))
        line = lax.broadcasted_iota(jnp.int32, (8, seq), 0)
        ir[m] = jnp.where(line == 0, code, jnp.where(line == 1, low, place))
        line = lax.broadcasted_iota(jnp.int32, (128, seq), 0)
        every_row = jnp.where(line == DH, code, jnp.where(line == DH + 1, low, place))
        tab[m] = jnp.transpose(every_row, (1, 0))

    def turn_rows(i, carry):
        at = pl.ds(pl.multiple_of(i % (seq // 64) * 64, 64), 64)
        m = i // (seq // 64)
        lane = lane_iota((1, 128))
        freq = jnp.exp((lane % (DH // 2)).astype(F32) * (-math.log(10000.0) / (DH // 2)))
        shift = jnp.where(lane < DH // 2, 0.5 * math.pi, 0.0)
        old = tab[m, at, :]
        tab[m, at, :] = jnp.where(lane < DH, jnp.sin(old[:, 0:1] * freq + shift), old)
        return carry

    lax.fori_loop(0, mbs * (seq // 64), turn_rows, 0)
    acc[...] = jnp.zeros_like(acc)

    relay(0)
    for g in range(1, len(pieces)):
        wsend_to(g, nz - 1, wat(g, p.d), p.d, p.xn)
    for i, peer in enumerate(p.tpeers):
        part = midf.at[0, pl.ds(pl.multiple_of((p.t + 4 - (i + 1)) % 4 * n, n), n)]
        remote(part, part, small_s.at[n - 1 + i], small_r.at[n - 1 + i], tensor=peer).wait_recv()
    every = 4 * n

    def gathered(row, base, count, lanes):
        per = count // (lanes // 128)

        def item(k):
            part = seat(k % 4, base + k // 4)[row : row + 1, :]
            turn = k % per * (128 // per)
            return pltpu.roll(part, turn, 1) if turn else part

        for r in range(lanes // 128):
            total = item(r * per)
            for j in range(1, per):
                total = total + item(r * per + j)
            vec[row : row + 1, 128 * r : 128 * r + 128] = total

    gathered(0, p.t * (n // 4), n, hw)
    gathered(1, 0, every, width)
    gathered(2, 0, every, width)
    gathered(3, p.t * (n // 4), n, hidden)
    gathered(4, p.t * (n // 4), n, hidden)
    wready(0)

    ones = head_ones()

    def stage_qkv(m):
        xown[m].wait()

        def work(index):
            at = pl.ds(pl.multiple_of(index * rows, rows), rows)
            xb = x[m, at, :]
            cb, sb = turns(tab[m, at, :])
            scales = []
            for which, dst in enumerate((q, k)):
                raw = nn(xb, w[0, :, which * hw : (which + 1) * hw])
                for half in range(hw // 128):
                    lanes = slice(128 * half, 128 * half + 128)
                    piece = raw[:, lanes]
                    turned = piece * cb + partner(piece) * sb
                    scale = lax.rsqrt(split_sum(turned * turned, ones) + 1e-06)
                    scales.append(scale)
                    dst[m, at, lanes] = (turned * scale * vec[0:1, lanes]).astype(BF16)
            v[m, at, :] = nn(xb, w[0, :, 2 * hw : 3 * hw]).astype(BF16)
            for half in range(hw // 128):
                both = jnp.where(lane_iota(cb.shape) % DH < DH // 2, scales[half], scales[hw // 128 + half])
                rqk[m, at, 128 * half : 128 * half + 128] = both.astype(BF16)

        gx[m].each(work)

    win = seq - 128
    c_exp = math.sqrt(DH) * LOG2E

    def attend(m):
        def body(b, carry):
            at = pl.ds(pl.multiple_of(b * QB, QB), QB)
            keys = pl.ds(pl.multiple_of(((b + 3) // 8) * 128, 128), win)
            ccol = tab[m, at, DH : DH + 1]
            lcol_ = tab[m, at, DH + 1 : DH + 2]
            crow = ir[m, 0:1, keys]
            bias = jnp.where((crow <= ccol) & (crow >= lcol_), 0.0, -1e30)
            qb = q[m, at, :]
            lane = lane_iota((QB, hw)) // DH
            for h in range(heads):
                qm[h * QB : (h + 1) * QB, :] = jnp.where(lane == h, qb, jnp.zeros_like(qb))
            kb = k[m, keys, :]
            vb = v[m, keys, :]
            total = jnp.zeros((QB, hw), F32)
            lsum = jnp.zeros((QB, 128), F32)
            lane_l = lane_iota((QB, 128))
            for h in range(heads):
                scores = nt(qm[h * QB : (h + 1) * QB, :], kb)
                expo = jnp.exp2(scores * c_exp + bias)
                inv = 1.0 / jnp.sum(expo, axis=-1, keepdims=True)
                part = nn(expo.astype(BF16), vb)
                total = jnp.where(lane == h, part * inv, total)
                lsum = jnp.where(lane_l == h, inv, lsum)
            mixed[m, at, :] = total.astype(BF16)
            lrow[m, pl.ds(pl.multiple_of(b * 8, 8), 8), :] = jnp.transpose(lsum, (1, 0))[0:8, :]
            return carry

        lax.fori_loop(0, seq // QB, body, 0)

    sc_a = [Scatter(p, sbuf.at[m], rbuf.at[m], rsa_s.at[m], rsa_r.at[m]) for m in range(mbs)]
    sc_m = [Scatter(p, sbuf.at[m], rbuf.at[m], rsm_s.at[m], rsm_r.at[m]) for m in range(mbs)]

    def stage_o(m):
        sc_a[m].run(
            lambda index: nt(rows_of(mixed.at[m], index, rows), w[0, :, 3 * hw : 3 * hw + hw]),
            attn.at[m],
        )

    chunk = 32

    def stage_mid(m):
        sc_a[m].finish()
        base = p.t * rows

        def body(i, carry):
            at = pl.ds(pl.multiple_of(i * chunk, chunk), chunk)
            own = pl.ds(pl.multiple_of(base + i * chunk, chunk), chunk)
            a = attn[m, at, :] + rbuf[m, 1, at, :].astype(F32) + rbuf[m, 2, at, :].astype(F32)
            attn[m, at, :] = a
            h = x[m, own, :].astype(F32)
            na = a * lax.rsqrt(mean_sq(a) + 1e-06)
            zz = h + vec[1:2, :] * (na - h)
            out = zz * lax.rsqrt(mean_sq(zz) + 1e-06)
            midf[m, at, :] = out
            mid[m, own, :] = out.astype(BF16)
            return carry

        lax.fori_loop(0, rows // chunk, body, 0)
        gmi[m].start(gmi[m].at(p.t))


    def stage_up(m):
        def work(index):
            at = pl.ds(pl.multiple_of(index * rows, rows), rows)

            def body(c, carry):
                lanes = pl.ds(pl.multiple_of(c * WIDE, WIDE), WIDE)
                mb = mid[m, at, :]
                u = nn(mb, w[1, :, lanes])
                g = nn(mb, w[2, :, lanes])
                up[m, at, lanes] = u.astype(BF16)
                gate[m, at, lanes] = g.astype(BF16)
                gs = g * vec[4:5, lanes]
                inner[m, at, lanes] = ((u * vec[3:4, lanes]) * (gs / (1.0 + jnp.exp(-gs)))).astype(BF16)
                return carry

            lax.fori_loop(0, hidden // WIDE, body, 0)

        gmi[m].each(work)

    def stage_down(m):
        sc_m[m].run(lambda index: nt(rows_of(inner.at[m], index, rows), w[3]), mlp.at[m])

    gg = [Gather(p, gm.at[m], agg_s.at[m], agg_r.at[m], rows) for m in range(mbs)]

    def stage_end(m):
        sc_m[m].finish()

        def body(i, carry):
            at = pl.ds(pl.multiple_of(i * chunk, chunk), chunk)
            a = mlp[m, at, :] + rbuf[m, 1, at, :].astype(F32) + rbuf[m, 2, at, :].astype(F32)
            h = midf[m, at, :]
            ra = lax.rsqrt(mean_sq(a) + 1e-06)
            na = a * ra
            al = vec[2:3, :]
            zz = h + al * (na - h)
            rz = lax.rsqrt(mean_sq(zz) + 1e-06)
            out = zz * rz
            cot = ogv[m, at, :].astype(F32)
            ogv[m, at, :] = out.astype(BF16)
            dz = rz * (cot - out * jnp.mean(cot * out, axis=-1, keepdims=True))
            dn = al * dz
            acc[0:8, :] += fold8(dz * (na - h))
            gmd[m, at, :] = dz - dn
            grad = (ra * (dn - na * jnp.mean(dn * na, axis=-1, keepdims=True))).astype(BF16)
            gm[m, pl.ds(pl.multiple_of(p.t * rows + i * chunk, chunk), chunk), :] = grad
            return carry

        lax.fori_loop(0, rows // chunk, body, 0)
        gg[m].start(gg[m].at(p.t))

    gga = [Gather(p, ga.at[m], aga_s.at[m], aga_r.at[m], rows) for m in range(mbs)]
    sc_b = [Scatter(p, sbuf.at[m], rbuf.at[m], rsb_s.at[m], rsb_r.at[m]) for m in range(mbs)]
    sc_i = [Scatter(p, sbuf.at[m], rbuf.at[m], rsi_s.at[m], rsi_r.at[m]) for m in range(mbs)]
    cols = 256

    def stage_inner(m):
        def work(index):
            at = pl.ds(pl.multiple_of(index * rows, rows), rows)

            def body(c, carry):
                lanes = pl.ds(pl.multiple_of(c * WIDE, WIDE), WIDE)
                gi = nn(gm[m, at, :], w[3, :, lanes])
                u = up[m, at, lanes].astype(F32)
                g = gate[m, at, lanes].astype(F32)
                su = vec[3:4, lanes]
                sg = vec[4:5, lanes]
                gsc = g * sg
                sig = 1.0 / (1.0 + jnp.exp(-gsc))
                gu = gi * (gsc * sig)
                ggs = gi * (u * su) * sig * (1.0 + gsc * (1.0 - sig))
                acc[16:24, lanes] += fold8(gu * u)
                acc[24:32, lanes] += fold8(ggs * g)
                up[m, at, lanes] = (gu * su).astype(BF16)
                gate[m, at, lanes] = (ggs * sg).astype(BF16)
                return carry

            lax.fori_loop(0, hidden // WIDE, body, 0)

        gg[m].each(work)

    def stage_back(m):
        sc_b[m].run(
            lambda index: nt(rows_of(up.at[m], index, rows), w[1])
            + nt(rows_of(gate.at[m], index, rows), w[2]),
            back.at[m],
        )

    def stage_attn(m):
        sc_b[m].finish()
        base = p.t * rows

        def body(i, carry):
            at = pl.ds(pl.multiple_of(i * chunk, chunk), chunk)
            own = pl.ds(pl.multiple_of(base + i * chunk, chunk), chunk)
            part = back[m, at, :] + rbuf[m, 1, at, :].astype(F32)
            cot = gmd[m, at, :] + part + rbuf[m, 2, at, :].astype(F32)
            a = attn[m, at, :]
            h = ga[m, own, :].astype(F32)
            ra = lax.rsqrt(mean_sq(a) + 1e-06)
            na = a * ra
            al = vec[1:2, :]
            zz = h + al * (na - h)
            rz = lax.rsqrt(mean_sq(zz) + 1e-06)
            out = zz * rz
            dz = rz * (cot - out * jnp.mean(cot * out, axis=-1, keepdims=True))
            dn = al * dz
            acc[8:16, :] += fold8(dz * (na - h))
            gmd[m, at, :] = dz - dn
            ga[m, own, :] = (ra * (dn - na * jnp.mean(dn * na, axis=-1, keepdims=True))).astype(BF16)
            return carry

        lax.fori_loop(0, rows // chunk, body, 0)
        gga[m].start(gga[m].at(p.t))

    def stage_mixed(m):
        def work(index):
            at = pl.ds(pl.multiple_of(index * rows, rows), rows)
            gmix[m][at, :] = nn(ga[m, at, :], w[0, :, 3 * hw : 4 * hw]).astype(BF16)

        gga[m].each(work)

    def attend_back(m):
        kt[...] = jnp.transpose(k[m], (1, 0))
        dk[...] = jnp.zeros_like(dk)
        dv[...] = jnp.zeros_like(dv)

        def body(b, carry):
            at = pl.ds(pl.multiple_of(b * QB, QB), QB)
            keys = pl.ds(pl.multiple_of(((b + 3) // 8) * 128, 128), win)
            crow = ir[m, 0:1, at]
            lrow_ = ir[m, 1:2, at]
            ccol = tab[m, keys, DH : DH + 1]
            bias = jnp.where((ccol <= crow) & (ccol >= lrow_), 0.0, -1e30)
            qb = q[m, at, :]
            gb = gmix[m][at, :]
            lane = lane_iota((QB, hw)) // DH
            for h in range(heads):
                qs[h * QB : (h + 1) * QB, :] = jnp.where(lane == h, qb, jnp.zeros_like(qb))
                gs[h * QB : (h + 1) * QB, :] = jnp.where(lane == h, gb, jnp.zeros_like(gb))
            kb = k[m, keys, :]
            vb = v[m, keys, :]
            for h in range(heads):
                hl = slice(h * QB, (h + 1) * QB)
                scores = nt(kb, qs[hl, :])
                inv = lrow[m, pl.ds(pl.multiple_of(b * 8, 8), 8), :][h : h + 1, :]
                pt = jnp.exp2(scores * c_exp + bias) * inv
                dpt = nt(vb, gs[hl, :])
                delta = jnp.sum(pt * dpt, axis=0, keepdims=True)
                dst = (pt * (dpt - delta)).astype(BF16)
                pts[:, hl] = pt.astype(BF16)
                dss[:, hl] = dst
                dqt[h * DH : (h + 1) * DH, at] = nn(kt[h * DH : (h + 1) * DH, keys], dst)
            dv[keys, :] += nn(pts[...], gs[...])
            dk[keys, :] += nn(dss[...], qs[...])
            return carry

        lax.fori_loop(0, seq // QB, body, 0)

        step = 256

        def after(i, carry):
            at = pl.ds(pl.multiple_of(i * step, step), step)
            cb, sb = turns(tab[m, at, :])
            v[m, at, :] = dv[at, :].astype(BF16)
            for which in range(2):
                src = (q, k)[which]
                for half in range(hw // 128):
                    lanes = slice(128 * half, 128 * half + 128)
                    if which == 0:
                        grad = jnp.transpose(dqt[lanes, at], (1, 0)) * math.sqrt(DH)
                    else:
                        grad = dk[at, lanes] * math.sqrt(DH)
                    gain = vec[0:1, lanes]
                    unit = src[m, at, lanes].astype(F32) / gain
                    acc[32:40, lanes] += fold8(grad * unit)
                    dn = grad * gain
                    both = rqk[m, at, lanes].astype(F32)
                    first = lane_iota(both.shape) % DH < DH // 2
                    rsc = jnp.where(first, both, partner(both)) if which == 0 else jnp.where(first, partner(both), both)
                    dy = rsc * (dn - unit * split_sum(dn * unit, ones))
                    src[m, at, lanes] = (dy * cb - partner(dy) * sb).astype(BF16)
            return carry

        lax.fori_loop(0, seq // step, after, 0)

    def stage_in(m):
        def part(index):
            at = pl.ds(pl.multiple_of(index * rows, rows), rows)
            return (
                nt(q[m, at, :], w[0, :, 0:hw])
                + nt(k[m, at, :], w[0, :, hw : 2 * hw])
                + nt(v[m, at, :], w[0, :, 2 * hw : 3 * hw])
            )

        sc_i[m].run(part, back.at[m])

    def stage_out(m):
        sc_i[m].finish()

        def body(i, carry):
            at = pl.ds(pl.multiple_of(i * chunk, chunk), chunk)
            part = back[m, at, :] + rbuf[m, 1, at, :].astype(F32)
            total = gmd[m, at, :] + part + rbuf[m, 2, at, :].astype(F32)
            sbuf[m, 0, at, :] = total.astype(BF16)
            return carry

        lax.fori_loop(0, rows // chunk, body, 0)
        ocopy(sbuf.at[m, 0], o_in.at[m])

    gpieces = {
        3: (w.at[3], 3, 0, width),
        1: (w.at[1], 1, 0, width),
        2: (w.at[2], 2, 0, width),
        0: (gm.at[0], 0, 0, 3 * hw),
        4: (gm.at[0], 0, 3 * hw, 4 * hw),
    }

    def weight_grad(key, left, rights):
        into = gpieces[key][0]

        def body(c, carry):
            lanes = pl.ds(pl.multiple_of(c * cols, cols), cols)
            for lo, hi, right in rights:
                total = tn(left[0, :, lanes], right[0])
                for m in range(1, mbs):
                    total = total + tn(left[m, :, lanes], right[m])
                into[lanes, lo:hi] = total.astype(BF16)
            return carry

        lax.fori_loop(0, width // cols, body, 0)

    def wrow(key, index):
        ref, _, lo, hi = gpieces[key]
        return ref.at[pl.ds(pl.multiple_of(index * shard, shard), shard), pl.ds(lo, hi - lo)]

    def held(buf, key, index):
        _, g, lo, hi = gpieces[key]
        return buf.at[g, index, :, pl.ds(lo, hi - lo)]

    gsends = []

    def rs_start(key):
        for kk in list(range(1, nz)) + [0]:
            zz = (p.z + kk) % nz
            other = 2 * zz + 1 - p.xi
            copy = remote(wrow(key, other), held(xrecv, key, zz), xs.at[key, kk], xr.at[key, zz], dp=p.xn)
            copy.start()
            gsends.append(copy)

    def rs_arrive(key, kk):
        zz = (p.z + kk) % nz
        got = held(xrecv, key, zz)
        remote(got, got, xs.at[key, kk], xr.at[key, zz], dp=p.xn).wait_recv()
        return got, zz

    def rs_mid(key):
        for kk in range(1, nz):
            got, zz = rs_arrive(key, kk)
            mine = 2 * zz + p.xi
            got[...] = (got[...].astype(F32) + wrow(key, mine)[...].astype(F32)).astype(BF16)
            copy = remote(got, held(zrecv, key, kk - 1), zs.at[key, kk - 1], zr.at[key, kk - 1], dp=mine)
            copy.start()
            gsends.append(copy)

    def rs_end(key):
        _, g, lo, hi = gpieces[key]
        got, _ = rs_arrive(key, 0)
        total = got[...].astype(F32) + wrow(key, p.d)[...].astype(F32)
        for kk in range(1, nz):
            got = held(zrecv, key, kk - 1)
            remote(got, got, zs.at[key, kk - 1], zr.at[key, kk - 1], dp=p.xn).wait_recv()
            total = total + got[...].astype(F32)
        fin = attn.at[g // 2, pl.ds((g % 2) * shard, shard)]
        fin[:, lo:hi] = total
        if g == 0:
            for i, dst in enumerate((o_gq, o_gk, o_gv, o_go)):
                if lo <= i * hw < hi:
                    ocopy(fin.at[:, pl.ds(i * hw, hw)], dst)
        else:
            ocopy(fin, (o_gu, o_gg, o_gd)[g - 1])

    stage_qkv(0)
    kept_x = [lcopy(x.at[0], o_x.at[0])]
    relay(1)
    attend(0)
    relay(2)
    wready(1)
    stage_o(0)
    stage_qkv(1)
    kept_x.append(lcopy(x.at[1], o_x.at[1]))
    attend(1)
    for copy in small_t + small_d:
        copy.wait_send()
    stage_mid(0)
    relay(3)
    stage_o(1)
    relay(4)
    wready(2)
    wready(3)
    stage_up(0)
    kept_mid = [lcopy(mid.at[0], o_mid.at[0])]
    stage_mid(1)
    wready(4)
    gmi[0].drain()
    kept_mid[0].wait()
    stage_down(0)
    stage_up(1)
    kept_mid.append(lcopy(mid.at[1], o_mid.at[1]))
    gmi[1].drain()
    kept_mid[1].wait()
    stage_down(1)
    og_in.wait()
    stage_end(0)
    for m in range(mbs):
        gx[m].drain()
        kept_x[m].wait()
    for copy in sends:
        copy.wait_send()
    stage_end(1)
    ocopy(ogv, o_out)
    stage_inner(0)
    stage_back(0)
    stage_inner(1)
    weight_grad(3, gm, [(0, hidden, inner)])
    rs_start(3)
    for gather in gg:
        gather.drain()
    l_mid = [lcopy(o_mid.at[m], gm.at[m]) for m in range(mbs)]
    stage_attn(0)
    stage_back(1)
    for copy in l_mid:
        copy.wait()
    weight_grad(1, gm, [(0, hidden, up)])
    rs_start(1)
    l_x = [lcopy(o_x.at[m], up.at[m]) for m in range(mbs)]
    stage_mixed(0)
    rs_mid(3)
    attend_back(0)
    stage_attn(1)
    stage_in(0)
    weight_grad(2, gm, [(0, hidden, gate)])
    rs_start(2)
    rs_mid(1)
    stage_mixed(1)
    weight_grad(4, ga, [(3 * hw, 4 * hw, mixed)])
    rs_start(4)
    attend_back(1)
    rs_mid(2)

    per = width // 128
    for r in range(5):
        sums = jnp.sum(acc[8 * r : 8 * r + 8, :], axis=0, keepdims=True)
        for j in range(per):
            vsend[per * r + j : per * r + j + 1, :] = sums[:, 128 * j : 128 * j + 128]
    vcopies = []
    for i, peer in enumerate(p.dpeers):
        copy = remote(vsend, vrecv.at[i], vs.at[i], vr.at[i], dp=peer)
        copy.start()
        vcopies.append(copy)
    for copy in l_x:
        copy.wait()
    weight_grad(0, up, [(0, hw, q), (hw, 2 * hw, k), (2 * hw, 3 * hw, v)])
    rs_start(0)
    rs_mid(4)
    stage_in(1)
    stage_out(0)
    rs_mid(0)
    total = vsend[...]
    for i in range(n - 1):
        remote(vrecv.at[i], vrecv.at[i], vs.at[i], vr.at[i], dp=p.xn).wait_recv()
        total = total + vrecv[i]
    tv[p.t] = total
    for i, peer in enumerate(p.tpeers):
        copy = remote(tv.at[p.t], tv.at[p.t], vs.at[n - 1 + i], vr.at[n - 1 + i], tensor=peer)
        copy.start()
        vcopies.append(copy)
    rs_end(3)
    rs_end(1)
    rs_end(2)
    stage_out(1)
    for i, peer in enumerate(p.tpeers):
        src = (p.t + 4 - (i + 1)) % 4
        remote(tv.at[src], tv.at[src], vs.at[n - 1 + i], vr.at[n - 1 + i], tensor=peer).wait_recv()
    ocopy(tv, o_tv)
    rs_end(4)
    rs_end(0)
    for gather in gga:
        gather.drain()
    for copy in gsends + vcopies:
        copy.wait_send()
    for copy in outs:
        copy.wait()


def out_kernel(turned, hw, i_tv, *refs):
    count = (len(refs) - 8 - turned) // 3
    ins, outs, vecs = refs[:count], refs[count : 2 * count], refs[2 * count : 2 * count + 5]
    tv, isem, osem = refs[2 * count + 5], refs[-2], refs[-1]
    bufs = refs[2 * count + 6 : -2]
    tv_in = pltpu.make_async_copy(i_tv, tv, isem.at[count])
    tv_in.start()
    loads = [pltpu.make_async_copy(ins[i], bufs[i], isem.at[i]) for i in range(count)]
    for copy in loads:
        copy.start()
    stores = []
    for i, copy in enumerate(loads):
        copy.wait()
        buf = bufs[i]
        if i >= count - turned:
            buf = bufs[turned + i]
            buf[...] = jnp.transpose(bufs[i][...], (1, 0))
        stores.append(pltpu.make_async_copy(buf, outs[i], osem.at[i]))
        stores[-1].start()
    tv_in.wait()
    flat = 4 * lax.axis_index("dp") + lax.axis_index("tensor")
    per = tv.shape[1] // 5
    for ref, row, whole in zip(vecs, (4, 1, 0, 2, 3), (hw, 0, 0, per * 128, per * 128)):
        size = ref.shape[1]
        start = flat * size
        if whole:
            line = per * row + start % whole // 128
            part = tv[start // whole, pl.ds(line, 1), :]
        else:
            line = per * row + start // 128
            part = tv[0, pl.ds(line, 1), :]
            for a in range(1, tv.shape[0]):
                part = part + tv[a, pl.ds(line, 1), :]
        part = pltpu.roll(jnp.broadcast_to(part, (8, 128)), (128 - start % 128) % 128, 1)
        ref[...] = part[0:1, :size]
    for copy in stores:
        copy.wait()


def shards(
    hidden_in, out_grad, doc_ids, w_query, w_key, w_value, w_output, w_up, w_gate, w_down,
    scale_qk, alpha_attn, alpha_mlp, scale_up, scale_gate,
):
    n = lax.axis_size("dp")
    mbs, rows, width = hidden_in.shape
    seq = doc_ids.shape[2]
    hw = w_query.shape[1]
    hidden = w_up.shape[1]
    shard = w_query.shape[0]
    nz = n // 2
    flat = 4 * lax.axis_index("dp") + lax.axis_index("tensor")

    small = jnp.stack(
        [jnp.pad(item, (0, 128 - item.shape[0])) for item in (scale_qk, alpha_attn, alpha_mlp, scale_up, scale_gate)]
        + [jnp.zeros((128,), F32)] * 3
    )

    any_ = pl.BlockSpec(memory_space=pl.ANY)
    vm = pltpu.VMEM
    dma = pltpu.SemaphoreType.DMA

    def sds(shape, dtype):
        return jax.ShapeDtypeStruct(shape, dtype)

    nvec = 5 * (width // 128)
    rows32 = vm((mbs, rows, width), F32)
    rows16 = vm((mbs, rows, width), BF16)
    full = vm((mbs, seq, width), BF16)
    wide = vm((mbs, seq, hidden), BF16)
    slim = vm((mbs, seq, hw), BF16)
    scat = vm((mbs, 3, rows, width), BF16)
    pair = dma((mbs, 3))
    heads = hw // DH
    gshape = sds((shard, hw), F32)
    fshape = sds((shard, hidden), F32)
    g_out, _, _, g_in, gq, gk, gv, go, gu, gg, gd, tv = pl.pallas_call(
        functools.partial(layer_kernel, n),
        name="layer",
        out_shape=(
            sds((mbs, rows, width), BF16), sds((mbs, seq, width), BF16), sds((mbs, seq, width), BF16),
            sds((mbs, rows, width), BF16), gshape, gshape, gshape, gshape, fshape, fshape, fshape,
            sds((4, nvec, 128), F32),
        ),
        in_specs=[any_] * 11,
        out_specs=(any_,) * 12,
        scratch_shapes=[
            vm((4, width, width), BF16), full, slim, slim, slim, slim,
            vm((mbs, seq // 16, 128), F32), slim, full, wide, wide, wide,
            rows32, rows32, rows32, rows32, vm((8, width), F32), vm((40, width), F32),
            vm((mbs, seq, 128), F32), vm((mbs, 8, seq), F32),
            vm((mbs, 1, seq), jnp.int32), rows16, vm((heads * QB, hw), BF16),
            scat, scat,
            vm((hw, seq), BF16), vm((seq, hw), F32), vm((seq, hw), F32),
            vm((4, nz, shard, width), BF16), vm((4, nz - 1, shard, width), BF16),
            vm((nvec, 128), F32), vm((n - 1, nvec, 128), F32), vm((4, nvec, 128), F32),
            dma((5, n)), dma((5, n)), dma((n + 2,)), dma((n + 2,)), dma((24,)),
            pair, pair, pair, pair, pair, pair, pair, pair,
            pair, pair, pair, pair, pair, pair, pair, pair,
            dma((5, nz)), dma((5, nz)), dma((5, nz - 1)), dma((5, nz - 1)),
            dma((n + 2,)), dma((n + 2,)), dma((16,)),
        ],
        compiler_params=pltpu.CompilerParams(
            collective_id=0, has_side_effects=True, vmem_limit_bytes=VMEM_LIMIT
        ),
    )(w_query, w_key, w_value, w_output.T, w_up, w_gate, w_down.T, hidden_in, out_grad, small, doc_ids)
    results = [gq, gk, gv, gu, gg, g_out, g_in, go, gd]
    turned = 2 if shard % 128 == 0 else 0
    if not turned:
        results = results[:-2]
    finals = [sds(item.shape, item.dtype) for item in results]
    for i in range(len(results) - turned, len(results)):
        finals[i] = sds(finals[i].shape[::-1], F32)
    ones = [scale_qk, alpha_attn, alpha_mlp, scale_up, scale_gate]
    done = pl.pallas_call(
        functools.partial(out_kernel, turned, hw),
        name="results",
        out_shape=tuple(finals) + tuple(sds((1, item.shape[0]), F32) for item in ones),
        in_specs=[any_] * (len(results) + 1),
        out_specs=(any_,) * len(finals) + (pl.BlockSpec(memory_space=vm),) * 5,
        scratch_shapes=[
            vm(tv.shape, F32),
            *[vm(item.shape, item.dtype) for item in results],
            *[vm(item.shape, item.dtype) for item in finals[len(results) - turned :]],
            dma((len(results) + 1,)), dma((len(results),)),
        ],
        compiler_params=pltpu.CompilerParams(vmem_limit_bytes=VMEM_LIMIT),
    )(tv, *results)
    vecs = [item.reshape(-1) for item in done[len(finals) :]]
    gq, gk, gv, gu, gg, out, g_in = done[:7]
    go, gd = done[7:9] if turned else (go.T, gd.T)
    return (out, g_in, gq, gk, gv, go, gu, gg, gd, *vecs)


def solution(mesh):
    rows = P("dp", "tensor", None)
    inward = P("dp", "tensor")
    outward = P("tensor", "dp")
    flat = P(("dp", "tensor"))
    weights = (inward, inward, inward, outward, inward, inward, outward)
    in_specs = (rows, rows, P("dp", None, None)) + weights + (flat,) * 5
    out_specs = (rows, rows) + weights + (flat,) * 5
    return jax.shard_map(shards, mesh=mesh, in_specs=in_specs, out_specs=out_specs, check_vma=False)
```
